256 devices in a mesh: lat: 8 (over y, x_lo), lon: 32 (over x_hi, z, core).
Axes of the slice: x: 4 (x_hi: 2, x_lo: 2; x = x_hi * 2 + x_lo), y: 4, z: 8, core: 2. Of those that a mesh axis runs over, the one named last changes fastest.
Arguments:
- tokens_in: bfloat16 [2, 96, 768, 1024], P(None, 'lat', 'lon'), may hold values from -6 to 6
- grad_out: bfloat16 [2, 96, 768, 1024], P(None, 'lat', 'lon'), may hold values from -6 to 6
- norm_gain: float32 [1024], replicated, may hold values from 0.25 to 1.75
- w_qkv: bfloat16 [1024, 1536], replicated
- w_proj: bfloat16 [512, 1024], replicated, may hold values from -0.25 to 0.25
Outputs:
- grad_in: bfloat16 [2, 96, 768, 1024], P(None, 'lat', 'lon')
- grad_qkv: float32 [1024, 1536], P(('lat', 'lon'))
- grad_proj: float32 [512, 1024], P(None, ('lat', 'lon'))
- gain_gradient: float32 [1024], P(('lat', 'lon'))
The draws below stay inside these ranges and needn't reach their ends.
All inputs are finite; a program needn't handle non-finite values.
Results may differ from the reference program's by a relative error of at most 0.0095.
Values may be sent and summed in bfloat16 or wider, within the bound.
No kernel may reach another device: no remote copies, remote signals or barrier semaphores. Data moves between devices by JAX's collectives and lax.ppermute only.
A program may use at most 128 MiB of HBM per device.

```python
import jax
import jax.numpy as jnp
from jax import lax

D = 1024
HEADS = 8
HD = 64
WLAT = 6
WLON = 12
LEV = 2
HH = 512
NLAT = 96
NLON = 768
TOKENS = 147456


def draw_w_qkv(key, part):
    weights = jax.random.normal(key, (D, 3 * HH), jnp.float32) * D ** (-0.5)
    return weights.astype(jnp.bfloat16)


def with_spikes(array, stream_key, source, target, parts, factor):
    def block_of(axis_at):
        return (jnp.arange(array.shape[axis_at]) // (array.shape[axis_at] // parts)).reshape((-1,) + (1,) * (array.ndim - 1 - axis_at))

    first = jax.random.permutation(stream_key, parts)[block_of(target)]
    far = (block_of(target) + parts // 2) % parts
    return jnp.where((block_of(source) == first) | (block_of(source) == far), factor * array, array)


def levels(stream_key, shape, shards, least, top_value):
    gain = 1.0
    for axis_at, parts in shards:
        heights = jax.random.uniform(jax.random.fold_in(jax.random.fold_in(stream_key, 6), axis_at), (parts,), jnp.float32, least / len(shards), top_value / len(shards))
        gain = gain * jnp.repeat(jnp.exp(heights), shape[axis_at] // parts).reshape((-1,) + (1,) * (len(shape) - 1 - axis_at))
    return gain


def scatter_about(rng, shape, deviation, bound, cuts=(), kind=jnp.bfloat16):
    factor_of = levels(rng, shape, cuts, -0.22, 0.18) if cuts else 1.0
    result = jax.random.normal(rng, shape, jnp.float32) * deviation * factor_of
    return jnp.minimum(jnp.maximum(result, -bound), bound).astype(kind)


def gaussian_with(key, shape, scale, most, shards, heavy, kind=jnp.bfloat16):
    values = scale * jax.random.normal(key, shape, jnp.float32)
    if shards:
        values = values * levels(key, shape, shards, -0.22, 0.18)
    return jnp.clip(with_spikes(values, jax.random.fold_in(key, 3), *heavy), -most, most).astype(kind)


def setup_inputs(seed: int = 0) -> dict:
    key_list = jax.random.split(jax.random.key(seed), 6)
    tokens_in = gaussian_with(key_list[0], (LEV, NLAT, NLON, D), 1.0, 6.0, ((1, 8), (2, 32)), (2, 3, 32, 2.75))
    grad_out = scatter_about(key_list[1], (LEV, NLAT, NLON, D), 1.0, 6.0, ((1, 8), (2, 32)))
    norm_gain = jnp.clip(1.0 + 0.15 * jax.random.normal(key_list[2], (D,), jnp.float32), 0.25, 1.75)
    w_qkv = draw_w_qkv(jax.random.fold_in(key_list[5], 71), 0)
    w_proj = scatter_about(key_list[4], (HH, D), HH ** -0.5, 0.25)
    return dict(tokens_in=tokens_in, grad_out=grad_out, norm_gain=norm_gain, w_qkv=w_qkv, w_proj=w_proj)


def grad_windows(xs, dys, gain_vector, w_qkv, w_proj, flags):
    lev, rows, cols, width = xs.shape
    nlat = rows // WLAT
    nlon = cols // WLON
    tok = lev * WLAT * WLON
    count = nlat * nlon

    def part(a):
        return a.reshape(lev, nlat, WLAT, nlon, WLON, width).transpose(1, 3, 0, 2, 4, 5).reshape(count * tok, width)
    xw = part(xs).astype(jnp.float32)
    gradient_times_gain = part(dys)
    mean_value = lax.optimization_barrier(jnp.mean(xw, -1, keepdims=True))
    centered_input = xw - mean_value
    inverse_deviation = lax.rsqrt(lax.optimization_barrier(jnp.mean(centered_input * centered_input, -1, keepdims=True)) + 1e-05)
    standardized_input = centered_input * inverse_deviation
    normalized_input = (standardized_input * gain_vector).astype(jnp.bfloat16)
    qkv = jnp.dot(normalized_input, w_qkv, preferred_element_type=jnp.float32).astype(jnp.bfloat16)
    qkv = qkv.reshape(count, tok, 3, HEADS, HD).astype(jnp.float32)
    qry, key, val = (qkv[:, :, 0], qkv[:, :, 1], qkv[:, :, 2])
    group = jnp.arange(tok) // WLON % WLAT < WLAT // 2
    allow = (group[:, None] == group[None, :])[None] | jnp.logical_not(flags)[:, None, None]
    scale = HD ** (-0.5)
    scores = jnp.einsum('wqhd,wkhd->whqk', qry, key) * scale
    scores = jnp.where(allow[:, None], scores, -1000000000.0)
    top = lax.optimization_barrier(jnp.max(scores, -1, keepdims=True))
    expo = jnp.exp(scores - top)
    probs = expo / lax.optimization_barrier(jnp.sum(expo, -1, keepdims=True))
    probs_b = probs.astype(jnp.bfloat16).astype(jnp.float32)
    attended = jnp.einsum('whqk,wkhd->wqhd', probs_b, val).astype(jnp.bfloat16).reshape(count * tok, HEADS * HD)
    grad_att = jnp.dot(gradient_times_gain, w_proj.T, preferred_element_type=jnp.float32).astype(jnp.bfloat16)
    grad_proj = jnp.dot(attended.T, gradient_times_gain, preferred_element_type=jnp.float32)
    grad_heads = grad_att.reshape(count, tok, HEADS, HD).astype(jnp.float32)
    dprob = jnp.einsum('wqhd,wkhd->whqk', grad_heads, val)
    dscore = (probs * (dprob - lax.optimization_barrier(jnp.sum(probs * dprob, -1, keepdims=True))) * scale).astype(jnp.bfloat16).astype(jnp.float32)
    grad_q = jnp.einsum('whqk,wkhd->wqhd', dscore, key).astype(jnp.bfloat16)
    grad_k = jnp.einsum('whqk,wqhd->wkhd', dscore, qry).astype(jnp.bfloat16)
    grad_v = jnp.einsum('whqk,wqhd->wkhd', probs_b, grad_heads).astype(jnp.bfloat16)
    grad_act = jnp.stack([grad_q, grad_k, grad_v], axis=2).reshape(count * tok, 3 * HEADS * HD)
    grad_qkv = jnp.dot(normalized_input.T, grad_act, preferred_element_type=jnp.float32)
    normalized_gradient = jnp.dot(grad_act, w_qkv.T, preferred_element_type=jnp.float32)
    gain_gradient = lax.optimization_barrier(jnp.sum(normalized_gradient * standardized_input, 0))
    gated_output = normalized_gradient * gain_vector
    input_gradient = gradient_times_gain.astype(jnp.float32) + inverse_deviation * (gated_output - lax.optimization_barrier(jnp.mean(gated_output, -1, keepdims=True)) - standardized_input * lax.optimization_barrier(jnp.mean(gated_output * standardized_input, -1, keepdims=True)))
    input_gradient = input_gradient.astype(jnp.bfloat16).reshape(nlat, nlon, lev, WLAT, WLON, width).transpose(2, 0, 3, 1, 4, 5).reshape(lev, rows, cols, width)
    return (input_gradient, grad_qkv, grad_proj, gain_gradient)

def reference(tokens_in, grad_out, norm_gain, w_qkv, w_proj):
    lev, nrows, ncols, width = tokens_in.shape
    nslab = nrows // WLAT
    nwin = ncols // WLON
    rolled_x = jnp.roll(tokens_in, (-(WLAT // 2), -(WLON // 2)), (1, 2))
    rolled_g = jnp.roll(grad_out, (-(WLAT // 2), -(WLON // 2)), (1, 2))
    slabs_x = rolled_x.reshape(lev, nslab, WLAT, ncols, width).transpose(1, 0, 2, 3, 4)
    slabs_g = rolled_g.reshape(lev, nslab, WLAT, ncols, width).transpose(1, 0, 2, 3, 4)

    def step(carry, item):
        slab_x, slab_g, index = item
        flags = jnp.broadcast_to(index == nslab - 1, (nwin,))
        input_gradient, gq, gp, gg = grad_windows(slab_x, slab_g, norm_gain, w_qkv, w_proj, flags)
        return ((carry[0] + gq, carry[1] + gp, carry[2] + gg), input_gradient)
    init = (jnp.zeros((width, 3 * HEADS * HD), jnp.float32), jnp.zeros((HEADS * HD, width), jnp.float32), jnp.zeros((width,), jnp.float32))
    sums, grad_slabs = lax.scan(step, init, (slabs_x, slabs_g, jnp.arange(nslab, dtype=jnp.int32)))
    input_gradient = grad_slabs.transpose(1, 0, 2, 3, 4).reshape(lev, nrows, ncols, width)
    input_gradient = jnp.roll(input_gradient, (WLAT // 2, WLON // 2), (1, 2))
    factor = 1.0 / jnp.sqrt(jnp.float32(TOKENS))
    return (input_gradient, sums[0] * factor, sums[1] * factor, sums[2] * factor)
```

```python
import functools

import jax
import jax.numpy as jnp
from jax import lax
from jax.experimental import pallas as pl
from jax.experimental.pallas import tpu as pltpu
from jax.sharding import Mesh, PartitionSpec as P

F32 = jnp.float32
BF = jnp.bfloat16
D = 1024
HH = 512
TOK = 144
NWIN = 4
ROWS = NWIN * TOK
LEV, NR, NC = 2, 12, 24
LATN = 112
LONN = 112
DIAGN = 48
EPS = 1e-05
VLIM = 60 * 1024 * 1024

NN = (((1,), (0,)), ((), ()))
NT = (((1,), (1,)), ((), ()))
TN = (((0,), (0,)), ((), ()))


def dot(a, b, dims):
    return lax.dot_general(a, b, dims, preferred_element_type=F32)


def params():
    return pltpu.CompilerParams(vmem_limit_bytes=VLIM)


def cost(flops, nbytes):
    return pl.CostEstimate(flops=int(flops), bytes_accessed=int(nbytes), transcendentals=0)


def window_row(lev, rr, cc):
    return ((rr // 6) * 2 + cc // 12) * TOK + lev * 72 + (rr % 6) * 12 + cc % 12


def own_segments():
    for lev in range(LEV):
        for rr in range(9):
            base = (lev * NR + rr + 3) * NC
            yield base + 6, window_row(lev, rr, 0), 12
            yield base + 18, window_row(lev, rr, 12), 6


def lat_segments():
    for lev in range(LEV):
        for r in range(3):
            base = (lev * 3 + r) * 18
            yield base, window_row(lev, 9 + r, 0), 12, (lev * NR + r) * NC + 6
            yield base + 12, window_row(lev, 9 + r, 12), 6, (lev * NR + r) * NC + 18


def lon_segments():
    for lev in range(LEV):
        for rr in range(9):
            yield (lev * 9 + rr) * 6, window_row(lev, rr, 18), 6, (lev * NR + rr + 3) * NC


def diag_segments():
    for lev in range(LEV):
        for r in range(3):
            yield (lev * 3 + r) * 6, window_row(lev, 9 + r, 18), 6, (lev * NR + r) * NC


def pack_kernel(x_ref, dy_ref, lat_ref, lon_ref, diag_ref, src, dst):
    for a, ref in enumerate((x_ref, dy_ref)):
        for lev in range(LEV):
            for r in range(NR):
                at = (lev * NR + r) * NC
                src[at : at + NC, :] = ref[lev, r].astype(F32)
        for out, segments in ((lat_ref, lat_segments), (lon_ref, lon_segments), (diag_ref, diag_segments)):
            count = out.shape[1]
            dst[count - 16 : count, :] = jnp.zeros((16, D), F32)
            for at, _, size, own in segments():
                dst[at : at + size, :] = src[own : own + size, :]
            out[a] = dst[:count, :].astype(BF)


def pack(x, dy):
    return pl.pallas_call(
        pack_kernel,
        out_shape=(
            jax.ShapeDtypeStruct((2, LATN, D), BF),
            jax.ShapeDtypeStruct((2, LONN, D), BF),
            jax.ShapeDtypeStruct((2, DIAGN, D), BF),
        ),
        scratch_shapes=[pltpu.VMEM((ROWS, D), F32), pltpu.VMEM((LATN, D), F32)],
        compiler_params=params(),
        cost_estimate=cost(1e6, 4e6),
        name="pack",
    )(x, dy)


def assemble(a, ref, lat_ref, lon_ref, diag_ref, src, win):
    for lev in range(LEV):
        for r in range(3, NR):
            at = (lev * NR + r) * NC
            src[at : at + NC, :] = ref[lev, r].astype(F32)
    for own, at, size in own_segments():
        win[at : at + size, :] = src[own : own + size, :]
    for halo, segments in ((lat_ref, lat_segments), (lon_ref, lon_segments), (diag_ref, diag_segments)):
        count = halo.shape[1]
        src[:count, :] = halo[a].astype(F32)
        for here, at, size, _ in segments():
            win[at : at + size, :] = src[here : here + size, :]


def layer_stats(x):
    mean = jnp.mean(x, -1, keepdims=True)
    cen = x - mean
    inv = lax.rsqrt(jnp.mean(cen * cen, -1, keepdims=True) + EPS)
    return cen, inv


def main_kernel(
    x_ref, dy_ref, lat_ref, lon_ref, diag_ref, gain_ref, wq_ref, wp_ref,
    keep_ref, send_ref, gact_ref, xw_ref, dyw_ref,
    src, win, nrm, qkv, gatt, att, normt,
):
    core = lax.axis_index("c")
    last = jnp.logical_and(lax.axis_index("y") == 3, lax.axis_index("xl") == 1)
    assemble(0, x_ref, lat_ref, lon_ref, diag_ref, src, win)
    for w in range(NWIN):
        rows = slice(w * TOK, (w + 1) * TOK)
        x = win[rows, :]
        xw_ref[rows, :] = x.astype(BF)
        cen, inv = layer_stats(x)
        nrm[rows, :] = (cen * inv * gain_ref[...]).astype(BF)
    assemble(1, dy_ref, lat_ref, lon_ref, diag_ref, src, win)
    for w in range(NWIN):
        rows = slice(w * TOK, (w + 1) * TOK)
        dyw_ref[rows, :] = win[rows, :].astype(BF)
    for j in range(6):
        cols = slice(j * 256, (j + 1) * 256)
        qkv[:, cols] = dot(nrm[...], wq_ref[:, cols], NN).astype(BF)
    for j in range(2):
        cols = slice(j * 256, (j + 1) * 256)
        gatt[:, cols] = dot(dyw_ref[...], wp_ref[cols, :], NT).astype(BF)

    low = lax.broadcasted_iota(jnp.int32, (TOK, 128), 1) < 64
    keyg = (lax.broadcasted_iota(jnp.int32, (TOK, 2 * TOK), 0) // 12) % 6 < 3
    qryg = (lax.broadcasted_iota(jnp.int32, (TOK, 2 * TOK), 1) // 12) % 6 < 3
    apart = jnp.logical_and(keyg != qryg, last)

    def stacked(v):
        z = jnp.zeros_like(v)
        return jnp.concatenate([jnp.where(low, v, z), jnp.where(low, z, v)], axis=0)

    for w in range(NWIN):
        rows = slice(w * TOK, (w + 1) * TOK)
        for hp in range(4):
            at = hp * 128
            q2 = stacked(qkv[rows, at : at + 128] * jnp.bfloat16(0.125))
            k = qkv[rows, HH + at : HH + at + 128]
            v = qkv[rows, 2 * HH + at : 2 * HH + at + 128]
            g2 = stacked(gatt[rows, at : at + 128])
            s = dot(k, q2, NT)
            if w >= 2:
                s = jnp.where(apart, -1000000000.0, s)
            e = jnp.exp(s - jnp.max(s, 0, keepdims=True))
            p = e * (1.0 / jnp.sum(e, 0, keepdims=True))
            pb = p.astype(BF)
            dp = dot(v, g2, NT)
            ds = (p * (dp - jnp.sum(p * dp, 0, keepdims=True))).astype(BF)
            o = dot(pb, v, TN)
            att[rows, at : at + 128] = jnp.where(low, o[:TOK], o[TOK:]).astype(BF)
            dq = dot(ds, k, TN)
            gact_ref[rows, at : at + 128] = (jnp.where(low, dq[:TOK], dq[TOK:]) * 0.125).astype(BF)
            gact_ref[rows, HH + at : HH + at + 128] = dot(ds, q2, NN).astype(BF)
            gact_ref[rows, 2 * HH + at : 2 * HH + at + 128] = dot(pb, g2, NN).astype(BF)

    def put(slot_is_low, rows, cols, value):
        @pl.when(core == slot_is_low)
        def _():
            keep_ref[rows, cols] = value

        @pl.when(core != slot_is_low)
        def _():
            send_ref[rows, cols] = value

    normt[...] = nrm[...].T
    for i in range(4):
        rows = slice(i * 256, (i + 1) * 256)
        lhs = normt[rows, :]
        put(0, rows, slice(0, 1024), dot(lhs, gact_ref[:, 0:1024], NN).astype(BF))
        put(1, rows, slice(0, 512), dot(lhs, gact_ref[:, 1024:1536], NN).astype(BF))
    normt[...] = dyw_ref[...].T
    for i in range(4):
        rows = slice(i * 256, (i + 1) * 256)
        put(1, rows, slice(512, 1024), dot(normt[rows, :], att[...], NN).astype(BF))


def main_call(x, dy, lat, lon, diag, gain, wq, wp):
    return pl.pallas_call(
        main_kernel,
        out_shape=(
            jax.ShapeDtypeStruct((D, 1024), BF),
            jax.ShapeDtypeStruct((D, 1024), BF),
            jax.ShapeDtypeStruct((ROWS, 1536), BF),
            jax.ShapeDtypeStruct((ROWS, D), BF),
            jax.ShapeDtypeStruct((ROWS, D), BF),
        ),
        scratch_shapes=[
            pltpu.VMEM((ROWS, D), F32),
            pltpu.VMEM((ROWS, D), F32),
            pltpu.VMEM((ROWS, D), BF),
            pltpu.VMEM((ROWS, 1536), BF),
            pltpu.VMEM((ROWS, HH), BF),
            pltpu.VMEM((ROWS, HH), BF),
            pltpu.VMEM((D, ROWS), BF),
        ],
        compiler_params=params(),
        cost_estimate=cost(5.5e9, 14e6),
        name="main",
    )(x, dy, lat, lon, diag, gain, wq, wp)


def input_kernel(
    gact_ref, xw_ref, dyw_ref, gain_ref, wq_ref,
    own_ref, lat_ref, lon_ref, diag_ref, gg_ref,
    win, dst,
):
    gain = gain_ref[...]
    acc = jnp.zeros((1, D), F32)
    for w in range(NWIN):
        rows = slice(w * TOK, (w + 1) * TOK)
        gn = dot(gact_ref[rows, :], wq_ref[...], NT)
        cen, inv = layer_stats(xw_ref[rows, :].astype(F32))
        xhat = cen * inv
        acc += jnp.sum(gn * xhat, 0, keepdims=True)
        g = gn * gain
        win[rows, :] = dyw_ref[rows, :].astype(F32) + inv * (
            g - jnp.mean(g, -1, keepdims=True) - xhat * jnp.mean(g * xhat, -1, keepdims=True)
        )
    for j in range(8):
        gg_ref[j : j + 1, :] = acc[:, j * 128 : (j + 1) * 128]
    for out, segments in ((lat_ref, lat_segments), (lon_ref, lon_segments), (diag_ref, diag_segments)):
        count = out.shape[0]
        dst[count - 16 : count, :] = jnp.zeros((16, D), F32)
        for at, here, size, _ in segments():
            dst[at : at + size, :] = win[here : here + size, :]
        out[...] = dst[:count, :].astype(BF)
    for own, here, size in own_segments():
        dst[own : own + size, :] = win[here : here + size, :]
    for lev in range(LEV):
        for r in range(3, NR):
            at = (lev * NR + r) * NC
            own_ref[lev, r - 3] = dst[at : at + NC, :].astype(BF)


def input_call(gact, xw, dyw, gain, wq):
    return pl.pallas_call(
        input_kernel,
        out_shape=(
            jax.ShapeDtypeStruct((LEV, 9, NC, D), BF),
            jax.ShapeDtypeStruct((LATN, D), BF),
            jax.ShapeDtypeStruct((LONN, D), BF),
            jax.ShapeDtypeStruct((DIAGN, D), BF),
            jax.ShapeDtypeStruct((8, 128), F32),
        ),
        scratch_shapes=[pltpu.VMEM((ROWS, D), F32), pltpu.VMEM((ROWS, D), F32)],
        compiler_params=params(),
        cost_estimate=cost(2e9, 9e6),
        name="input",
    )(gact, xw, dyw, gain, wq)


def join_kernel(own_ref, lat_ref, lon_ref, diag_ref, out_ref, src, dst):
    for lev in range(LEV):
        for r in range(3, NR):
            at = (lev * NR + r) * NC
            dst[at : at + NC, :] = own_ref[lev, r - 3].astype(F32)
    for halo, segments in ((lat_ref, lat_segments), (lon_ref, lon_segments), (diag_ref, diag_segments)):
        count = halo.shape[0]
        src[:count, :] = halo[...].astype(F32)
        for here, _, size, own in segments():
            dst[own : own + size, :] = src[here : here + size, :]
    for lev in range(LEV):
        for r in range(NR):
            at = (lev * NR + r) * NC
            out_ref[lev, r] = dst[at : at + NC, :].astype(BF)


def join_call(own, lat, lon, diag):
    return pl.pallas_call(
        join_kernel,
        out_shape=jax.ShapeDtypeStruct((LEV, NR, NC, D), BF),
        scratch_shapes=[pltpu.VMEM((LATN, D), F32), pltpu.VMEM((ROWS, D), F32)],
        compiler_params=params(),
        cost_estimate=cost(1e6, 4e6),
        name="join",
    )(own, lat, lon, diag)


MSG = 272


def split_kernel(keep_ref, recv_ref, gg_ref, own_ref, a_ref, b_ref, c_ref):
    y = lax.axis_index("y")
    hi = gg_ref[...].astype(BF)
    lo = (gg_ref[...] - hi.astype(F32)).astype(BF)
    for k, out in enumerate((own_ref, a_ref, b_ref, c_ref)):
        at = pl.multiple_of(lax.rem(y + k, 4) * 256, 256)
        rows = pl.ds(at, 256)
        out[0:256, :] = (keep_ref[rows, :].astype(F32) + recv_ref[rows, :].astype(F32)).astype(out.dtype)
        if k:
            out[256:MSG, :] = jnp.zeros((MSG - 256, 1024), BF)
            out[256:264, 0:128] = hi
            out[256:264, 128:256] = lo


def split_call(keep, recv, gg):
    msg = jax.ShapeDtypeStruct((MSG, 1024), BF)
    return pl.pallas_call(
        split_kernel,
        out_shape=(jax.ShapeDtypeStruct((256, 1024), F32), msg, msg, msg),
        compiler_params=params(),
        cost_estimate=cost(1e6, 8e6),
        name="split",
    )(keep, recv, gg)


def gather_kernel(own_ref, gg_ref, a_ref, b_ref, c_ref, out_ref):
    gg = gg_ref[...]
    for ref in (a_ref, b_ref, c_ref):
        gg += ref[256:264, 0:128].astype(F32) + ref[256:264, 128:256].astype(F32)
    gg = gg.astype(BF)
    for i in range(16):
        rows = slice(i * 16, (i + 1) * 16)
        total = own_ref[rows, :]
        for ref in (a_ref, b_ref, c_ref):
            total += ref[rows, :].astype(F32)
        total = total.astype(BF)
        for j in range(2):
            out_ref[2 * i + j, :, 0:1024] = total[j * 8 : (j + 1) * 8, :]
            out_ref[2 * i + j, :, 1024:1152] = gg


def gather_call(own, gg, a, b, c):
    return pl.pallas_call(
        gather_kernel,
        out_shape=jax.ShapeDtypeStruct((32, 8, 1152), BF),
        compiler_params=params(),
        cost_estimate=cost(1e6, 4e6),
        name="gather",
    )(own, gg, a, b, c)


def shift(n, k):
    return [(i, (i + k) % n) for i in range(n)]


def shift_both(k):
    pairs = []
    for i in range(8):
        for j in range(32):
            pairs.append((i * 32 + j, ((i + k) % 8) * 32 + (j + k) % 32))
    return pairs


LAT = ("y", "xl")
LON = ("xh", "z", "c")
ALL = LAT + LON


def per_device(x, dy, gain, wq, wp):
    gain2 = gain.reshape(1, D)
    lat, lon, diag = pack(x, dy)
    lat = lax.ppermute(lat, LAT, shift(8, -1))
    lon = lax.ppermute(lon, LON, shift(32, -1))
    diag = lax.ppermute(diag, ALL, shift_both(-1))
    keep, send, gact, xw, dyw = main_call(x, dy, lat, lon, diag, gain2, wq, wp)
    recv = lax.ppermute(send, "c", [(0, 1), (1, 0)])
    own, lat, lon, diag, gg = input_call(gact, xw, dyw, gain2, wq)
    lat = lax.ppermute(lat, LAT, shift(8, 1))
    lon = lax.ppermute(lon, LON, shift(32, 1))
    diag = lax.ppermute(diag, ALL, shift_both(1))
    mine, a, b, c = split_call(keep, recv, gg)
    a = lax.ppermute(a, "y", shift(4, 1))
    b = lax.ppermute(b, "y", shift(4, 2))
    c = lax.ppermute(c, "y", shift(4, 3))
    grad_in = join_call(own, lat, lon, diag)
    blocks = gather_call(mine, gg, a, b, c)
    blocks = lax.all_to_all(blocks, ("xl", "xh", "z"), 0, 0, tiled=True)
    total = jnp.sum(blocks.astype(F32), 0)
    other = lax.ppermute(total, "c", [(0, 1), (1, 0)])
    core = lax.axis_index("c")
    first = jnp.where(core == 0, total, other)
    second = jnp.where(core == 0, other, total)
    first = lax.dynamic_slice_in_dim(first, core * 4, 4, 0)
    second4 = lax.dynamic_slice_in_dim(second, core * 4, 4, 0)
    factor = 1.0 / jnp.sqrt(F32(147456))
    grad_qkv = jnp.concatenate([first[:, :1024], second4[:, :512]], 1) * factor
    grad_proj = second4[:, 512:1024].T * factor
    gsum = (total[:, 1024:] + other[:, 1024:]).reshape(1024)
    index = lax.axis_index(LAT) * 32 + lax.axis_index(LON)
    grad_gain = lax.dynamic_slice_in_dim(gsum, index * 4, 4, 0) * factor
    return grad_in, grad_qkv, grad_proj, grad_gain


def solution(mesh):
    mesh = Mesh(mesh.devices.reshape(4, 2, 2, 8, 2), ALL)
    return jax.shard_map(
        per_device,
        mesh=mesh,
        in_specs=(P(None, LAT, LON, None), P(None, LAT, LON, None), P(), P(), P()),
        out_specs=(P(None, LAT, LON, None), P(ALL, None), P(None, ALL), P(ALL)),
        check_vma=False,
    )
```

```python
import functools

import jax
import jax.numpy as jnp
from jax import lax
from jax.experimental import pallas as pl
from jax.experimental.pallas import tpu as pltpu
from jax.sharding import Mesh, PartitionSpec as P

F32 = jnp.float32
BF = jnp.bfloat16
D = 1024
HH = 512
TOK = 144
NWIN = 4
ROWS = NWIN * TOK
LEV, NR, NC = 2, 12, 24
LATN = 112
LONN = 112
DIAGN = 48
EPS = 1e-05

NN = (((1,), (0,)), ((), ()))
NT = (((1,), (1,)), ((), ()))
TN = (((0,), (0,)), ((), ()))


def dot(a, b, dims):
    return lax.dot_general(a, b, dims, preferred_element_type=F32)


def params(mib):
    return pltpu.CompilerParams(vmem_limit_bytes=mib * 1024 * 1024)


def cost(flops, nbytes):
    return pl.CostEstimate(flops=int(flops), bytes_accessed=int(nbytes), transcendentals=0)


def window_row(lev, rr, cc):
    return ((rr // 6) * 2 + cc // 12) * TOK + lev * 72 + (rr % 6) * 12 + cc % 12


def own_segments():
    for lev in range(LEV):
        for rr in range(9):
            base = (lev * NR + rr + 3) * NC
            yield base + 6, window_row(lev, rr, 0), 12
            yield base + 18, window_row(lev, rr, 12), 6


def lat_segments():
    for lev in range(LEV):
        for r in range(3):
            base = (lev * 3 + r) * 18
            yield base, window_row(lev, 9 + r, 0), 12, (lev * NR + r) * NC + 6
            yield base + 12, window_row(lev, 9 + r, 12), 6, (lev * NR + r) * NC + 18


def lon_segments():
    for lev in range(LEV):
        for rr in range(9):
            yield (lev * 9 + rr) * 6, window_row(lev, rr, 18), 6, (lev * NR + rr + 3) * NC


def diag_segments():
    for lev in range(LEV):
        for r in range(3):
            yield (lev * 3 + r) * 6, window_row(lev, 9 + r, 18), 6, (lev * NR + r) * NC


def pack_kernel(x_ref, dy_ref, lat_ref, lon_ref, diag_ref, src, dst):
    for a, ref in enumerate((x_ref, dy_ref)):
        for lev in range(LEV):
            for r in range(NR):
                at = (lev * NR + r) * NC
                src[at : at + NC, :] = ref[lev, r].astype(F32)
        for out, segments in ((lat_ref, lat_segments), (lon_ref, lon_segments), (diag_ref, diag_segments)):
            count = out.shape[1]
            dst[count - 16 : count, :] = jnp.zeros((16, D), F32)
            for at, _, size, own in segments():
                dst[at : at + size, :] = src[own : own + size, :]
            out[a] = dst[:count, :].astype(BF)


def pack(x, dy):
    return pl.pallas_call(
        pack_kernel,
        out_shape=(
            jax.ShapeDtypeStruct((2, LATN, D), BF),
            jax.ShapeDtypeStruct((2, LONN, D), BF),
            jax.ShapeDtypeStruct((2, DIAGN, D), BF),
        ),
        scratch_shapes=[pltpu.VMEM((ROWS, D), F32), pltpu.VMEM((LATN, D), F32)],
        compiler_params=params(12),
        cost_estimate=cost(1e6, 4e6),
        name="pack",
    )(x, dy)


def assemble(a, ref, lat_ref, lon_ref, diag_ref, src, win):
    for lev in range(LEV):
        for r in range(3, NR):
            at = (lev * NR + r) * NC
            src[at : at + NC, :] = ref[lev, r].astype(F32)
    for own, at, size in own_segments():
        win[at : at + size, :] = src[own : own + size, :]
    for halo, segments in ((lat_ref, lat_segments), (lon_ref, lon_segments), (diag_ref, diag_segments)):
        count = halo.shape[1]
        src[:count, :] = halo[a].astype(F32)
        for here, at, size, _ in segments():
            win[at : at + size, :] = src[here : here + size, :]


def layer_stats(x):
    mean = jnp.mean(x, -1, keepdims=True)
    cen = x - mean
    inv = lax.rsqrt(jnp.mean(cen * cen, -1, keepdims=True) + EPS)
    return cen, inv


def main_kernel(
    x_ref, dy_ref, lat_ref, lon_ref, diag_ref, gain_ref, wq_ref, wp_ref,
    keep_ref, send_ref, gact_ref, xw_ref, dyw_ref,
    src, win, nrm, qkv, gatt, att, normt,
):
    core = lax.axis_index("c")
    last = jnp.logical_and(lax.axis_index("y") == 3, lax.axis_index("xl") == 1)
    assemble(0, x_ref, lat_ref, lon_ref, diag_ref, src, win)
    for w in range(NWIN):
        rows = slice(w * TOK, (w + 1) * TOK)
        x = win[rows, :]
        xw_ref[rows, :] = x.astype(BF)
        cen, inv = layer_stats(x)
        nrm[rows, :] = (cen * inv * gain_ref[...]).astype(BF)
    assemble(1, dy_ref, lat_ref, lon_ref, diag_ref, src, win)
    for w in range(NWIN):
        rows = slice(w * TOK, (w + 1) * TOK)
        dyw_ref[rows, :] = win[rows, :].astype(BF)
    for j in range(6):
        cols = slice(j * 256, (j + 1) * 256)
        qkv[:, cols] = dot(nrm[...], wq_ref[:, cols], NN).astype(BF)
    for j in range(2):
        cols = slice(j * 256, (j + 1) * 256)
        gatt[:, cols] = dot(dyw_ref[...], wp_ref[cols, :], NT).astype(BF)

    low = lax.broadcasted_iota(jnp.int32, (TOK, 128), 1) < 64
    keyg = (lax.broadcasted_iota(jnp.int32, (TOK, 2 * TOK), 0) // 12) % 6 < 3
    qryg = (lax.broadcasted_iota(jnp.int32, (TOK, 2 * TOK), 1) // 12) % 6 < 3
    apart = jnp.logical_and(keyg != qryg, last)

    def stacked(v):
        z = jnp.zeros_like(v)
        return jnp.concatenate([jnp.where(low, v, z), jnp.where(low, z, v)], axis=0)

    for w in range(NWIN):
        rows = slice(w * TOK, (w + 1) * TOK)
        for hp in range(4):
            at = hp * 128
            q2 = stacked(qkv[rows, at : at + 128] * jnp.bfloat16(0.125))
            k = qkv[rows, HH + at : HH + at + 128]
            v = qkv[rows, 2 * HH + at : 2 * HH + at + 128]
            g2 = stacked(gatt[rows, at : at + 128])
            s = dot(k, q2, NT)
            if w >= 2:
                s = jnp.where(apart, -1000000000.0, s)
            e = jnp.exp(s - jnp.max(s, 0, keepdims=True))
            p = e * (1.0 / jnp.sum(e, 0, keepdims=True))
            pb = p.astype(BF)
            dp = dot(v, g2, NT)
            ds = (p * (dp - jnp.sum(p * dp, 0, keepdims=True))).astype(BF)
            o = dot(pb, v, TN)
            att[rows, at : at + 128] = jnp.where(low, o[:TOK], o[TOK:]).astype(BF)
            dq = dot(ds, k, TN)
            gact_ref[rows, at : at + 128] = (jnp.where(low, dq[:TOK], dq[TOK:]) * 0.125).astype(BF)
            gact_ref[rows, HH + at : HH + at + 128] = dot(ds, q2, NN).astype(BF)
            gact_ref[rows, 2 * HH + at : 2 * HH + at + 128] = dot(pb, g2, NN).astype(BF)

    def put(slot_is_low, rows, cols, value):
        @pl.when(core == slot_is_low)
        def _():
            keep_ref[rows, cols] = value

        @pl.when(core != slot_is_low)
        def _():
            send_ref[rows, cols] = value

    normt[...] = nrm[...].T
    for i in range(4):
        rows = slice(i * 256, (i + 1) * 256)
        lhs = normt[rows, :]
        put(0, rows, slice(0, 1024), dot(lhs, gact_ref[:, 0:1024], NN).astype(BF))
        put(1, rows, slice(0, 512), dot(lhs, gact_ref[:, 1024:1536], NN).astype(BF))
    normt[...] = dyw_ref[...].T
    for i in range(4):
        rows = slice(i * 256, (i + 1) * 256)
        put(1, rows, slice(512, 1024), dot(normt[rows, :], att[...], NN).astype(BF))


def main_call(x, dy, lat, lon, diag, gain, wq, wp):
    return pl.pallas_call(
        main_kernel,
        out_shape=(
            jax.ShapeDtypeStruct((D, 1024), BF),
            jax.ShapeDtypeStruct((D, 1024), BF),
            jax.ShapeDtypeStruct((ROWS, 1536), BF),
            jax.ShapeDtypeStruct((ROWS, D), BF),
            jax.ShapeDtypeStruct((ROWS, D), BF),
        ),
        scratch_shapes=[
            pltpu.VMEM((ROWS, D), F32),
            pltpu.VMEM((ROWS, D), F32),
            pltpu.VMEM((ROWS, D), BF),
            pltpu.VMEM((ROWS, 1536), BF),
            pltpu.VMEM((ROWS, HH), BF),
            pltpu.VMEM((ROWS, HH), BF),
            pltpu.VMEM((D, ROWS), BF),
        ],
        compiler_params=params(36),
        cost_estimate=cost(5.5e9, 14e6),
        name="main",
    )(x, dy, lat, lon, diag, gain, wq, wp)


def input_rows(w, gact_ref, xw_ref, dyw_ref, gain, wq_ref, win):
    rows = slice(w * TOK, (w + 1) * TOK)
    gn = dot(gact_ref[rows, :], wq_ref[...], NT)
    cen, inv = layer_stats(xw_ref[rows, :].astype(F32))
    xhat = cen * inv
    g = gn * gain
    win[rows, :] = dyw_ref[rows, :].astype(F32) + inv * (
        g - jnp.mean(g, -1, keepdims=True) - xhat * jnp.mean(g * xhat, -1, keepdims=True)
    )
    return jnp.sum(gn * xhat, 0, keepdims=True)


def input_low_kernel(
    gact_ref, xw_ref, dyw_ref, gain_ref, wq_ref, own_ref, lat_ref, lon_ref, diag_ref, gg_ref, win, dst
):
    gain = gain_ref[...]
    gg_ref[...] = sum(input_rows(w, gact_ref, xw_ref, dyw_ref, gain, wq_ref, win) for w in (2, 3))
    for out, segments in ((lat_ref, lat_segments()), (lon_ref, lon_out_segments(0)), (diag_ref, diag_segments())):
        count = out.shape[0]
        dst[count - 16 : count, :] = jnp.zeros((16, D), F32)
        for at, here, size, _ in segments:
            dst[at : at + size, :] = win[here : here + size, :]
        out[...] = dst[:count, :].astype(BF)
    for own, here, size in own_segments():
        if here >= 2 * TOK:
            dst[own : own + size, :] = win[here : here + size, :]
    for lev in range(LEV):
        for r in range(9, NR):
            at = (lev * NR + r) * NC
            own_ref[lev, r - 9] = dst[at : at + NC, :].astype(BF)


def input_high_kernel(gact_ref, xw_ref, dyw_ref, gain_ref, wq_ref, lon0_ref, gg0_ref, own_ref, lon_ref, gg_ref, win, dst):
    gain = gain_ref[...]
    acc = gg0_ref[...] + sum(input_rows(w, gact_ref, xw_ref, dyw_ref, gain, wq_ref, win) for w in (0, 1))
    for j in range(8):
        gg_ref[j : j + 1, :] = acc[:, j * 128 : (j + 1) * 128]
    lon_ref[0:48, :] = lon0_ref[...]
    dst[64:80, :] = jnp.zeros((16, D), F32)
    for at, here, size, _ in lon_out_segments(1):
        dst[at - 48 : at - 48 + size, :] = win[here : here + size, :]
    lon_ref[48:128, :] = dst[0:80, :].astype(BF)
    for own, here, size in own_segments():
        if here < 2 * TOK:
            dst[own : own + size, :] = win[here : here + size, :]
    for lev in range(LEV):
        for r in range(3, 9):
            at = (lev * NR + r) * NC
            own_ref[lev, r - 3] = dst[at : at + NC, :].astype(BF)


def lon_out_segments(part):
    for lev in range(LEV):
        for rr in (range(6, 9), range(6))[part]:
            at = (48 + (lev * 6 + rr) * 6) if part else (lev * 3 + rr - 6) * 6
            yield at, window_row(lev, rr, 18), 6, (lev * NR + rr + 3) * NC


def input_low_call(gact, xw, dyw, gain, wq):
    return pl.pallas_call(
        input_low_kernel,
        out_shape=(
            jax.ShapeDtypeStruct((LEV, 3, NC, D), BF),
            jax.ShapeDtypeStruct((LATN, D), BF),
            jax.ShapeDtypeStruct((48, D), BF),
            jax.ShapeDtypeStruct((DIAGN, D), BF),
            jax.ShapeDtypeStruct((1, D), F32),
        ),
        scratch_shapes=[pltpu.VMEM((ROWS, D), F32), pltpu.VMEM((ROWS, D), F32)],
        compiler_params=params(24),
        cost_estimate=cost(1e9, 9e6),
        name="input_low",
    )(gact, xw, dyw, gain, wq)


def input_high_call(gact, xw, dyw, gain, wq, lon0, gg0):
    return pl.pallas_call(
        input_high_kernel,
        out_shape=(
            jax.ShapeDtypeStruct((LEV, 6, NC, D), BF),
            jax.ShapeDtypeStruct((128, D), BF),
            jax.ShapeDtypeStruct((8, 128), F32),
        ),
        scratch_shapes=[pltpu.VMEM((ROWS, D), F32), pltpu.VMEM((ROWS, D), F32)],
        compiler_params=params(24),
        cost_estimate=cost(1e9, 9e6),
        name="input_high",
    )(gact, xw, dyw, gain, wq, lon0, gg0)


def join_kernel(high_ref, low_ref, lat_ref, lon_ref, diag_ref, out_ref, src, dst):
    for lev in range(LEV):
        for r in range(3, NR):
            at = (lev * NR + r) * NC
            part = high_ref[lev, r - 3] if r < 9 else low_ref[lev, r - 9]
            dst[at : at + NC, :] = part.astype(F32)
    lon_parts = [*lon_out_segments(0), *lon_out_segments(1)]
    for halo, segments in ((lat_ref, lat_segments()), (lon_ref, lon_parts), (diag_ref, diag_segments())):
        count = halo.shape[0]
        src[:count, :] = halo[...].astype(F32)
        for here, _, size, own in segments:
            dst[own : own + size, :] = src[here : here + size, :]
    for lev in range(LEV):
        for r in range(NR):
            at = (lev * NR + r) * NC
            out_ref[lev, r] = dst[at : at + NC, :].astype(BF)


def join_call(high, low, lat, lon, diag):
    return pl.pallas_call(
        join_kernel,
        out_shape=jax.ShapeDtypeStruct((LEV, NR, NC, D), BF),
        scratch_shapes=[pltpu.VMEM((128, D), F32), pltpu.VMEM((ROWS, D), F32)],
        compiler_params=params(12),
        cost_estimate=cost(1e6, 4e6),
        name="join",
    )(high, low, lat, lon, diag)


def split_kernel(keep_ref, recv_ref, own_ref, a_ref, b_ref, c_ref):
    y = lax.axis_index("y")
    for k, out in enumerate((own_ref, a_ref, b_ref, c_ref)):
        rows = pl.ds(pl.multiple_of(lax.rem(y + k, 4) * 256, 256), 256)
        out[...] = (keep_ref[rows, :].astype(F32) + recv_ref[rows, :].astype(F32)).astype(out.dtype)


def split_call(keep, recv):
    msg = jax.ShapeDtypeStruct((256, 1024), BF)
    return pl.pallas_call(
        split_kernel,
        out_shape=(jax.ShapeDtypeStruct((256, 1024), F32), msg, msg, msg),
        compiler_params=params(10),
        cost_estimate=cost(1e6, 8e6),
        name="split",
    )(keep, recv)


def gather_kernel(own_ref, a_ref, b_ref, c_ref, gg_ref, ga_ref, gb_ref, gc_ref, out_ref):
    gg = (gg_ref[...] + ga_ref[...] + gb_ref[...] + gc_ref[...]).astype(BF)
    for i in range(16):
        rows = slice(i * 16, (i + 1) * 16)
        total = own_ref[rows, :]
        for ref in (a_ref, b_ref, c_ref):
            total += ref[rows, :].astype(F32)
        total = total.astype(BF)
        for j in range(2):
            out_ref[2 * i + j, :, 0:1024] = total[j * 8 : (j + 1) * 8, :]
            out_ref[2 * i + j, :, 1024:1152] = gg


def gather_call(*operands):
    return pl.pallas_call(
        gather_kernel,
        out_shape=jax.ShapeDtypeStruct((32, 8, 1152), BF),
        compiler_params=params(6),
        cost_estimate=cost(1e6, 4e6),
        name="gather",
    )(*operands)


def shift(n, k):
    return [(i, (i + k) % n) for i in range(n)]


def shift_both(k):
    pairs = []
    for i in range(8):
        for j in range(32):
            pairs.append((i * 32 + j, ((i + k) % 8) * 32 + (j + k) % 32))
    return pairs


LAT = ("y", "xl")
LON = ("xh", "z", "c")
ALL = LAT + LON


def per_device(x, dy, gain, wq, wp):
    gain2 = gain.reshape(1, D)
    lat, lon, diag = pack(x, dy)
    lat = lax.ppermute(lat, LAT, shift(8, -1))
    lon = lax.ppermute(lon, LON, shift(32, -1))
    diag = lax.ppermute(diag, ALL, shift_both(-1))
    keep, send, gact, xw, dyw = main_call(x, dy, lat, lon, diag, gain2, wq, wp)
    recv = lax.ppermute(send, "c", [(0, 1), (1, 0)])
    low, lat, lon0, diag, gg0 = input_low_call(gact, xw, dyw, gain2, wq)
    recv, gg0 = lax.optimization_barrier((recv, gg0))
    mine, a, b, c = split_call(keep, recv)
    a = lax.ppermute(a, "y", shift(4, 1))
    b = lax.ppermute(b, "y", shift(4, 2))
    c = lax.ppermute(c, "y", shift(4, 3))
    gact, mine = lax.optimization_barrier((gact, mine))
    high, lon, gg = input_high_call(gact, xw, dyw, gain2, wq, lon0, gg0)
    lat = lax.ppermute(lat, LAT, shift(8, 1))
    lon = lax.ppermute(lon, LON, shift(32, 1))
    diag = lax.ppermute(diag, ALL, shift_both(1))
    ga, gb, gc = (lax.ppermute(gg, "y", shift(4, k)) for k in (1, 2, 3))
    a, b, c, ga, gb, gc, lat, lon, diag = lax.optimization_barrier((a, b, c, ga, gb, gc, lat, lon, diag))
    grad_in = join_call(high, low, lat, lon, diag)
    blocks = gather_call(mine, a, b, c, gg, ga, gb, gc)
    blocks = lax.all_to_all(blocks, ("xl", "xh", "z"), 0, 0, tiled=True)
    total = jnp.sum(blocks.astype(F32), 0)
    other = lax.ppermute(total, "c", [(0, 1), (1, 0)])
    core = lax.axis_index("c")
    first = jnp.where(core == 0, total, other)
    second = jnp.where(core == 0, other, total)
    first = lax.dynamic_slice_in_dim(first, core * 4, 4, 0)
    second4 = lax.dynamic_slice_in_dim(second, core * 4, 4, 0)
    factor = 1.0 / jnp.sqrt(F32(147456))
    grad_qkv = jnp.concatenate([first[:, :1024], second4[:, :512]], 1) * factor
    grad_proj = second4[:, 512:1024].T * factor
    gsum = (total[:, 1024:] + other[:, 1024:]).reshape(1024)
    index = lax.axis_index(LAT) * 32 + lax.axis_index(LON)
    grad_gain = lax.dynamic_slice_in_dim(gsum, index * 4, 4, 0) * factor
    return grad_in, grad_qkv, grad_proj, grad_gain


def solution(mesh):
    mesh = Mesh(mesh.devices.reshape(4, 2, 2, 8, 2), ALL)
    return jax.shard_map(
        per_device,
        mesh=mesh,
        in_specs=(P(None, LAT, LON, None), P(None, LAT, LON, None), P(), P(), P()),
        out_specs=(P(None, LAT, LON, None), P(ALL, None), P(None, ALL), P(ALL)),
        check_vma=False,
    )
```

```python
import functools

import jax
import jax.numpy as jnp
from jax import lax
from jax.experimental import pallas as pl
from jax.experimental.pallas import tpu as pltpu
from jax.sharding import Mesh, PartitionSpec as P

F32 = jnp.float32
BF = jnp.bfloat16
D = 1024
HH = 512
TOK = 144
NWIN = 4
ROWS = NWIN * TOK
LEV, NR, NC = 2, 12, 24
LATN = 112
LONN = 112
DIAGN = 48
EPS = 1e-05

NN = (((1,), (0,)), ((), ()))
NT = (((1,), (1,)), ((), ()))
TN = (((0,), (0,)), ((), ()))


def dot(a, b, dims):
    return lax.dot_general(a, b, dims, preferred_element_type=F32)


def params(mib):
    return pltpu.CompilerParams(vmem_limit_bytes=mib * 1024 * 1024)


def cost(flops, nbytes):
    return pl.CostEstimate(flops=int(flops), bytes_accessed=int(nbytes), transcendentals=0)


def window_row(lev, rr, cc):
    return ((rr // 6) * 2 + cc // 12) * TOK + lev * 72 + (rr % 6) * 12 + cc % 12


def own_segments():
    for lev in range(LEV):
        for rr in range(9):
            base = (lev * NR + rr + 3) * NC
            yield base + 6, window_row(lev, rr, 0), 12
            yield base + 18, window_row(lev, rr, 12), 6


def lat_segments():
    for lev in range(LEV):
        for r in range(3):
            base = (lev * 3 + r) * 18
            yield base, window_row(lev, 9 + r, 0), 12, (lev * NR + r) * NC + 6
            yield base + 12, window_row(lev, 9 + r, 12), 6, (lev * NR + r) * NC + 18


def lon_segments():
    for lev in range(LEV):
        for rr in range(9):
            yield (lev * 9 + rr) * 6, window_row(lev, rr, 18), 6, (lev * NR + rr + 3) * NC


def diag_segments():
    for lev in range(LEV):
        for r in range(3):
            yield (lev * 3 + r) * 6, window_row(lev, 9 + r, 18), 6, (lev * NR + r) * NC


def pack_kernel(x_ref, dy_ref, lat_ref, lon_ref, diag_ref, top, side, src, dst, sems):
    copies = []
    for a, ref in enumerate((x_ref, dy_ref)):
        copies.append(
            (
                pltpu.make_async_copy(ref.at[:, 0:3], top.at[a], sems.at[a, 0]),
                pltpu.make_async_copy(ref.at[:, 3:12, 0:8, :], side.at[a], sems.at[a, 1]),
            )
        )
    for pair in copies:
        for copy in pair:
            copy.start()
    for a, pair in enumerate(copies):
        pair[0].wait()
        for lev in range(LEV):
            for r in range(3):
                at = (lev * NR + r) * NC
                src[at : at + NC, :] = top[a, lev, r].astype(F32)
        pair[1].wait()
        for lev in range(LEV):
            for r in range(3, NR):
                at = (lev * NR + r) * NC
                src[at : at + 8, :] = side[a, lev, r - 3].astype(F32)
        for out, segments in ((lat_ref, lat_segments), (lon_ref, lon_segments), (diag_ref, diag_segments)):
            count = out.shape[1]
            dst[count - 16 : count, :] = jnp.zeros((16, D), F32)
            for at, _, size, own in segments():
                dst[at : at + size, :] = src[own : own + size, :]
            out[a] = dst[:count, :].astype(BF)


def pack(x, dy):
    return pl.pallas_call(
        pack_kernel,
        in_specs=[pl.BlockSpec(memory_space=pltpu.HBM)] * 2,
        out_shape=(
            jax.ShapeDtypeStruct((2, LATN, D), BF),
            jax.ShapeDtypeStruct((2, LONN, D), BF),
            jax.ShapeDtypeStruct((2, DIAGN, D), BF),
        ),
        scratch_shapes=[
            pltpu.VMEM((2, LEV, 3, NC, D), BF),
            pltpu.VMEM((2, LEV, 9, 8, D), BF),
            pltpu.VMEM((ROWS, D), F32),
            pltpu.VMEM((LATN, D), F32),
            pltpu.SemaphoreType.DMA((2, 2)),
        ],
        compiler_params=params(60),
        cost_estimate=cost(1e6, 4e6),
        name="pack",
    )(x, dy)


def copy_own(ref, src, win, local):
    for lev in range(LEV):
        for r in range(3, 9 if local else NR):
            at = (lev * NR + r) * NC
            src[at : at + NC, :] = ref[lev, r].astype(F32)
    for own, at, size in own_segments():
        if (at < TOK) == local:
            win[at : at + size, :] = src[own : own + size, :]


def assemble(a, ref, lat_ref, lon_ref, diag_ref, src, win):
    copy_own(ref, src, win, False)
    for halo, segments in ((lat_ref, lat_segments), (lon_ref, lon_segments), (diag_ref, diag_segments)):
        count = halo.shape[1]
        src[:count, :] = halo[a].astype(F32)
        for here, at, size, _ in segments():
            win[at : at + size, :] = src[here : here + size, :]


def layer_stats(x):
    mean = jnp.mean(x, -1, keepdims=True)
    cen = x - mean
    inv = lax.rsqrt(jnp.mean(cen * cen, -1, keepdims=True) + EPS)
    return cen, inv


def normalize(windows, win, gain_ref, xw_ref, nrm):
    for w in windows:
        rows = slice(w * TOK, (w + 1) * TOK)
        x = win[rows, :]
        xw_ref[rows, :] = x.astype(BF)
        cen, inv = layer_stats(x)
        nrm[rows, :] = (cen * inv * gain_ref[...]).astype(BF)


def project(rows, nrm, dyw_ref, wq_ref, wp_ref, qkv, gatt):
    for j in range(6):
        cols = slice(j * 256, (j + 1) * 256)
        qkv[rows, cols] = dot(nrm[rows, :], wq_ref[:, cols], NN).astype(BF)
    for j in range(2):
        cols = slice(j * 256, (j + 1) * 256)
        gatt[rows, cols] = dot(dyw_ref[rows, :], wp_ref[cols, :], NT).astype(BF)


def attend(windows, last, qkv, gatt, att, gact_ref):
    low = lax.broadcasted_iota(jnp.int32, (TOK, 128), 1) < 64
    keyg = (lax.broadcasted_iota(jnp.int32, (TOK, 2 * TOK), 0) // 12) % 6 < 3
    qryg = (lax.broadcasted_iota(jnp.int32, (TOK, 2 * TOK), 1) // 12) % 6 < 3

    def stacked(v):
        z = jnp.zeros_like(v)
        return jnp.concatenate([jnp.where(low, v, z), jnp.where(low, z, v)], axis=0)

    for w in windows:
        rows = slice(w * TOK, (w + 1) * TOK)
        for hp in range(4):
            at = hp * 128
            q2 = stacked(qkv[rows, at : at + 128] * jnp.bfloat16(0.125))
            k = qkv[rows, HH + at : HH + at + 128]
            v = qkv[rows, 2 * HH + at : 2 * HH + at + 128]
            g2 = stacked(gatt[rows, at : at + 128])
            s = dot(k, q2, NT)
            if w >= 2:
                s = jnp.where(jnp.logical_and(keyg != qryg, last), -1000000000.0, s)
            e = jnp.exp(s - jnp.max(s, 0, keepdims=True))
            p = e * (1.0 / jnp.sum(e, 0, keepdims=True))
            pb = p.astype(BF)
            dp = dot(v, g2, NT)
            ds = (p * (dp - jnp.sum(p * dp, 0, keepdims=True))).astype(BF)
            o = dot(pb, v, TN)
            att[rows, at : at + 128] = jnp.where(low, o[:TOK], o[TOK:]).astype(BF)
            dq = dot(ds, k, TN)
            gact_ref[rows, at : at + 128] = (jnp.where(low, dq[:TOK], dq[TOK:]) * 0.125).astype(BF)
            gact_ref[rows, HH + at : HH + at + 128] = dot(ds, q2, NN).astype(BF)
            gact_ref[rows, 2 * HH + at : 2 * HH + at + 128] = dot(pb, g2, NN).astype(BF)


def local_kernel(
    x_ref, dy_ref, gain_ref, wq_ref, wp_ref,
    nrm_ref, xw_ref, dyw_ref, gact_ref, att_ref,
    src, win, qkv, gatt,
):
    copy_own(x_ref, src, win, True)
    normalize((0,), win, gain_ref, xw_ref, nrm_ref)
    copy_own(dy_ref, src, win, True)
    dyw_ref[...] = win[...].astype(BF)
    project(slice(0, TOK), nrm_ref, dyw_ref, wq_ref, wp_ref, qkv, gatt)
    attend((0,), False, qkv, gatt, att_ref, gact_ref)


def local_call(x, dy, gain, wq, wp):
    wide = jax.ShapeDtypeStruct((TOK, D), BF)
    return pl.pallas_call(
        local_kernel,
        out_shape=(
            wide,
            wide,
            wide,
            jax.ShapeDtypeStruct((TOK, 1536), BF),
            jax.ShapeDtypeStruct((TOK, HH), BF),
        ),
        scratch_shapes=[
            pltpu.VMEM((ROWS, D), F32),
            pltpu.VMEM((TOK, D), F32),
            pltpu.VMEM((TOK, 1536), BF),
            pltpu.VMEM((TOK, HH), BF),
        ],
        compiler_params=params(16),
        cost_estimate=cost(2e9, 9e6),
        name="local",
    )(x, dy, gain, wq, wp)


def main_kernel(
    x_ref, dy_ref, lat_ref, lon_ref, diag_ref, gain_ref, wq_ref, wp_ref,
    nrm0_ref, xw0_ref, dyw0_ref, gact0_ref, att0_ref,
    keep_ref, send_ref, gact_ref, xw_ref, dyw_ref,
    src, win, nrm, qkv, gatt, att, normt,
):
    core = lax.axis_index("c")
    last = jnp.logical_and(lax.axis_index("y") == 3, lax.axis_index("xl") == 1)
    for to, at in ((nrm, nrm0_ref), (xw_ref, xw0_ref), (dyw_ref, dyw0_ref), (gact_ref, gact0_ref), (att, att0_ref)):
        to[0:TOK, :] = at[...]
    rest = slice(TOK, ROWS)
    assemble(0, x_ref, lat_ref, lon_ref, diag_ref, src, win)
    normalize((1, 2, 3), win, gain_ref, xw_ref, nrm)
    assemble(1, dy_ref, lat_ref, lon_ref, diag_ref, src, win)
    dyw_ref[rest, :] = win[rest, :].astype(BF)
    project(rest, nrm, dyw_ref, wq_ref, wp_ref, qkv, gatt)
    attend((1, 2, 3), last, qkv, gatt, att, gact_ref)

    def put(slot_is_low, rows, cols, value):
        @pl.when(core == slot_is_low)
        def _():
            keep_ref[rows, cols] = value

        @pl.when(core != slot_is_low)
        def _():
            send_ref[rows, cols] = value

    normt[...] = nrm[...].T
    for i in range(4):
        rows = slice(i * 256, (i + 1) * 256)
        lhs = normt[rows, :]
        put(0, rows, slice(0, 1024), dot(lhs, gact_ref[:, 0:1024], NN).astype(BF))
        put(1, rows, slice(0, 512), dot(lhs, gact_ref[:, 1024:1536], NN).astype(BF))
    normt[...] = dyw_ref[...].T
    for i in range(4):
        rows = slice(i * 256, (i + 1) * 256)
        put(1, rows, slice(512, 1024), dot(normt[rows, :], att[...], NN).astype(BF))


def main_call(*operands):
    return pl.pallas_call(
        main_kernel,
        out_shape=(
            jax.ShapeDtypeStruct((D, 1024), BF),
            jax.ShapeDtypeStruct((D, 1024), BF),
            jax.ShapeDtypeStruct((ROWS, 1536), BF),
            jax.ShapeDtypeStruct((ROWS, D), BF),
            jax.ShapeDtypeStruct((ROWS, D), BF),
        ),
        scratch_shapes=[
            pltpu.VMEM((ROWS, D), F32),
            pltpu.VMEM((ROWS, D), F32),
            pltpu.VMEM((ROWS, D), BF),
            pltpu.VMEM((ROWS, 1536), BF),
            pltpu.VMEM((ROWS, HH), BF),
            pltpu.VMEM((ROWS, HH), BF),
            pltpu.VMEM((D, ROWS), BF),
        ],
        compiler_params=params(32),
        cost_estimate=cost(5.5e9, 14e6),
        name="main",
    )(*operands)


def input_rows(w, gact_ref, xw_ref, dyw_ref, gain, wq_ref, win):
    rows = slice(w * TOK, (w + 1) * TOK)
    gn = dot(gact_ref[rows, :], wq_ref[...], NT)
    cen, inv = layer_stats(xw_ref[rows, :].astype(F32))
    xhat = cen * inv
    g = gn * gain
    win[rows, :] = dyw_ref[rows, :].astype(F32) + inv * (
        g - jnp.mean(g, -1, keepdims=True) - xhat * jnp.mean(g * xhat, -1, keepdims=True)
    )
    return jnp.sum(gn * xhat, 0, keepdims=True)


def input_low_kernel(
    gact_ref, xw_ref, dyw_ref, gain_ref, wq_ref, own_ref, lat_ref, lon_ref, diag_ref, gg_ref, win, dst
):
    gain = gain_ref[...]
    gg_ref[...] = sum(input_rows(w, gact_ref, xw_ref, dyw_ref, gain, wq_ref, win) for w in (2, 3))
    for out, segments in ((lat_ref, lat_segments()), (lon_ref, lon_out_segments(0)), (diag_ref, diag_segments())):
        count = out.shape[0]
        dst[count - 16 : count, :] = jnp.zeros((16, D), F32)
        for at, here, size, _ in segments:
            dst[at : at + size, :] = win[here : here + size, :]
        out[...] = dst[:count, :].astype(BF)
    for own, here, size in own_segments():
        if here >= 2 * TOK:
            dst[own : own + size, :] = win[here : here + size, :]
    for lev in range(LEV):
        for r in range(9, NR):
            at = (lev * NR + r) * NC
            own_ref[lev, r - 9] = dst[at : at + NC, :].astype(BF)


def input_high_kernel(gact_ref, xw_ref, dyw_ref, gain_ref, wq_ref, lon0_ref, gg0_ref, own_ref, lon_ref, gg_ref, win, dst):
    gain = gain_ref[...]
    acc = gg0_ref[...] + sum(input_rows(w, gact_ref, xw_ref, dyw_ref, gain, wq_ref, win) for w in (0, 1))
    for j in range(8):
        gg_ref[j : j + 1, :] = acc[:, j * 128 : (j + 1) * 128]
    lon_ref[0:48, :] = lon0_ref[...]
    dst[64:80, :] = jnp.zeros((16, D), F32)
    for at, here, size, _ in lon_out_segments(1):
        dst[at - 48 : at - 48 + size, :] = win[here : here + size, :]
    lon_ref[48:128, :] = dst[0:80, :].astype(BF)
    for own, here, size in own_segments():
        if here < 2 * TOK:
            dst[own : own + size, :] = win[here : here + size, :]
    for lev in range(LEV):
        for r in range(3, 9):
            at = (lev * NR + r) * NC
            own_ref[lev, r - 3] = dst[at : at + NC, :].astype(BF)


def lon_out_segments(part):
    for lev in range(LEV):
        for rr in (range(6, 9), range(6))[part]:
            at = (48 + (lev * 6 + rr) * 6) if part else (lev * 3 + rr - 6) * 6
            yield at, window_row(lev, rr, 18), 6, (lev * NR + rr + 3) * NC


def input_low_call(gact, xw, dyw, gain, wq):
    return pl.pallas_call(
        input_low_kernel,
        out_shape=(
            jax.ShapeDtypeStruct((LEV, 3, NC, D), BF),
            jax.ShapeDtypeStruct((LATN, D), BF),
            jax.ShapeDtypeStruct((48, D), BF),
            jax.ShapeDtypeStruct((DIAGN, D), BF),
            jax.ShapeDtypeStruct((1, D), F32),
        ),
        scratch_shapes=[pltpu.VMEM((ROWS, D), F32), pltpu.VMEM((ROWS, D), F32)],
        compiler_params=params(24),
        cost_estimate=cost(1e9, 9e6),
        name="input_low",
    )(gact, xw, dyw, gain, wq)


def input_high_call(gact, xw, dyw, gain, wq, lon0, gg0):
    return pl.pallas_call(
        input_high_kernel,
        out_shape=(
            jax.ShapeDtypeStruct((LEV, 6, NC, D), BF),
            jax.ShapeDtypeStruct((128, D), BF),
            jax.ShapeDtypeStruct((8, 128), F32),
        ),
        scratch_shapes=[pltpu.VMEM((ROWS, D), F32), pltpu.VMEM((ROWS, D), F32)],
        compiler_params=params(24),
        cost_estimate=cost(1e9, 9e6),
        name="input_high",
    )(gact, xw, dyw, gain, wq, lon0, gg0)


def join_kernel(high_ref, low_ref, lat_ref, lon_ref, diag_ref, out_ref, src, dst):
    for lev in range(LEV):
        for r in range(3, NR):
            at = (lev * NR + r) * NC
            part = high_ref[lev, r - 3] if r < 9 else low_ref[lev, r - 9]
            dst[at : at + NC, :] = part.astype(F32)
    lon_parts = [*lon_out_segments(0), *lon_out_segments(1)]
    for halo, segments in ((lat_ref, lat_segments()), (lon_ref, lon_parts), (diag_ref, diag_segments())):
        count = halo.shape[0]
        src[:count, :] = halo[...].astype(F32)
        for here, _, size, own in segments:
            dst[own : own + size, :] = src[here : here + size, :]
    for lev in range(LEV):
        for r in range(NR):
            at = (lev * NR + r) * NC
            out_ref[lev, r] = dst[at : at + NC, :].astype(BF)


def join_call(high, low, lat, lon, diag):
    return pl.pallas_call(
        join_kernel,
        out_shape=jax.ShapeDtypeStruct((LEV, NR, NC, D), BF),
        scratch_shapes=[pltpu.VMEM((128, D), F32), pltpu.VMEM((ROWS, D), F32)],
        compiler_params=params(12),
        cost_estimate=cost(1e6, 4e6),
        name="join",
    )(high, low, lat, lon, diag)


MSG = 272


def x_of():
    return lax.axis_index("xh") * 2 + lax.axis_index("xl")


def x_block(x):
    return lax.rem(x, 2) * 2 + x // 2


def put_gain(out, at, gg):
    hi = gg.astype(BF)
    out[at : at + 16, :] = jnp.zeros((16, 512), BF)
    out[at : at + 8, 0:128] = hi
    out[at : at + 8, 128:256] = (gg - hi.astype(F32)).astype(BF)


def take_gain(ref, at):
    return ref[at : at + 8, 0:128].astype(F32) + ref[at : at + 8, 128:256].astype(F32)


def split_kernel(keep_ref, recv_ref, gg_ref, owna, a1, a2, a3, ownb, b1, b2, b3):
    y = lax.axis_index("y")
    x = x_of()

    def total(rows, cols):
        return keep_ref[rows, cols].astype(F32) + recv_ref[rows, cols].astype(F32)

    for k, out in enumerate((owna, a1, a2, a3)):
        rows = pl.ds(pl.multiple_of(lax.rem(y + k, 4) * 256, 256), 256)
        out[0:256, :] = total(rows, slice(0, 512)).astype(out.dtype)
        if k:
            put_gain(out, 256, gg_ref[...])
    for k, out in enumerate((ownb, b1, b2, b3)):
        block = x_block(lax.rem(x + k, 4))
        for j in range(4):
            rows = pl.ds(pl.multiple_of(j * 256 + block * 64, 64), 64)
            out[j * 64 : (j + 1) * 64, :] = total(rows, slice(512, 1024)).astype(out.dtype)


def split_call(keep, recv, gg):
    mine = jax.ShapeDtypeStruct((256, 512), F32)
    a = jax.ShapeDtypeStruct((MSG, 512), BF)
    b = jax.ShapeDtypeStruct((256, 512), BF)
    return pl.pallas_call(
        split_kernel,
        out_shape=(mine, a, a, a, mine, b, b, b),
        compiler_params=params(12),
        cost_estimate=cost(1e6, 8e6),
        name="split",
    )(keep, recv, gg)


def cross_kernel(owna, a1, a2, a3, ownb, b1, b2, b3, gg_ref, gout, nowna, na1, na2, na3, nownb, nb1, nb2, nb3):
    y = lax.axis_index("y")
    x = x_of()
    gg = gg_ref[...] + take_gain(a1, 256) + take_gain(a2, 256) + take_gain(a3, 256)
    gout[...] = gg

    def total(rows, own, refs):
        value = own[rows, :]
        for ref in refs:
            value += ref[rows, :].astype(F32)
        return value

    for k, out in enumerate((nowna, na1, na2, na3)):
        rows = pl.ds(pl.multiple_of(x_block(lax.rem(x + k, 4)) * 64, 64), 64)
        out[0:64, :] = total(rows, owna, (a1, a2, a3)).astype(out.dtype)
        if k:
            put_gain(out, 64, gg)
    for k, out in enumerate((nownb, nb1, nb2, nb3)):
        rows = pl.ds(pl.multiple_of(lax.rem(y + k, 4) * 64, 64), 64)
        out[...] = total(rows, ownb, (b1, b2, b3)).astype(out.dtype)


def cross_call(*operands):
    mine = jax.ShapeDtypeStruct((64, 512), F32)
    a = jax.ShapeDtypeStruct((80, 512), BF)
    b = jax.ShapeDtypeStruct((64, 512), BF)
    return pl.pallas_call(
        cross_kernel,
        out_shape=(jax.ShapeDtypeStruct((8, 128), F32), mine, a, a, a, mine, b, b, b),
        compiler_params=params(8),
        cost_estimate=cost(1e6, 4e6),
        name="cross",
    )(*operands)


def gather_kernel(owna, a1, a2, a3, ownb, b1, b2, b3, gg_ref, out_ref):
    gg = gg_ref[...] + take_gain(a1, 64) + take_gain(a2, 64) + take_gain(a3, 64)
    hi = gg.astype(BF)
    lo = (gg - hi.astype(F32)).astype(BF)
    for i in range(4):
        rows = slice(i * 16, (i + 1) * 16)
        for at, own, refs in ((0, owna, (a1, a2, a3)), (512, ownb, (b1, b2, b3))):
            value = own[rows, :]
            for ref in refs:
                value += ref[rows, :].astype(F32)
            for j in range(2):
                out_ref[2 * i + j, :, at : at + 512] = value[j * 8 : (j + 1) * 8, :].astype(BF)
        for j in range(2):
            out_ref[2 * i + j, :, 1024:1152] = hi
            out_ref[2 * i + j, :, 1152:1280] = lo


def gather_call(*operands):
    return pl.pallas_call(
        gather_kernel,
        out_shape=jax.ShapeDtypeStruct((8, 8, 1280), BF),
        compiler_params=params(6),
        cost_estimate=cost(1e6, 4e6),
        name="gather",
    )(*operands)


def shift_x(value, k):
    pairs = []
    for xl in range(2):
        for xh in range(2):
            to = (xh * 2 + xl + k) % 4
            pairs.append((xl * 2 + xh, (to % 2) * 2 + to // 2))
    return lax.ppermute(value, ("xl", "xh"), pairs)


def shift_y(value, k):
    return lax.ppermute(value, "y", shift(4, k))


def shift(n, k):
    return [(i, (i + k) % n) for i in range(n)]


def shift_both(k):
    pairs = []
    for i in range(8):
        for j in range(32):
            pairs.append((i * 32 + j, ((i + k) % 8) * 32 + (j + k) % 32))
    return pairs


LAT = ("y", "xl")
LON = ("xh", "z", "c")
ALL = LAT + LON


def per_device(x, dy, gain, wq, wp):
    gain2 = gain.reshape(1, D)
    lat, lon, diag = pack(x, dy)
    lat = lax.ppermute(lat, LAT, shift(8, -1))
    lon = lax.ppermute(lon, LON, shift(32, -1))
    diag = lax.ppermute(diag, ALL, shift_both(-1))
    early = local_call(x, dy, gain2, wq, wp)
    keep, send, gact, xw, dyw = main_call(x, dy, lat, lon, diag, gain2, wq, wp, *early)
    recv = lax.ppermute(send, "c", [(0, 1), (1, 0)])
    low, lat, lon0, diag, gg0 = input_low_call(gact, xw, dyw, gain2, wq)
    high, lon, gg = input_high_call(gact, xw, dyw, gain2, wq, lon0, gg0)
    oa, a1, a2, a3, ob, b1, b2, b3 = split_call(keep, recv, gg)
    a1, a2, a3 = (shift_y(v, k) for k, v in ((1, a1), (2, a2), (3, a3)))
    b1, b2, b3 = (shift_x(v, k) for k, v in ((1, b1), (2, b2), (3, b3)))
    lat = lax.ppermute(lat, LAT, shift(8, 1))
    lon = lax.ppermute(lon, LON, shift(32, 1))
    diag = lax.ppermute(diag, ALL, shift_both(1))
    gg, oa, a1, a2, a3, ob, b1, b2, b3 = cross_call(oa, a1, a2, a3, ob, b1, b2, b3, gg)
    a1, a2, a3 = (shift_x(v, k) for k, v in ((1, a1), (2, a2), (3, a3)))
    b1, b2, b3 = (shift_y(v, k) for k, v in ((1, b1), (2, b2), (3, b3)))
    a1, lat, lon, diag = lax.optimization_barrier((a1, lat, lon, diag))
    grad_in = join_call(high, low, lat, lon, diag)
    blocks = gather_call(oa, a1, a2, a3, ob, b1, b2, b3, gg)
    blocks = lax.all_to_all(blocks, "z", 0, 0, tiled=True)
    total = jnp.sum(blocks.astype(F32), 0)
    total = jnp.concatenate([total[:, :1024], total[:, 1024:1152] + total[:, 1152:1280]], 1)
    other = lax.ppermute(total, "c", [(0, 1), (1, 0)])
    core = lax.axis_index("c")
    first = jnp.where(core == 0, total, other)
    second = jnp.where(core == 0, other, total)
    first = lax.dynamic_slice_in_dim(first, core * 4, 4, 0)
    second4 = lax.dynamic_slice_in_dim(second, core * 4, 4, 0)
    factor = 1.0 / jnp.sqrt(F32(147456))
    grad_qkv = jnp.concatenate([first[:, :1024], second4[:, :512]], 1) * factor
    grad_proj = second4[:, 512:1024].T * factor
    gsum = (total[:, 1024:] + other[:, 1024:]).reshape(1024)
    index = lax.axis_index(LAT) * 32 + lax.axis_index(LON)
    grad_gain = lax.dynamic_slice_in_dim(gsum, index * 4, 4, 0) * factor
    return grad_in, grad_qkv, grad_proj, grad_gain


def solution(mesh):
    mesh = Mesh(mesh.devices.reshape(4, 2, 2, 8, 2), ALL)
    return jax.shard_map(
        per_device,
        mesh=mesh,
        in_specs=(P(None, LAT, LON, None), P(None, LAT, LON, None), P(), P(), P()),
        out_specs=(P(None, LAT, LON, None), P(ALL, None), P(None, ALL), P(ALL)),
        check_vma=False,
    )
```

```python
import functools

import jax
import jax.numpy as jnp
from jax import lax
from jax.experimental import pallas as pl
from jax.experimental.pallas import tpu as pltpu
from jax.sharding import Mesh, PartitionSpec as P

F32 = jnp.float32
BF = jnp.bfloat16
D = 1024
HH = 512
TOK = 144
NWIN = 4
ROWS = NWIN * TOK
LEV, NR, NC = 2, 12, 24
LATN = 112
LONN = 112
DIAGN = 48
EPS = 1e-05
FACTOR = 1.0 / 384.0

NN = (((1,), (0,)), ((), ()))
NT = (((1,), (1,)), ((), ()))
TN = (((0,), (0,)), ((), ()))


def dot(a, b, dims):
    return lax.dot_general(a, b, dims, preferred_element_type=F32)


def params(mib):
    return pltpu.CompilerParams(vmem_limit_bytes=mib * 1024 * 1024)


def cost(flops, nbytes):
    return pl.CostEstimate(flops=int(flops), bytes_accessed=int(nbytes), transcendentals=0)


def window_row(lev, rr, cc):
    return ((rr // 6) * 2 + cc // 12) * TOK + lev * 72 + (rr % 6) * 12 + cc % 12


def own_segments():
    for lev in range(LEV):
        for rr in range(9):
            base = (lev * NR + rr + 3) * NC
            yield base + 6, window_row(lev, rr, 0), 12
            yield base + 18, window_row(lev, rr, 12), 6


def lat_segments():
    for lev in range(LEV):
        for r in range(3):
            base = (lev * 3 + r) * 18
            yield base, window_row(lev, 9 + r, 0), 12, (lev * NR + r) * NC + 6
            yield base + 12, window_row(lev, 9 + r, 12), 6, (lev * NR + r) * NC + 18


def lon_segments():
    for lev in range(LEV):
        for rr in range(9):
            yield (lev * 9 + rr) * 6, window_row(lev, rr, 18), 6, (lev * NR + rr + 3) * NC


def diag_segments():
    for lev in range(LEV):
        for r in range(3):
            yield (lev * 3 + r) * 6, window_row(lev, 9 + r, 18), 6, (lev * NR + r) * NC


def pack_kernel(x_ref, dy_ref, lat_ref, lon_ref, diag_ref, top, side, src, dst, sems):
    copies = []
    for a, ref in enumerate((x_ref, dy_ref)):
        copies.append(
            (
                pltpu.make_async_copy(ref.at[:, 0:3], top.at[a], sems.at[a, 0]),
                pltpu.make_async_copy(ref.at[:, 3:12, 0:8, :], side.at[a], sems.at[a, 1]),
            )
        )
    for pair in copies:
        for copy in pair:
            copy.start()
    for a, pair in enumerate(copies):
        pair[0].wait()
        for lev in range(LEV):
            for r in range(3):
                at = (lev * NR + r) * NC
                src[at : at + NC, :] = top[a, lev, r].astype(F32)
        pair[1].wait()
        for lev in range(LEV):
            for r in range(3, NR):
                at = (lev * NR + r) * NC
                src[at : at + 8, :] = side[a, lev, r - 3].astype(F32)
        for out, segments in ((lat_ref, lat_segments), (lon_ref, lon_segments), (diag_ref, diag_segments)):
            count = out.shape[1]
            dst[count - 16 : count, :] = jnp.zeros((16, D), F32)
            for at, _, size, own in segments():
                dst[at : at + size, :] = src[own : own + size, :]
            out[a] = dst[:count, :].astype(BF)


def pack(x, dy):
    return pl.pallas_call(
        pack_kernel,
        in_specs=[pl.BlockSpec(memory_space=pltpu.HBM)] * 2,
        out_shape=(
            jax.ShapeDtypeStruct((2, LATN, D), BF),
            jax.ShapeDtypeStruct((2, LONN, D), BF),
            jax.ShapeDtypeStruct((2, DIAGN, D), BF),
        ),
        scratch_shapes=[
            pltpu.VMEM((2, LEV, 3, NC, D), BF),
            pltpu.VMEM((2, LEV, 9, 8, D), BF),
            pltpu.VMEM((ROWS, D), F32),
            pltpu.VMEM((LATN, D), F32),
            pltpu.SemaphoreType.DMA((2, 2)),
        ],
        compiler_params=params(60),
        cost_estimate=cost(1e6, 4e6),
        name="pack",
    )(x, dy)


def copy_own(ref, src, win, local):
    for lev in range(LEV):
        for r in range(3, 9 if local else NR):
            at = (lev * NR + r) * NC
            src[at : at + NC, :] = ref[lev, r].astype(F32)
    for own, at, size in own_segments():
        if (at < TOK) == local:
            win[at : at + size, :] = src[own : own + size, :]


def assemble(a, ref, lat_ref, lon_ref, diag_ref, src, win):
    copy_own(ref, src, win, False)
    for halo, segments in ((lat_ref, lat_segments), (lon_ref, lon_segments), (diag_ref, diag_segments)):
        count = halo.shape[1]
        src[:count, :] = halo[a].astype(F32)
        for here, at, size, _ in segments():
            win[at : at + size, :] = src[here : here + size, :]


def layer_stats(x):
    mean = jnp.mean(x, -1, keepdims=True)
    cen = x - mean
    inv = lax.rsqrt(jnp.mean(cen * cen, -1, keepdims=True) + EPS)
    return cen, inv


def normalize(windows, win, gain_ref, xw_ref, nrm):
    for w in windows:
        rows = slice(w * TOK, (w + 1) * TOK)
        x = win[rows, :]
        xw_ref[rows, :] = x.astype(BF)
        cen, inv = layer_stats(x)
        nrm[rows, :] = (cen * inv * gain_ref[...]).astype(BF)


def project(rows, nrm, dyw_ref, wq_ref, wp_ref, qkv, gatt):
    for j in range(6):
        cols = slice(j * 256, (j + 1) * 256)
        qkv[rows, cols] = dot(nrm[rows, :], wq_ref[:, cols], NN).astype(BF)
    for j in range(2):
        cols = slice(j * 256, (j + 1) * 256)
        gatt[rows, cols] = dot(dyw_ref[rows, :], wp_ref[cols, :], NT).astype(BF)


def attend(windows, last, qkv, gatt, att, gact_ref):
    low = lax.broadcasted_iota(jnp.int32, (TOK, 128), 1) < 64
    keyg = (lax.broadcasted_iota(jnp.int32, (TOK, 2 * TOK), 0) // 12) % 6 < 3
    qryg = (lax.broadcasted_iota(jnp.int32, (TOK, 2 * TOK), 1) // 12) % 6 < 3

    def stacked(v):
        z = jnp.zeros_like(v)
        return jnp.concatenate([jnp.where(low, v, z), jnp.where(low, z, v)], axis=0)

    for w in windows:
        rows = slice(w * TOK, (w + 1) * TOK)
        for hp in range(4):
            at = hp * 128
            q2 = stacked(qkv[rows, at : at + 128] * jnp.bfloat16(0.125))
            k = qkv[rows, HH + at : HH + at + 128]
            v = qkv[rows, 2 * HH + at : 2 * HH + at + 128]
            g2 = stacked(gatt[rows, at : at + 128])
            s = dot(k, q2, NT)
            if w >= 2:
                s = jnp.where(jnp.logical_and(keyg != qryg, last), -1000000000.0, s)
            e = jnp.exp(s - jnp.max(s, 0, keepdims=True))
            p = e * (1.0 / jnp.sum(e, 0, keepdims=True))
            pb = p.astype(BF)
            dp = dot(v, g2, NT)
            ds = (p * (dp - jnp.sum(p * dp, 0, keepdims=True))).astype(BF)
            o = dot(pb, v, TN)
            att[rows, at : at + 128] = jnp.where(low, o[:TOK], o[TOK:]).astype(BF)
            dq = dot(ds, k, TN)
            gact_ref[rows, at : at + 128] = (jnp.where(low, dq[:TOK], dq[TOK:]) * 0.125).astype(BF)
            gact_ref[rows, HH + at : HH + at + 128] = dot(ds, q2, NN).astype(BF)
            gact_ref[rows, 2 * HH + at : 2 * HH + at + 128] = dot(pb, g2, NN).astype(BF)


def local_kernel(
    x_ref, dy_ref, gain_ref, wq_ref, wp_ref,
    nrm_ref, xw_ref, dyw_ref, gact_ref, att_ref,
    src, win, qkv, gatt,
):
    copy_own(x_ref, src, win, True)
    normalize((0,), win, gain_ref, xw_ref, nrm_ref)
    copy_own(dy_ref, src, win, True)
    dyw_ref[...] = win[...].astype(BF)
    project(slice(0, TOK), nrm_ref, dyw_ref, wq_ref, wp_ref, qkv, gatt)
    attend((0,), False, qkv, gatt, att_ref, gact_ref)


def local_call(x, dy, gain, wq, wp):
    wide = jax.ShapeDtypeStruct((TOK, D), BF)
    return pl.pallas_call(
        local_kernel,
        out_shape=(
            wide,
            wide,
            wide,
            jax.ShapeDtypeStruct((TOK, 1536), BF),
            jax.ShapeDtypeStruct((TOK, HH), BF),
        ),
        scratch_shapes=[
            pltpu.VMEM((ROWS, D), F32),
            pltpu.VMEM((TOK, D), F32),
            pltpu.VMEM((TOK, 1536), BF),
            pltpu.VMEM((TOK, HH), BF),
        ],
        compiler_params=params(16),
        cost_estimate=cost(2e9, 9e6),
        name="local",
    )(x, dy, gain, wq, wp)


def main_kernel(
    x_ref, dy_ref, lat_ref, lon_ref, diag_ref, gain_ref, wq_ref, wp_ref,
    nrm0_ref, xw0_ref, dyw0_ref, gact0_ref, att0_ref,
    keep_ref, send_ref, gact_ref, xw_ref, dyw_ref,
    src, win, nrm, qkv, gatt, att, normt,
):
    core = lax.axis_index("c")
    last = jnp.logical_and(lax.axis_index("y") == 3, lax.axis_index("xl") == 1)
    for to, at in ((nrm, nrm0_ref), (xw_ref, xw0_ref), (dyw_ref, dyw0_ref), (gact_ref, gact0_ref), (att, att0_ref)):
        to[0:TOK, :] = at[...]
    rest = slice(TOK, ROWS)
    assemble(0, x_ref, lat_ref, lon_ref, diag_ref, src, win)
    normalize((1, 2, 3), win, gain_ref, xw_ref, nrm)
    assemble(1, dy_ref, lat_ref, lon_ref, diag_ref, src, win)
    dyw_ref[rest, :] = win[rest, :].astype(BF)
    project(rest, nrm, dyw_ref, wq_ref, wp_ref, qkv, gatt)
    attend((1, 2, 3), last, qkv, gatt, att, gact_ref)

    def put(slot_is_low, rows, cols, value):
        @pl.when(core == slot_is_low)
        def _():
            keep_ref[rows, cols] = value

        @pl.when(core != slot_is_low)
        def _():
            send_ref[rows, cols] = value

    normt[...] = nrm[...].T
    for i in range(4):
        rows = slice(i * 256, (i + 1) * 256)
        lhs = normt[rows, :]
        put(0, rows, slice(0, 1024), dot(lhs, gact_ref[:, 0:1024], NN).astype(BF))
        put(1, rows, slice(0, 512), dot(lhs, gact_ref[:, 1024:1536], NN).astype(BF))
    normt[...] = dyw_ref[...].T
    for i in range(4):
        rows = slice(i * 256, (i + 1) * 256)
        put(1, rows, slice(512, 1024), dot(normt[rows, :], att[...], NN).astype(BF))


def main_call(*operands):
    return pl.pallas_call(
        main_kernel,
        out_shape=(
            jax.ShapeDtypeStruct((D, 1024), BF),
            jax.ShapeDtypeStruct((D, 1024), BF),
            jax.ShapeDtypeStruct((ROWS, 1536), BF),
            jax.ShapeDtypeStruct((ROWS, D), BF),
            jax.ShapeDtypeStruct((ROWS, D), BF),
        ),
        scratch_shapes=[
            pltpu.VMEM((ROWS, D), F32),
            pltpu.VMEM((ROWS, D), F32),
            pltpu.VMEM((ROWS, D), BF),
            pltpu.VMEM((ROWS, 1536), BF),
            pltpu.VMEM((ROWS, HH), BF),
            pltpu.VMEM((ROWS, HH), BF),
            pltpu.VMEM((D, ROWS), BF),
        ],
        compiler_params=params(32),
        cost_estimate=cost(5.5e9, 14e6),
        name="main",
    )(*operands)


def input_rows(w, gact_ref, xw_ref, dyw_ref, gain, wq_ref, win):
    rows = slice(w * TOK, (w + 1) * TOK)
    gn = dot(gact_ref[rows, :], wq_ref[...], NT)
    cen, inv = layer_stats(xw_ref[rows, :].astype(F32))
    xhat = cen * inv
    g = gn * gain
    win[rows, :] = dyw_ref[rows, :].astype(F32) + inv * (
        g - jnp.mean(g, -1, keepdims=True) - xhat * jnp.mean(g * xhat, -1, keepdims=True)
    )
    return jnp.sum(gn * xhat, 0, keepdims=True)


def input_low_kernel(
    gact_ref, xw_ref, dyw_ref, gain_ref, wq_ref, own_ref, lat_ref, lon_ref, diag_ref, gg_ref, win, dst
):
    gain = gain_ref[...]
    gg_ref[...] = sum(input_rows(w, gact_ref, xw_ref, dyw_ref, gain, wq_ref, win) for w in (2, 3))
    for out, segments in ((lat_ref, lat_segments()), (lon_ref, lon_out_segments(0)), (diag_ref, diag_segments())):
        count = out.shape[0]
        dst[count - 16 : count, :] = jnp.zeros((16, D), F32)
        for at, here, size, _ in segments:
            dst[at : at + size, :] = win[here : here + size, :]
        out[...] = dst[:count, :].astype(BF)
    for own, here, size in own_segments():
        if here >= 2 * TOK:
            dst[own : own + size, :] = win[here : here + size, :]
    for lev in range(LEV):
        for r in range(9, NR):
            at = (lev * NR + r) * NC
            own_ref[lev, r - 9] = dst[at : at + NC, :].astype(BF)


def input_high_kernel(gact_ref, xw_ref, dyw_ref, gain_ref, wq_ref, lon0_ref, gg0_ref, own_ref, lon_ref, gg_ref, win, dst):
    gain = gain_ref[...]
    acc = gg0_ref[...] + sum(input_rows(w, gact_ref, xw_ref, dyw_ref, gain, wq_ref, win) for w in (0, 1))
    for j in range(8):
        gg_ref[j : j + 1, :] = acc[:, j * 128 : (j + 1) * 128]
    lon_ref[0:48, :] = lon0_ref[...]
    dst[64:80, :] = jnp.zeros((16, D), F32)
    for at, here, size, _ in lon_out_segments(1):
        dst[at - 48 : at - 48 + size, :] = win[here : here + size, :]
    lon_ref[48:128, :] = dst[0:80, :].astype(BF)
    for own, here, size in own_segments():
        if here < 2 * TOK:
            dst[own : own + size, :] = win[here : here + size, :]
    for lev in range(LEV):
        for r in range(3, 9):
            at = (lev * NR + r) * NC
            own_ref[lev, r - 3] = dst[at : at + NC, :].astype(BF)


def lon_out_segments(part):
    for lev in range(LEV):
        for rr in (range(6, 9), range(6))[part]:
            at = (48 + (lev * 6 + rr) * 6) if part else (lev * 3 + rr - 6) * 6
            yield at, window_row(lev, rr, 18), 6, (lev * NR + rr + 3) * NC


def input_low_call(gact, xw, dyw, gain, wq):
    return pl.pallas_call(
        input_low_kernel,
        out_shape=(
            jax.ShapeDtypeStruct((LEV, 3, NC, D), BF),
            jax.ShapeDtypeStruct((LATN, D), BF),
            jax.ShapeDtypeStruct((48, D), BF),
            jax.ShapeDtypeStruct((DIAGN, D), BF),
            jax.ShapeDtypeStruct((1, D), F32),
        ),
        scratch_shapes=[pltpu.VMEM((ROWS, D), F32), pltpu.VMEM((ROWS, D), F32)],
        compiler_params=params(24),
        cost_estimate=cost(1e9, 9e6),
        name="input_low",
    )(gact, xw, dyw, gain, wq)


def input_high_call(gact, xw, dyw, gain, wq, lon0, gg0):
    return pl.pallas_call(
        input_high_kernel,
        out_shape=(
            jax.ShapeDtypeStruct((LEV, 6, NC, D), BF),
            jax.ShapeDtypeStruct((128, D), BF),
            jax.ShapeDtypeStruct((8, 128), F32),
        ),
        scratch_shapes=[pltpu.VMEM((ROWS, D), F32), pltpu.VMEM((ROWS, D), F32)],
        compiler_params=params(24),
        cost_estimate=cost(1e9, 9e6),
        name="input_high",
    )(gact, xw, dyw, gain, wq, lon0, gg0)


def join_kernel(high_ref, low_ref, lat_ref, lon_ref, diag_ref, out_ref, src, dst):
    for lev in range(LEV):
        for r in range(3, NR):
            at = (lev * NR + r) * NC
            part = high_ref[lev, r - 3] if r < 9 else low_ref[lev, r - 9]
            dst[at : at + NC, :] = part.astype(F32)
    lon_parts = [*lon_out_segments(0), *lon_out_segments(1)]
    for halo, segments in ((lat_ref, lat_segments()), (lon_ref, lon_parts), (diag_ref, diag_segments())):
        count = halo.shape[0]
        src[:count, :] = halo[...].astype(F32)
        for here, _, size, own in segments:
            dst[own : own + size, :] = src[here : here + size, :]
    for lev in range(LEV):
        for r in range(NR):
            at = (lev * NR + r) * NC
            out_ref[lev, r] = dst[at : at + NC, :].astype(BF)


def join_call(high, low, lat, lon, diag):
    return pl.pallas_call(
        join_kernel,
        out_shape=jax.ShapeDtypeStruct((LEV, NR, NC, D), BF),
        scratch_shapes=[pltpu.VMEM((128, D), F32), pltpu.VMEM((ROWS, D), F32)],
        compiler_params=params(12),
        cost_estimate=cost(1e6, 4e6),
        name="join",
    )(high, low, lat, lon, diag)


MSG = 272


def x_of():
    return lax.axis_index("xh") * 2 + lax.axis_index("xl")


def x_block(x):
    return lax.rem(x, 2) * 2 + x // 2


def put_gain(out, at, gg):
    hi = gg.astype(BF)
    out[at : at + 16, :] = jnp.zeros((16, 512), BF)
    out[at : at + 8, 0:128] = hi
    out[at : at + 8, 128:256] = (gg - hi.astype(F32)).astype(BF)


def take_gain(ref, at):
    return ref[at : at + 8, 0:128].astype(F32) + ref[at : at + 8, 128:256].astype(F32)


def split_kernel(keep_ref, recv_ref, gg_ref, owna, a1, a2, a3, ownb, b1, b2, b3):
    y = lax.axis_index("y")
    x = x_of()

    def total(rows, cols):
        return keep_ref[rows, cols].astype(F32) + recv_ref[rows, cols].astype(F32)

    for k, out in enumerate((owna, a1, a2, a3)):
        rows = pl.ds(pl.multiple_of(lax.rem(y + k, 4) * 256, 256), 256)
        out[0:256, :] = total(rows, slice(0, 512)).astype(out.dtype)
        if k:
            put_gain(out, 256, gg_ref[...])
    for k, out in enumerate((ownb, b1, b2, b3)):
        block = x_block(lax.rem(x + k, 4))
        for j in range(4):
            rows = pl.ds(pl.multiple_of(j * 256 + block * 64, 64), 64)
            out[j * 64 : (j + 1) * 64, :] = total(rows, slice(512, 1024)).astype(out.dtype)


def split_call(keep, recv, gg):
    mine = jax.ShapeDtypeStruct((256, 512), F32)
    a = jax.ShapeDtypeStruct((MSG, 512), BF)
    b = jax.ShapeDtypeStruct((256, 512), BF)
    return pl.pallas_call(
        split_kernel,
        out_shape=(mine, a, a, a, mine, b, b, b),
        compiler_params=params(12),
        cost_estimate=cost(1e6, 8e6),
        name="split",
    )(keep, recv, gg)


def cross_kernel(owna, a1, a2, a3, ownb, b1, b2, b3, gg_ref, gout, nowna, na1, na2, na3, nownb, nb1, nb2, nb3):
    y = lax.axis_index("y")
    x = x_of()
    gg = gg_ref[...] + take_gain(a1, 256) + take_gain(a2, 256) + take_gain(a3, 256)
    gout[...] = gg

    def total(rows, own, refs):
        value = own[rows, :]
        for ref in refs:
            value += ref[rows, :].astype(F32)
        return value

    for k, out in enumerate((nowna, na1, na2, na3)):
        rows = pl.ds(pl.multiple_of(x_block(lax.rem(x + k, 4)) * 64, 64), 64)
        out[0:64, :] = total(rows, owna, (a1, a2, a3)).astype(out.dtype)
        if k:
            put_gain(out, 64, gg)
    for k, out in enumerate((nownb, nb1, nb2, nb3)):
        rows = pl.ds(pl.multiple_of(lax.rem(y + k, 4) * 64, 64), 64)
        out[...] = total(rows, ownb, (b1, b2, b3)).astype(out.dtype)


def cross_call(*operands):
    mine = jax.ShapeDtypeStruct((64, 512), F32)
    a = jax.ShapeDtypeStruct((80, 512), BF)
    b = jax.ShapeDtypeStruct((64, 512), BF)
    return pl.pallas_call(
        cross_kernel,
        out_shape=(jax.ShapeDtypeStruct((8, 128), F32), mine, a, a, a, mine, b, b, b),
        compiler_params=params(8),
        cost_estimate=cost(1e6, 4e6),
        name="cross",
    )(*operands)


def gather_kernel(owna, a1, a2, a3, ownb, b1, b2, b3, gg_ref, out_ref):
    gg = gg_ref[...] + take_gain(a1, 64) + take_gain(a2, 64) + take_gain(a3, 64)
    gg = gg.astype(BF)
    for i in range(8):
        rows = slice(i * 8, (i + 1) * 8)
        parts = []
        for own, refs in ((owna, (a1, a2, a3)), (ownb, (b1, b2, b3))):
            value = own[rows, :]
            for ref in refs:
                value += ref[rows, :].astype(F32)
            parts.append(value)
        for j in range(2):
            half = slice(j * 4, j * 4 + 4)
            out_ref[2 * i + j, :, 0:512] = jnp.concatenate([parts[0][half], parts[1][half]], 0).astype(BF)
            out_ref[2 * i + j, :, 512:640] = gg


def gather_call(*operands):
    return pl.pallas_call(
        gather_kernel,
        out_shape=jax.ShapeDtypeStruct((16, 8, 640), BF),
        compiler_params=params(6),
        cost_estimate=cost(1e6, 4e6),
        name="gather",
    )(*operands)


def final_kernel(blocks, wq_ref, wp_ref, gain_ref, gg):
    low = jnp.zeros((8, 640), F32)
    high = jnp.zeros((8, 640), F32)
    for z in range(8):
        low += blocks[2 * z].astype(F32)
        high += blocks[2 * z + 1].astype(F32)
    low = low * FACTOR
    high = high * FACTOR
    wq_ref[:, 0:512] = low[0:4, 0:512]
    wq_ref[:, 512:1024] = low[4:8, 0:512]
    wq_ref[:, 1024:1536] = high[0:4, 0:512]
    wp_ref[...] = high[4:8, 0:512]
    gg[...] = low[:, 512:640] + high[:, 512:640]
    device = lax.axis_index("y") * 64 + lax.axis_index("xl") * 32 + lax.axis_index("xh") * 16
    device = device + lax.axis_index("z") * 2 + lax.axis_index("c")
    row = gg[pl.ds(device // 32, 1), :]
    gain_ref[...] = pltpu.roll(row, lax.rem(128 - lax.rem(device, 32) * 4, 128), 1)[:, 0:4]


def final_call(blocks):
    return pl.pallas_call(
        final_kernel,
        out_shape=(
            jax.ShapeDtypeStruct((4, 1536), F32),
            jax.ShapeDtypeStruct((4, HH), F32),
            jax.ShapeDtypeStruct((1, 4), F32),
        ),
        scratch_shapes=[pltpu.VMEM((8, 128), F32)],
        compiler_params=params(4),
        cost_estimate=cost(1e6, 1e6),
        name="final",
    )(blocks)


def shift_x(value, k):
    pairs = []
    for xl in range(2):
        for xh in range(2):
            to = (xh * 2 + xl + k) % 4
            pairs.append((xl * 2 + xh, (to % 2) * 2 + to // 2))
    return lax.ppermute(value, ("xl", "xh"), pairs)


def shift_y(value, k):
    return lax.ppermute(value, "y", shift(4, k))


def shift(n, k):
    return [(i, (i + k) % n) for i in range(n)]


def shift_both(k):
    pairs = []
    for i in range(8):
        for j in range(32):
            pairs.append((i * 32 + j, ((i + k) % 8) * 32 + (j + k) % 32))
    return pairs


LAT = ("y", "xl")
LON = ("xh", "z", "c")
ALL = LAT + LON


def per_device(x, dy, gain, wq, wp):
    gain2 = gain.reshape(1, D)
    lat, lon, diag = pack(x, dy)
    lat = lax.ppermute(lat, LAT, shift(8, -1))
    lon = lax.ppermute(lon, LON, shift(32, -1))
    diag = lax.ppermute(diag, ALL, shift_both(-1))
    early = local_call(x, dy, gain2, wq, wp)
    keep, send, gact, xw, dyw = main_call(x, dy, lat, lon, diag, gain2, wq, wp, *early)
    recv = lax.ppermute(send, "c", [(0, 1), (1, 0)])
    low, lat, lon0, diag, gg0 = input_low_call(gact, xw, dyw, gain2, wq)
    high, lon, gg = input_high_call(gact, xw, dyw, gain2, wq, lon0, gg0)
    oa, a1, a2, a3, ob, b1, b2, b3 = split_call(keep, recv, gg)
    a1, a2, a3 = (shift_y(v, k) for k, v in ((1, a1), (2, a2), (3, a3)))
    b1, b2, b3 = (shift_x(v, k) for k, v in ((1, b1), (2, b2), (3, b3)))
    lat = lax.ppermute(lat, LAT, shift(8, 1))
    lon = lax.ppermute(lon, LON, shift(32, 1))
    diag = lax.ppermute(diag, ALL, shift_both(1))
    gg, oa, a1, a2, a3, ob, b1, b2, b3 = cross_call(oa, a1, a2, a3, ob, b1, b2, b3, gg)
    a1, a2, a3 = (shift_x(v, k) for k, v in ((1, a1), (2, a2), (3, a3)))
    b1, b2, b3 = (shift_y(v, k) for k, v in ((1, b1), (2, b2), (3, b3)))
    grad_in = join_call(high, low, lat, lon, diag)
    a1, grad_in = lax.optimization_barrier((a1, grad_in))
    blocks = gather_call(oa, a1, a2, a3, ob, b1, b2, b3, gg)
    blocks = lax.all_to_all(blocks, ("z", "c"), 0, 0, tiled=True)
    grad_qkv, grad_proj, grad_gain = final_call(blocks)
    return grad_in, grad_qkv, grad_proj.T, grad_gain.reshape(4)


def solution(mesh):
    mesh = Mesh(mesh.devices.reshape(4, 2, 2, 8, 2), ALL)
    return jax.shard_map(
        per_device,
        mesh=mesh,
        in_specs=(P(None, LAT, LON, None), P(None, LAT, LON, None), P(), P(), P()),
        out_specs=(P(None, LAT, LON, None), P(ALL, None), P(None, ALL), P(ALL)),
        check_vma=False,
    )
```

```python
import functools

import jax
import jax.numpy as jnp
from jax import lax
from jax.experimental import pallas as pl
from jax.experimental.pallas import tpu as pltpu
from jax.sharding import Mesh, PartitionSpec as P


F32 = jnp.float32
BF = jnp.bfloat16
D = 1024
HH = 512
TOK = 144
NWIN = 4
ROWS = NWIN * TOK
LEV, NR, NC = 2, 12, 24
LATN = 112
LONN = 112
DIAGN = 48
EPS = 1e-05
FACTOR = 1.0 / 384.0

NN = (((1,), (0,)), ((), ()))
NT = (((1,), (1,)), ((), ()))
TN = (((0,), (0,)), ((), ()))


def dot(a, b, dims):
    return lax.dot_general(a, b, dims, preferred_element_type=F32)


def params(mib):
    return pltpu.CompilerParams(vmem_limit_bytes=mib * 1024 * 1024)


def cost(flops, nbytes):
    return pl.CostEstimate(flops=int(flops), bytes_accessed=int(nbytes), transcendentals=0)


def window_row(lev, rr, cc):
    return ((rr // 6) * 2 + cc // 12) * TOK + lev * 72 + (rr % 6) * 12 + cc % 12


def own_segments():
    for lev in range(LEV):
        for rr in range(9):
            base = (lev * NR + rr + 3) * NC
            yield base + 6, window_row(lev, rr, 0), 12
            yield base + 18, window_row(lev, rr, 12), 6


def lat_segments():
    for lev in range(LEV):
        for r in range(3):
            base = (lev * 3 + r) * 18
            yield base, window_row(lev, 9 + r, 0), 12, (lev * NR + r) * NC + 6
            yield base + 12, window_row(lev, 9 + r, 12), 6, (lev * NR + r) * NC + 18


def lon_segments():
    for lev in range(LEV):
        for rr in range(9):
            yield (lev * 9 + rr) * 6, window_row(lev, rr, 18), 6, (lev * NR + rr + 3) * NC


def diag_segments():
    for lev in range(LEV):
        for r in range(3):
            yield (lev * 3 + r) * 6, window_row(lev, 9 + r, 18), 6, (lev * NR + r) * NC


def pack_kernel(ref, lat_ref, lon_ref, diag_ref, top, side, src, dst, sems):
    copies = (
        pltpu.make_async_copy(ref.at[:, 0:3], top, sems.at[0]),
        pltpu.make_async_copy(ref.at[:, 3:12, 0:8, :], side, sems.at[1]),
    )
    for copy in copies:
        copy.start()
    copies[0].wait()
    for lev in range(LEV):
        for r in range(3):
            at = (lev * NR + r) * NC
            src[at : at + NC, :] = top[lev, r].astype(F32)
    copies[1].wait()
    for lev in range(LEV):
        for r in range(3, NR):
            at = (lev * NR + r) * NC
            src[at : at + 8, :] = side[lev, r - 3].astype(F32)
    for out, segments in ((lat_ref, lat_segments), (lon_ref, lon_segments), (diag_ref, diag_segments)):
        count = out.shape[0]
        dst[count - 16 : count, :] = jnp.zeros((16, D), F32)
        for at, _, size, own in segments():
            dst[at : at + size, :] = src[own : own + size, :]
        out[...] = dst[:count, :].astype(BF)


def pack(value, mib):
    return pl.pallas_call(
        pack_kernel,
        in_specs=[pl.BlockSpec(memory_space=pltpu.HBM)],
        out_shape=(
            jax.ShapeDtypeStruct((LATN, D), BF),
            jax.ShapeDtypeStruct((LONN, D), BF),
            jax.ShapeDtypeStruct((DIAGN, D), BF),
        ),
        scratch_shapes=[
            pltpu.VMEM((LEV, 3, NC, D), BF),
            pltpu.VMEM((LEV, 9, 8, D), BF),
            pltpu.VMEM((ROWS, D), F32),
            pltpu.VMEM((LATN, D), F32),
            pltpu.SemaphoreType.DMA((2,)),
        ],
        compiler_params=params(mib),
        cost_estimate=cost(1e6, 2e6),
        name="pack",
    )(value)


def copy_own(ref, src, win, local):
    for lev in range(LEV):
        for r in range(3, 9 if local else NR):
            at = (lev * NR + r) * NC
            src[at : at + NC, :] = ref[lev, r].astype(F32)
    for own, at, size in own_segments():
        if (at < TOK) == local:
            win[at : at + size, :] = src[own : own + size, :]


def assemble(ref, lat_ref, lon_ref, diag_ref, src, win):
    copy_own(ref, src, win, False)
    for halo, segments in ((lat_ref, lat_segments), (lon_ref, lon_segments), (diag_ref, diag_segments)):
        count = halo.shape[0]
        src[:count, :] = halo[...].astype(F32)
        for here, at, size, _ in segments():
            win[at : at + size, :] = src[here : here + size, :]


def layer_stats(x):
    mean = jnp.mean(x, -1, keepdims=True)
    cen = x - mean
    inv = lax.rsqrt(jnp.mean(cen * cen, -1, keepdims=True) + EPS)
    return cen, inv


def normalize(windows, win, gain_ref, xw_ref, nrm):
    for w in windows:
        rows = slice(w * TOK, (w + 1) * TOK)
        x = win[rows, :]
        xw_ref[rows, :] = x.astype(BF)
        cen, inv = layer_stats(x)
        nrm[rows, :] = (cen * inv * gain_ref[...]).astype(BF)


def project(rows, a_ref, w_ref, out, dims):
    for j in range(out.shape[1] // 256):
        cols = slice(j * 256, (j + 1) * 256)
        w = w_ref[:, cols] if dims is NN else w_ref[cols, :]
        out[rows, cols] = dot(a_ref[rows, :], w, dims).astype(BF)


def low_lanes():
    return lax.broadcasted_iota(jnp.int32, (TOK, 128), 1) < 64


def stacked(v):
    z = jnp.zeros_like(v)
    return jnp.concatenate([jnp.where(low_lanes(), v, z), jnp.where(low_lanes(), z, v)], axis=0)


def merged(v):
    return jnp.where(low_lanes(), v[:TOK], v[TOK:])


def window_rows(w):
    return pl.ds(pl.multiple_of(w * TOK, TOK), TOK)


def forward_pair(w, hp, last, qkv, att):
    rows = window_rows(w)
    at = hp * 128
    q2 = stacked(qkv[rows, at : at + 128] * jnp.bfloat16(0.125))
    s = dot(qkv[rows, HH + at : HH + at + 128], q2, NT)
    if last is not None:
        keyg = (lax.broadcasted_iota(jnp.int32, (TOK, 2 * TOK), 0) // 12) % 6 < 3
        qryg = (lax.broadcasted_iota(jnp.int32, (TOK, 2 * TOK), 1) // 12) % 6 < 3
        s = jnp.where(jnp.logical_and(keyg != qryg, jnp.logical_and(last, w >= 2)), -1000000000.0, s)
    e = jnp.exp(s - jnp.max(s, 0, keepdims=True))
    p = e * (1.0 / jnp.sum(e, 0, keepdims=True))
    o = dot(p.astype(BF), qkv[rows, 2 * HH + at : 2 * HH + at + 128], TN)
    att[rows, at : at + 128] = merged(o).astype(BF)
    return p


def backward_pair(w, hp, p, qkv, g2, put):
    rows = window_rows(w)
    at = hp * 128
    q2 = stacked(qkv[rows, at : at + 128] * jnp.bfloat16(0.125))
    pb = p.astype(BF)
    dp = dot(qkv[rows, 2 * HH + at : 2 * HH + at + 128], g2, NT)
    ds = (p * (dp - jnp.sum(p * dp, 0, keepdims=True))).astype(BF)
    dq = dot(ds, qkv[rows, HH + at : HH + at + 128], TN)
    put(rows, 0, (merged(dq) * 0.125).astype(BF))
    put(rows, 1, dot(ds, q2, NN).astype(BF))
    put(rows, 2, dot(pb, g2, NN).astype(BF))


def local_kernel(
    x_ref, dy_ref, gain_ref, wq_ref, wp_ref,
    nrm_ref, xw_ref, dyw_ref, qkv_ref, gact_ref, att_ref,
    src, win, gatt,
):
    copy_own(x_ref, src, win, True)
    normalize((0,), win, gain_ref, xw_ref, nrm_ref)
    copy_own(dy_ref, src, win, True)
    dyw_ref[...] = win[...].astype(BF)
    rows = slice(0, TOK)
    project(rows, nrm_ref, wq_ref, qkv_ref, NN)
    project(rows, dyw_ref, wp_ref, gatt, NT)
    for hp in range(4):

        def put(rows, part, value):
            gact_ref[rows, part * HH + hp * 128 : part * HH + hp * 128 + 128] = value

        p = forward_pair(0, hp, None, qkv_ref, att_ref)
        backward_pair(0, hp, p, qkv_ref, stacked(gatt[rows, hp * 128 : hp * 128 + 128]), put)


def local_call(x, dy, gain, wq, wp):
    wide = jax.ShapeDtypeStruct((TOK, D), BF)
    three = jax.ShapeDtypeStruct((TOK, 1536), BF)
    return pl.pallas_call(
        local_kernel,
        out_shape=(wide, wide, wide, three, three, jax.ShapeDtypeStruct((TOK, HH), BF)),
        scratch_shapes=[
            pltpu.VMEM((ROWS, D), F32),
            pltpu.VMEM((TOK, D), F32),
            pltpu.VMEM((TOK, HH), BF),
        ],
        compiler_params=params(14),
        cost_estimate=cost(2e9, 9e6),
        name="local",
    )(x, dy, gain, wq, wp)


REST = slice(TOK, ROWS)


def forward_kernel(
    x_ref, lat_ref, lon_ref, diag_ref, gain_ref, wq_ref, nrm0_ref, xw0_ref, att0_ref,
    normt_ref, xw_ref, qkv_ref, att_ref, p_ref,
    src, win, nrm,
):
    last = jnp.logical_and(lax.axis_index("y") == 3, lax.axis_index("xl") == 1)
    for to, at in ((nrm, nrm0_ref), (xw_ref, xw0_ref), (att_ref, att0_ref)):
        to[0:TOK, :] = at[...]
    assemble(x_ref, lat_ref, lon_ref, diag_ref, src, win)
    normalize((1, 2, 3), win, gain_ref, xw_ref, nrm)
    project(REST, nrm, wq_ref, qkv_ref, NN)
    normt_ref[...] = nrm[...].T

    def window(w, carry):
        for hp in range(4):
            p_ref[(w - 1) * 4 + hp] = forward_pair(w, hp, last, qkv_ref, att_ref)
        return carry

    lax.fori_loop(1, NWIN, window, 0)


def forward_call(*operands):
    return pl.pallas_call(
        forward_kernel,
        out_shape=(
            jax.ShapeDtypeStruct((D, ROWS), BF),
            jax.ShapeDtypeStruct((ROWS, D), BF),
            jax.ShapeDtypeStruct((ROWS, 1536), BF),
            jax.ShapeDtypeStruct((ROWS, HH), BF),
            jax.ShapeDtypeStruct((12, TOK, 2 * TOK), F32),
        ),
        scratch_shapes=[pltpu.VMEM((ROWS, D), F32), pltpu.VMEM((ROWS, D), F32), pltpu.VMEM((ROWS, D), BF)],
        compiler_params=params(24),
        cost_estimate=cost(3e9, 9e6),
        name="forward",
    )(*operands)


def half_gradients(half, dyw_ref, dywt_ref, wp_ref, p_ref, qkv_ref, att_ref, normt_ref, put_gact, gact, gatt, keep_ref, send_ref):
    core = lax.axis_index("c")
    gatt[REST, :] = dot(dyw_ref[REST, :], wp_ref[half * 256 : half * 256 + 256, :], NT).astype(BF)

    def window(w, carry):
        for i in range(2):
            rows = window_rows(w)
            g2 = stacked(gatt[rows, i * 128 : i * 128 + 128])
            backward_pair(w, 2 * half + i, p_ref[(w - 1) * 4 + 2 * half + i], qkv_ref, g2, functools.partial(put_gact, i))
        return carry

    lax.fori_loop(1, NWIN, window, 0)

    def put(slot_is_low, rows, cols, value):
        @pl.when(core == slot_is_low)
        def _():
            keep_ref[rows, cols] = value

        @pl.when(core != slot_is_low)
        def _():
            send_ref[rows, cols] = value

    for i in range(4):
        rows = slice(i * 256, (i + 1) * 256)
        lhs = normt_ref[rows, :]
        for j in range(2):
            put(0, rows, slice(j * 256, j * 256 + 256), dot(lhs, gact(j), NN).astype(BF))
        put(1, rows, slice(0, 256), dot(lhs, gact(2), NN).astype(BF))
        value = dot(dywt_ref[rows, :], att_ref[:, half * 256 : half * 256 + 256], NN)
        put(1, rows, slice(256, 512), value.astype(BF))


def first_kernel(
    dy_ref, lat_ref, lon_ref, diag_ref, wp_ref, dyw0_ref, gact0_ref, normt_ref, qkv_ref, att_ref, p_ref,
    keep_ref, send_ref, gact_ref, dyw_ref, dywt_ref,
    src, win, gatt,
):
    dyw_ref[0:TOK, :] = dyw0_ref[...]
    for part in range(3):
        gact_ref[0:TOK, part * 256 : part * 256 + 256] = gact0_ref[:, part * HH : part * HH + 256]
    assemble(dy_ref, lat_ref, lon_ref, diag_ref, src, win)
    dyw_ref[REST, :] = win[REST, :].astype(BF)
    dywt_ref[...] = dyw_ref[...].T

    def put_gact(i, rows, part, value):
        gact_ref[rows, part * 256 + i * 128 : part * 256 + i * 128 + 128] = value

    half_gradients(
        0, dyw_ref, dywt_ref, wp_ref, p_ref, qkv_ref, att_ref, normt_ref, put_gact,
        lambda part: gact_ref[:, part * 256 : part * 256 + 256], gatt, keep_ref, send_ref,
    )


def first_call(*operands):
    block = jax.ShapeDtypeStruct((D, 512), BF)
    return pl.pallas_call(
        first_kernel,
        out_shape=(
            block,
            block,
            jax.ShapeDtypeStruct((ROWS, 768), BF),
            jax.ShapeDtypeStruct((ROWS, D), BF),
            jax.ShapeDtypeStruct((D, ROWS), BF),
        ),
        scratch_shapes=[pltpu.VMEM((ROWS, D), F32), pltpu.VMEM((ROWS, D), F32), pltpu.VMEM((ROWS, 256), BF)],
        compiler_params=params(24),
        cost_estimate=cost(2.5e9, 9e6),
        name="first",
    )(*operands)


def second_kernel(
    gact1_ref, gact0_ref, dyw_ref, dywt_ref, wp_ref, normt_ref, qkv_ref, att_ref, p_ref,
    keep_ref, send_ref, gact_ref,
    gatt,
):
    for part in range(3):
        at = part * HH
        gact_ref[:, at : at + 256] = gact1_ref[:, part * 256 : part * 256 + 256]
        gact_ref[0:TOK, at + 256 : at + 512] = gact0_ref[:, at + 256 : at + 512]

    def put_gact(i, rows, part, value):
        at = part * HH + 256 + i * 128
        gact_ref[rows, at : at + 128] = value

    half_gradients(
        1, dyw_ref, dywt_ref, wp_ref, p_ref, qkv_ref, att_ref, normt_ref, put_gact,
        lambda part: gact_ref[:, part * HH + 256 : part * HH + 512], gatt, keep_ref, send_ref,
    )


def second_call(*operands):
    block = jax.ShapeDtypeStruct((D, 512), BF)
    return pl.pallas_call(
        second_kernel,
        out_shape=(block, block, jax.ShapeDtypeStruct((ROWS, 1536), BF)),
        scratch_shapes=[pltpu.VMEM((ROWS, 256), BF)],
        compiler_params=params(20),
        cost_estimate=cost(2.5e9, 9e6),
        name="second",
    )(*operands)


def input_rows(w, gact_ref, xw_ref, dyw_ref, gain, wq_ref, win):
    rows = slice(w * TOK, (w + 1) * TOK)
    gn = dot(gact_ref[rows, :], wq_ref[...], NT)
    cen, inv = layer_stats(xw_ref[rows, :].astype(F32))
    xhat = cen * inv
    g = gn * gain
    win[rows, :] = dyw_ref[rows, :].astype(F32) + inv * (
        g - jnp.mean(g, -1, keepdims=True) - xhat * jnp.mean(g * xhat, -1, keepdims=True)
    )
    return jnp.sum(gn * xhat, 0, keepdims=True)


def input_low_kernel(
    gact_ref, xw_ref, dyw_ref, gain_ref, wq_ref, own_ref, lat_ref, lon_ref, diag_ref, gg_ref, win, dst
):
    gain = gain_ref[...]
    gg_ref[...] = sum(input_rows(w, gact_ref, xw_ref, dyw_ref, gain, wq_ref, win) for w in (2, 3))
    for out, segments in ((lat_ref, lat_segments()), (lon_ref, lon_out_segments(0)), (diag_ref, diag_segments())):
        count = out.shape[0]
        dst[count - 16 : count, :] = jnp.zeros((16, D), F32)
        for at, here, size, _ in segments:
            dst[at : at + size, :] = win[here : here + size, :]
        out[...] = dst[:count, :].astype(BF)
    for own, here, size in own_segments():
        if here >= 2 * TOK:
            dst[own : own + size, :] = win[here : here + size, :]
    for lev in range(LEV):
        for r in range(9, NR):
            at = (lev * NR + r) * NC
            own_ref[lev, r - 9] = dst[at : at + NC, :].astype(BF)


def input_high_kernel(gact_ref, xw_ref, dyw_ref, gain_ref, wq_ref, lon0_ref, gg0_ref, own_ref, lon_ref, gg_ref, win, dst):
    gain = gain_ref[...]
    acc = gg0_ref[...] + sum(input_rows(w, gact_ref, xw_ref, dyw_ref, gain, wq_ref, win) for w in (0, 1))
    for j in range(8):
        gg_ref[j : j + 1, :] = acc[:, j * 128 : (j + 1) * 128]
    lon_ref[0:48, :] = lon0_ref[...]
    dst[64:80, :] = jnp.zeros((16, D), F32)
    for at, here, size, _ in lon_out_segments(1):
        dst[at - 48 : at - 48 + size, :] = win[here : here + size, :]
    lon_ref[48:128, :] = dst[0:80, :].astype(BF)
    for own, here, size in own_segments():
        if here < 2 * TOK:
            dst[own : own + size, :] = win[here : here + size, :]
    for lev in range(LEV):
        for r in range(3, 9):
            at = (lev * NR + r) * NC
            own_ref[lev, r - 3] = dst[at : at + NC, :].astype(BF)


def lon_out_segments(part):
    for lev in range(LEV):
        for rr in (range(6, 9), range(6))[part]:
            at = (48 + (lev * 6 + rr) * 6) if part else (lev * 3 + rr - 6) * 6
            yield at, window_row(lev, rr, 18), 6, (lev * NR + rr + 3) * NC


def input_low_call(gact, xw, dyw, gain, wq):
    return pl.pallas_call(
        input_low_kernel,
        out_shape=(
            jax.ShapeDtypeStruct((LEV, 3, NC, D), BF),
            jax.ShapeDtypeStruct((LATN, D), BF),
            jax.ShapeDtypeStruct((48, D), BF),
            jax.ShapeDtypeStruct((DIAGN, D), BF),
            jax.ShapeDtypeStruct((1, D), F32),
        ),
        scratch_shapes=[pltpu.VMEM((ROWS, D), F32), pltpu.VMEM((ROWS, D), F32)],
        compiler_params=params(24),
        cost_estimate=cost(1e9, 9e6),
        name="input_low",
    )(gact, xw, dyw, gain, wq)


def input_high_call(gact, xw, dyw, gain, wq, lon0, gg0):
    return pl.pallas_call(
        input_high_kernel,
        out_shape=(
            jax.ShapeDtypeStruct((LEV, 6, NC, D), BF),
            jax.ShapeDtypeStruct((128, D), BF),
            jax.ShapeDtypeStruct((8, 128), F32),
        ),
        scratch_shapes=[pltpu.VMEM((ROWS, D), F32), pltpu.VMEM((ROWS, D), F32)],
        compiler_params=params(24),
        cost_estimate=cost(1e9, 9e6),
        name="input_high",
    )(gact, xw, dyw, gain, wq, lon0, gg0)


def join_kernel(high_ref, low_ref, lat_ref, lon_ref, diag_ref, out_ref, src, dst):
    for lev in range(LEV):
        for r in range(3, NR):
            at = (lev * NR + r) * NC
            part = high_ref[lev, r - 3] if r < 9 else low_ref[lev, r - 9]
            dst[at : at + NC, :] = part.astype(F32)
    lon_parts = [*lon_out_segments(0), *lon_out_segments(1)]
    for halo, segments in ((lat_ref, lat_segments()), (lon_ref, lon_parts), (diag_ref, diag_segments())):
        count = halo.shape[0]
        src[:count, :] = halo[...].astype(F32)
        for here, _, size, own in segments:
            dst[own : own + size, :] = src[here : here + size, :]
    for lev in range(LEV):
        for r in range(NR):
            at = (lev * NR + r) * NC
            out_ref[lev, r] = dst[at : at + NC, :].astype(BF)


def join_call(high, low, lat, lon, diag):
    return pl.pallas_call(
        join_kernel,
        out_shape=jax.ShapeDtypeStruct((LEV, NR, NC, D), BF),
        scratch_shapes=[pltpu.VMEM((128, D), F32), pltpu.VMEM((ROWS, D), F32)],
        compiler_params=params(12),
        cost_estimate=cost(1e6, 4e6),
        name="join",
    )(high, low, lat, lon, diag)


MSG = 272


def x_of():
    return lax.axis_index("xh") * 2 + lax.axis_index("xl")


def x_block(x):
    return lax.rem(x, 2) * 2 + x // 2


def put_gain(out, at, gg):
    hi = gg.astype(BF)
    out[at : at + 16, :] = jnp.zeros((16, 512), BF)
    out[at : at + 8, 0:128] = hi
    out[at : at + 8, 128:256] = (gg - hi.astype(F32)).astype(BF)


def take_gain(ref, at):
    return ref[at : at + 8, 0:128].astype(F32) + ref[at : at + 8, 128:256].astype(F32)


def sum_rows(rows, refs):
    value = refs[0][rows, :].astype(F32)
    for ref in refs[1:]:
        value += ref[rows, :].astype(F32)
    return value


def split_y_kernel(keep_ref, recv_ref, *outs):
    y = lax.axis_index("y")
    for k, out in enumerate(outs):
        rows = pl.ds(pl.multiple_of(lax.rem(y + k, 4) * 256, 256), 256)
        out[...] = sum_rows(rows, (keep_ref, recv_ref)).astype(out.dtype)


def split_y(keep, recv):
    a = jax.ShapeDtypeStruct((256, 512), BF)
    return pl.pallas_call(
        split_y_kernel,
        out_shape=(jax.ShapeDtypeStruct((256, 512), F32), a, a, a),
        compiler_params=params(8),
        cost_estimate=cost(1e6, 4e6),
        name="split_y",
    )(keep, recv)


def split_x_kernel(keep_ref, recv_ref, gg_ref, *outs):
    x = x_of()
    for k, out in enumerate(outs):
        block = x_block(lax.rem(x + k, 4))
        for j in range(4):
            rows = pl.ds(pl.multiple_of(j * 256 + block * 64, 64), 64)
            out[j * 64 : (j + 1) * 64, :] = sum_rows(rows, (keep_ref, recv_ref)).astype(out.dtype)
        if k:
            put_gain(out, 256, gg_ref[...])


def split_x(keep, recv, gg):
    b = jax.ShapeDtypeStruct((MSG, 512), BF)
    return pl.pallas_call(
        split_x_kernel,
        out_shape=(jax.ShapeDtypeStruct((256, 512), F32), b, b, b),
        compiler_params=params(8),
        cost_estimate=cost(1e6, 4e6),
        name="split_x",
    )(keep, recv, gg)


def cross_x_kernel(own, a1, a2, a3, *outs):
    x = x_of()
    for k, out in enumerate(outs):
        rows = pl.ds(pl.multiple_of(x_block(lax.rem(x + k, 4)) * 64, 64), 64)
        out[...] = sum_rows(rows, (own, a1, a2, a3)).astype(out.dtype)


def cross_x(*operands):
    a = jax.ShapeDtypeStruct((64, 512), BF)
    return pl.pallas_call(
        cross_x_kernel,
        out_shape=(jax.ShapeDtypeStruct((64, 512), F32), a, a, a),
        compiler_params=params(6),
        cost_estimate=cost(1e6, 2e6),
        name="cross_x",
    )(*operands)


def cross_y_kernel(own, b1, b2, b3, gg_ref, gout, *outs):
    y = lax.axis_index("y")
    gg = gg_ref[...] + take_gain(b1, 256) + take_gain(b2, 256) + take_gain(b3, 256)
    gout[...] = gg
    for k, out in enumerate(outs):
        rows = pl.ds(pl.multiple_of(lax.rem(y + k, 4) * 64, 64), 64)
        out[0:64, :] = sum_rows(rows, (own, b1, b2, b3)).astype(out.dtype)
        if k:
            put_gain(out, 64, gg)


def cross_y(*operands):
    b = jax.ShapeDtypeStruct((80, 512), BF)
    return pl.pallas_call(
        cross_y_kernel,
        out_shape=(jax.ShapeDtypeStruct((8, 128), F32), jax.ShapeDtypeStruct((64, 512), F32), b, b, b),
        compiler_params=params(6),
        cost_estimate=cost(1e6, 2e6),
        name="cross_y",
    )(*operands)


def gather_kernel(owna, a1, a2, a3, ownb, b1, b2, b3, gg_ref, out_ref):
    gg = gg_ref[...] + take_gain(b1, 64) + take_gain(b2, 64) + take_gain(b3, 64)
    gg = gg.astype(BF)
    for i in range(8):
        rows = slice(i * 8, (i + 1) * 8)
        parts = []
        for own, refs in ((owna, (a1, a2, a3)), (ownb, (b1, b2, b3))):
            value = own[rows, :]
            for ref in refs:
                value += ref[rows, :].astype(F32)
            parts.append(value)
        for j in range(2):
            half = slice(j * 4, j * 4 + 4)
            out_ref[2 * i + j, :, 0:512] = jnp.concatenate([parts[0][half], parts[1][half]], 0).astype(BF)
            out_ref[2 * i + j, :, 512:640] = gg


def gather_call(*operands):
    return pl.pallas_call(
        gather_kernel,
        out_shape=jax.ShapeDtypeStruct((16, 8, 640), BF),
        compiler_params=params(6),
        cost_estimate=cost(1e6, 4e6),
        name="gather",
    )(*operands)


def final_kernel(blocks, wq_ref, wp_ref, gain_ref, gg):
    low = jnp.zeros((8, 640), F32)
    high = jnp.zeros((8, 640), F32)
    for z in range(8):
        low += blocks[2 * z].astype(F32)
        high += blocks[2 * z + 1].astype(F32)
    low = low * FACTOR
    high = high * FACTOR
    for half in range(2):
        rows = slice(half * 4, half * 4 + 4)
        at = half * 256
        wq_ref[:, at : at + 256] = low[rows, 0:256]
        wq_ref[:, 512 + at : 768 + at] = low[rows, 256:512]
        wq_ref[:, 1024 + at : 1280 + at] = high[rows, 0:256]
        wp_ref[:, at : at + 256] = high[rows, 256:512]
    gg[...] = low[:, 512:640] + high[:, 512:640]
    device = lax.axis_index("y") * 64 + lax.axis_index("xl") * 32 + lax.axis_index("xh") * 16
    device = device + lax.axis_index("z") * 2 + lax.axis_index("c")
    row = gg[pl.ds(device // 32, 1), :]
    gain_ref[...] = pltpu.roll(row, lax.rem(128 - lax.rem(device, 32) * 4, 128), 1)[:, 0:4]


def final_call(blocks):
    return pl.pallas_call(
        final_kernel,
        out_shape=(
            jax.ShapeDtypeStruct((4, 1536), F32),
            jax.ShapeDtypeStruct((4, HH), F32),
            jax.ShapeDtypeStruct((1, 4), F32),
        ),
        scratch_shapes=[pltpu.VMEM((8, 128), F32)],
        compiler_params=params(4),
        cost_estimate=cost(1e6, 1e6),
        name="final",
    )(blocks)


def shift_x(value, k):
    pairs = []
    for xl in range(2):
        for xh in range(2):
            to = (xh * 2 + xl + k) % 4
            pairs.append((xl * 2 + xh, (to % 2) * 2 + to // 2))
    return lax.ppermute(value, ("xl", "xh"), pairs)


def shift_y(value, k):
    return lax.ppermute(value, "y", shift(4, k))


def shift(n, k):
    return [(i, (i + k) % n) for i in range(n)]


def shift_both(k):
    pairs = []
    for i in range(8):
        for j in range(32):
            pairs.append((i * 32 + j, ((i + k) % 8) * 32 + (j + k) % 32))
    return pairs


LAT = ("y", "xl")
LON = ("xh", "z", "c")
ALL = LAT + LON


def from_next(lat, lon, diag):
    return (
        lax.ppermute(lat, LAT, shift(8, -1)),
        lax.ppermute(lon, LON, shift(32, -1)),
        lax.ppermute(diag, ALL, shift_both(-1)),
    )


def exchange(move, values):
    out = []
    for k, v in enumerate(values):
        out.append(move(v, k + 1))
    return out


SWAP = [(0, 1), (1, 0)]


def program(x, dy, gain, wq, wp):
    gain2 = gain.reshape(1, D)
    xh = from_next(*pack(x, 60))
    nrm0, xw0, dyw0, _, gact0, att0 = local_call(x, dy, gain2, wq, wp)
    dh = pack(dy, 10)
    xh, dh = lax.optimization_barrier((xh, dh))
    dh = from_next(*dh)
    normt, xw, qkv, att, p = forward_call(x, *xh, gain2, wq, nrm0, xw0, att0)
    keep, send, gact1, dyw, dywt = first_call(dy, *dh, wp, dyw0, gact0, normt, qkv, att, p)
    recv = lax.ppermute(send, "c", SWAP)
    keep2, send2, gact = second_call(gact1, gact0, dyw, dywt, wp, normt, qkv, att, p)
    recv2 = lax.ppermute(send2, "c", SWAP)
    oa, *a = split_y(keep, recv)
    a = exchange(shift_y, a)
    gact, oa = lax.optimization_barrier((gact, oa))
    low, lat, lon0, diag, gg0 = input_low_call(gact, xw, dyw, gain2, wq)
    high, lon, gg = input_high_call(gact, xw, dyw, gain2, wq, lon0, gg0)
    ob, *b = split_x(keep2, recv2, gg)
    b = exchange(shift_x, b)
    lat = lax.ppermute(lat, LAT, shift(8, 1))
    lon = lax.ppermute(lon, LON, shift(32, 1))
    diag = lax.ppermute(diag, ALL, shift_both(1))
    oa, *a = cross_x(oa, *a)
    a = exchange(shift_x, a)
    gg, ob, *b = cross_y(ob, *b, gg)
    b = exchange(shift_y, b)
    grad_in = join_call(high, low, lat, lon, diag)
    oa, grad_in = lax.optimization_barrier((oa, grad_in))
    blocks = gather_call(oa, *a, ob, *b, gg)
    blocks = lax.all_to_all(blocks, ("z", "c"), 0, 0, tiled=True)
    grad_qkv, grad_proj, grad_gain = final_call(blocks)
    return grad_in, grad_qkv, grad_proj.T, grad_gain.reshape(4)


def solution(mesh):
    mesh = Mesh(mesh.devices.reshape(4, 2, 2, 8, 2), ALL)
    return jax.shard_map(
        program,
        mesh=mesh,
        in_specs=(P(None, LAT, LON, None), P(None, LAT, LON, None), P(), P(), P()),
        out_specs=(P(None, LAT, LON, None), P(ALL, None), P(None, ALL), P(ALL)),
        check_vma=False,
    )
```

```python
import functools

import jax
import jax.numpy as jnp
from jax import lax
from jax.experimental import pallas as pl
from jax.experimental.pallas import tpu as pltpu
from jax.sharding import Mesh, PartitionSpec as P

F32 = jnp.float32
BF = jnp.bfloat16
D = 1024
HH = 512
TOK = 144
NWIN = 4
ROWS = NWIN * TOK
LEV, NR, NC = 2, 12, 24
LATN = 112
LONN = 112
DIAGN = 48
EPS = 1e-05
FACTOR = 1.0 / 384.0

NN = (((1,), (0,)), ((), ()))
NT = (((1,), (1,)), ((), ()))
TN = (((0,), (0,)), ((), ()))


def dot(a, b, dims):
    return lax.dot_general(a, b, dims, preferred_element_type=F32)


def params(mib):
    return pltpu.CompilerParams(vmem_limit_bytes=mib * 1024 * 1024)


def cost(flops, nbytes):
    return pl.CostEstimate(flops=int(flops), bytes_accessed=int(nbytes), transcendentals=0)


def window_row(lev, rr, cc):
    return ((cc // 12) * 2 + rr // 6) * TOK + lev * 72 + (rr % 6) * 12 + cc % 12


def own_segments():
    for lev in range(LEV):
        for rr in range(9):
            base = (lev * NR + rr + 3) * NC
            yield base + 6, window_row(lev, rr, 0), 12
            yield base + 18, window_row(lev, rr, 12), 6


def lat_segments():
    for lev in range(LEV):
        for r in range(3):
            base = (lev * 3 + r) * 18
            yield base, window_row(lev, 9 + r, 0), 12, (lev * NR + r) * NC + 6
            yield base + 12, window_row(lev, 9 + r, 12), 6, (lev * NR + r) * NC + 18


def lon_segments():
    for lev in range(LEV):
        for rr in range(9):
            yield (lev * 9 + rr) * 6, window_row(lev, rr, 18), 6, (lev * NR + rr + 3) * NC


def diag_segments():
    for lev in range(LEV):
        for r in range(3):
            yield (lev * 3 + r) * 6, window_row(lev, 9 + r, 18), 6, (lev * NR + r) * NC


def pack_kernel(x_ref, dy_ref, lat_ref, lon_ref, diag_ref, top, side, src, dst, sems):
    copies = []
    for a, ref in enumerate((x_ref, dy_ref)):
        copies.append(
            (
                pltpu.make_async_copy(ref.at[:, 0:3], top.at[a], sems.at[a, 0]),
                pltpu.make_async_copy(ref.at[:, 3:12, 0:8, :], side.at[a], sems.at[a, 1]),
            )
        )
    for pair in copies:
        for copy in pair:
            copy.start()
    for a, pair in enumerate(copies):
        pair[0].wait()
        for lev in range(LEV):
            for r in range(3):
                at = (lev * NR + r) * NC
                src[at : at + NC, :] = top[a, lev, r].astype(F32)
        pair[1].wait()
        for lev in range(LEV):
            for r in range(3, NR):
                at = (lev * NR + r) * NC
                src[at : at + 8, :] = side[a, lev, r - 3].astype(F32)
        for out, segments in ((lat_ref, lat_segments), (lon_ref, lon_segments), (diag_ref, diag_segments)):
            count = out.shape[1]
            dst[count - 16 : count, :] = jnp.zeros((16, D), F32)
            for at, _, size, own in segments():
                dst[at : at + size, :] = src[own : own + size, :]
            out[a] = dst[:count, :].astype(BF)


def pack(x, dy):
    return pl.pallas_call(
        pack_kernel,
        in_specs=[pl.BlockSpec(memory_space=pltpu.HBM)] * 2,
        out_shape=(
            jax.ShapeDtypeStruct((2, LATN, D), BF),
            jax.ShapeDtypeStruct((2, LONN, D), BF),
            jax.ShapeDtypeStruct((2, DIAGN, D), BF),
        ),
        scratch_shapes=[
            pltpu.VMEM((2, LEV, 3, NC, D), BF),
            pltpu.VMEM((2, LEV, 9, 8, D), BF),
            pltpu.VMEM((ROWS, D), F32),
            pltpu.VMEM((LATN, D), F32),
            pltpu.SemaphoreType.DMA((2, 2)),
        ],
        compiler_params=params(60),
        cost_estimate=cost(1e6, 4e6),
        name="pack",
    )(x, dy)


def slot(at):
    return at // TOK


def assemble(slots, ref, halos, src, win):
    for lev in range(LEV):
        for r in range(3, NR):
            at = (lev * NR + r) * NC
            src[at : at + NC, :] = ref[lev, r].astype(F32)
    for own, at, size in own_segments():
        if slot(at) in slots:
            win[at : at + size, :] = src[own : own + size, :]
    for halo, segments in halos:
        count = halo.shape[-2]
        src[:count, :] = halo[...].astype(F32)
        for here, at, size, _ in segments():
            if slot(at) in slots:
                win[at : at + size, :] = src[here : here + size, :]


def layer_stats(x):
    mean = jnp.mean(x, -1, keepdims=True)
    cen = x - mean
    inv = lax.rsqrt(jnp.mean(cen * cen, -1, keepdims=True) + EPS)
    return cen, inv


def normalize(slots, base, win, gain_ref, xw_ref, nrm):
    for w in slots:
        x = win[w * TOK : (w + 1) * TOK, :]
        rows = slice((w - base) * TOK, (w - base + 1) * TOK)
        xw_ref[rows, :] = x.astype(BF)
        cen, inv = layer_stats(x)
        nrm[rows, :] = (cen * inv * gain_ref[...]).astype(BF)


def project(rows, nrm, dyw_ref, wq_ref, wp_ref, qkv, gatt):
    for j in range(6):
        cols = slice(j * 256, (j + 1) * 256)
        qkv[rows, cols] = dot(nrm[rows, :], wq_ref[:, cols], NN).astype(BF)
    for j in range(2):
        cols = slice(j * 256, (j + 1) * 256)
        gatt[rows, cols] = dot(dyw_ref[rows, :], wp_ref[cols, :], NT).astype(BF)


def attend(slots, base, qkv, gatt, att, gact_ref):
    low = lax.broadcasted_iota(jnp.int32, (TOK, 128), 1) < 64
    keyg = (lax.broadcasted_iota(jnp.int32, (TOK, 2 * TOK), 0) // 12) % 6 < 3
    qryg = (lax.broadcasted_iota(jnp.int32, (TOK, 2 * TOK), 1) // 12) % 6 < 3
    last = jnp.logical_and(lax.axis_index("y") == 3, lax.axis_index("xl") == 1)
    apart = jnp.logical_and(keyg != qryg, last)

    def stacked(v):
        z = jnp.zeros_like(v)
        return jnp.concatenate([jnp.where(low, v, z), jnp.where(low, z, v)], axis=0)

    for w in slots:
        rows = slice((w - base) * TOK, (w - base + 1) * TOK)
        for hp in range(4):
            at = hp * 128
            q2 = stacked(qkv[rows, at : at + 128] * jnp.bfloat16(0.125))
            k = qkv[rows, HH + at : HH + at + 128]
            v = qkv[rows, 2 * HH + at : 2 * HH + at + 128]
            g2 = stacked(gatt[rows, at : at + 128])
            s = dot(k, q2, NT)
            if w % 2:
                s = jnp.where(apart, -1000000000.0, s)
            e = jnp.exp(s - jnp.max(s, 0, keepdims=True))
            p = e * (1.0 / jnp.sum(e, 0, keepdims=True))
            pb = p.astype(BF)
            dp = dot(v, g2, NT)
            ds = (p * (dp - jnp.sum(p * dp, 0, keepdims=True))).astype(BF)
            o = dot(pb, v, TN)
            att[rows, at : at + 128] = jnp.where(low, o[:TOK], o[TOK:]).astype(BF)
            dq = dot(ds, k, TN)
            gact_ref[rows, at : at + 128] = (jnp.where(low, dq[:TOK], dq[TOK:]) * 0.125).astype(BF)
            gact_ref[rows, HH + at : HH + at + 128] = dot(ds, q2, NN).astype(BF)
            gact_ref[rows, 2 * HH + at : 2 * HH + at + 128] = dot(pb, g2, NN).astype(BF)


def early_kernel(w, x_ref, dy_ref, *refs):
    halo, refs = (refs[0], refs[1:]) if w else (None, refs)
    gain_ref, wq_ref, wp_ref, nrm_ref, xw_ref, dyw_ref, gact_ref, att_ref, src, win, qkv, gatt = refs
    halos = [((halo.at[a], lat_segments),) if w else () for a in range(2)]
    assemble((w,), x_ref, halos[0], src, win)
    normalize((w,), w, win, gain_ref, xw_ref, nrm_ref)
    assemble((w,), dy_ref, halos[1], src, win)
    dyw_ref[...] = win[w * TOK : (w + 1) * TOK, :].astype(BF)
    project(slice(0, TOK), nrm_ref, dyw_ref, wq_ref, wp_ref, qkv, gatt)
    attend((w,), w, qkv, gatt, att_ref, gact_ref)


def early_call(w, *operands):
    wide = jax.ShapeDtypeStruct((TOK, D), BF)
    return pl.pallas_call(
        functools.partial(early_kernel, w),
        out_shape=(
            wide,
            wide,
            wide,
            jax.ShapeDtypeStruct((TOK, 1536), BF),
            jax.ShapeDtypeStruct((TOK, HH), BF),
        ),
        scratch_shapes=[
            pltpu.VMEM((ROWS, D), F32),
            pltpu.VMEM((2 * TOK, D), F32),
            pltpu.VMEM((TOK, 1536), BF),
            pltpu.VMEM((TOK, HH), BF),
        ],
        compiler_params=params(16),
        cost_estimate=cost(2e9, 9e6),
        name=f"early{w}",
    )(*operands)


def main_kernel(x_ref, dy_ref, lat_ref, lon_ref, diag_ref, gain_ref, wq_ref, wp_ref, *refs):
    early, refs = (refs[0:5], refs[5:10]), refs[10:]
    keep_ref, send_ref, gact_ref, xw_ref, dyw_ref, src, win, nrm, qkv, gatt, att, normt = refs
    core = lax.axis_index("c")
    for w in range(2):
        for to, at in zip((nrm, xw_ref, dyw_ref, gact_ref, att), early[w]):
            to[w * TOK : (w + 1) * TOK, :] = at[...]
    rest = slice(2 * TOK, ROWS)
    for a, ref in enumerate((x_ref, dy_ref)):
        halos = ((lat_ref.at[a], lat_segments), (lon_ref.at[a], lon_segments), (diag_ref.at[a], diag_segments))
        assemble((2, 3), ref, halos, src, win)
        if a:
            dyw_ref[rest, :] = win[rest, :].astype(BF)
        else:
            normalize((2, 3), 0, win, gain_ref, xw_ref, nrm)
    project(rest, nrm, dyw_ref, wq_ref, wp_ref, qkv, gatt)
    attend((2, 3), 0, qkv, gatt, att, gact_ref)

    def put(slot_is_low, rows, cols, value):
        @pl.when(core == slot_is_low)
        def _():
            keep_ref[rows, cols] = value

        @pl.when(core != slot_is_low)
        def _():
            send_ref[rows, cols] = value

    normt[...] = nrm[...].T
    rows = slice(0, D)
    for j in range(4):
        cols = slice(j * 256, j * 256 + 256)
        put(0, rows, cols, dot(normt[...], gact_ref[:, cols], NN).astype(BF))
    for j in range(2):
        at = j * 256
        put(1, rows, slice(at, at + 256), dot(normt[...], gact_ref[:, 1024 + at : 1280 + at], NN).astype(BF))
    normt[...] = dyw_ref[...].T
    for j in range(2):
        at = j * 256
        put(1, rows, slice(512 + at, 768 + at), dot(normt[...], att[:, at : at + 256], NN).astype(BF))


def main_call(*operands):
    return pl.pallas_call(
        main_kernel,
        out_shape=(
            jax.ShapeDtypeStruct((D, 1024), BF),
            jax.ShapeDtypeStruct((D, 1024), BF),
            jax.ShapeDtypeStruct((ROWS, 1536), BF),
            jax.ShapeDtypeStruct((ROWS, D), BF),
            jax.ShapeDtypeStruct((ROWS, D), BF),
        ),
        scratch_shapes=[
            pltpu.VMEM((ROWS, D), F32),
            pltpu.VMEM((ROWS, D), F32),
            pltpu.VMEM((ROWS, D), BF),
            pltpu.VMEM((ROWS, 1536), BF),
            pltpu.VMEM((ROWS, HH), BF),
            pltpu.VMEM((ROWS, HH), BF),
            pltpu.VMEM((D, ROWS), BF),
        ],
        compiler_params=params(32),
        cost_estimate=cost(5.5e9, 14e6),
        name="main",
    )(*operands)


def input_rows(w, gact_ref, xw_ref, dyw_ref, gain, wq_ref, win):
    rows = slice(w * TOK, (w + 1) * TOK)
    gn = dot(gact_ref[rows, :], wq_ref[...], NT)
    cen, inv = layer_stats(xw_ref[rows, :].astype(F32))
    xhat = cen * inv
    g = gn * gain
    win[rows, :] = dyw_ref[rows, :].astype(F32) + inv * (
        g - jnp.mean(g, -1, keepdims=True) - xhat * jnp.mean(g * xhat, -1, keepdims=True)
    )
    return jnp.sum(gn * xhat, 0, keepdims=True)


def input_low_kernel(
    gact_ref, xw_ref, dyw_ref, gain_ref, wq_ref, own_ref, lat_ref, lon_ref, diag_ref, gg_ref, win, dst
):
    gain = gain_ref[...]
    gg_ref[...] = sum(input_rows(w, gact_ref, xw_ref, dyw_ref, gain, wq_ref, win) for w in (1, 3))
    for out, segments in ((lat_ref, lat_segments()), (lon_ref, lon_out_segments(0)), (diag_ref, diag_segments())):
        count = out.shape[0]
        dst[count - 16 : count, :] = jnp.zeros((16, D), F32)
        for at, here, size, _ in segments:
            dst[at : at + size, :] = win[here : here + size, :]
        out[...] = dst[:count, :].astype(BF)
    for own, here, size in own_segments():
        if slot(here) % 2:
            dst[own : own + size, :] = win[here : here + size, :]
    for lev in range(LEV):
        for r in range(9, NR):
            at = (lev * NR + r) * NC
            own_ref[lev, r - 9] = dst[at : at + NC, :].astype(BF)


def input_high_kernel(gact_ref, xw_ref, dyw_ref, gain_ref, wq_ref, lon0_ref, gg0_ref, own_ref, lon_ref, gg_ref, win, dst):
    gain = gain_ref[...]
    acc = gg0_ref[...] + sum(input_rows(w, gact_ref, xw_ref, dyw_ref, gain, wq_ref, win) for w in (0, 2))
    for j in range(8):
        gg_ref[j : j + 1, :] = acc[:, j * 128 : (j + 1) * 128]
    lon_ref[0:48, :] = lon0_ref[...]
    dst[64:80, :] = jnp.zeros((16, D), F32)
    for at, here, size, _ in lon_out_segments(1):
        dst[at - 48 : at - 48 + size, :] = win[here : here + size, :]
    lon_ref[48:128, :] = dst[0:80, :].astype(BF)
    for own, here, size in own_segments():
        if slot(here) % 2 == 0:
            dst[own : own + size, :] = win[here : here + size, :]
    for lev in range(LEV):
        for r in range(3, 9):
            at = (lev * NR + r) * NC
            own_ref[lev, r - 3] = dst[at : at + NC, :].astype(BF)


def lon_out_segments(part):
    for lev in range(LEV):
        for rr in (range(6, 9), range(6))[part]:
            at = (48 + (lev * 6 + rr) * 6) if part else (lev * 3 + rr - 6) * 6
            yield at, window_row(lev, rr, 18), 6, (lev * NR + rr + 3) * NC


def input_low_call(gact, xw, dyw, gain, wq):
    return pl.pallas_call(
        input_low_kernel,
        out_shape=(
            jax.ShapeDtypeStruct((LEV, 3, NC, D), BF),
            jax.ShapeDtypeStruct((LATN, D), BF),
            jax.ShapeDtypeStruct((48, D), BF),
            jax.ShapeDtypeStruct((DIAGN, D), BF),
            jax.ShapeDtypeStruct((1, D), F32),
        ),
        scratch_shapes=[pltpu.VMEM((ROWS, D), F32), pltpu.VMEM((ROWS, D), F32)],
        compiler_params=params(24),
        cost_estimate=cost(1e9, 9e6),
        name="input_low",
    )(gact, xw, dyw, gain, wq)


def input_high_call(gact, xw, dyw, gain, wq, lon0, gg0):
    return pl.pallas_call(
        input_high_kernel,
        out_shape=(
            jax.ShapeDtypeStruct((LEV, 6, NC, D), BF),
            jax.ShapeDtypeStruct((128, D), BF),
            jax.ShapeDtypeStruct((8, 128), F32),
        ),
        scratch_shapes=[pltpu.VMEM((ROWS, D), F32), pltpu.VMEM((ROWS, D), F32)],
        compiler_params=params(24),
        cost_estimate=cost(1e9, 9e6),
        name="input_high",
    )(gact, xw, dyw, gain, wq, lon0, gg0)


def join_kernel(high_ref, low_ref, lat_ref, lon_ref, diag_ref, out_ref, src, dst):
    for lev in range(LEV):
        for r in range(3, NR):
            at = (lev * NR + r) * NC
            part = high_ref[lev, r - 3] if r < 9 else low_ref[lev, r - 9]
            dst[at : at + NC, :] = part.astype(F32)
    lon_parts = [*lon_out_segments(0), *lon_out_segments(1)]
    for halo, segments in ((lat_ref, lat_segments()), (lon_ref, lon_parts), (diag_ref, diag_segments())):
        count = halo.shape[0]
        src[:count, :] = halo[...].astype(F32)
        for here, _, size, own in segments:
            dst[own : own + size, :] = src[here : here + size, :]
    for lev in range(LEV):
        for r in range(NR):
            at = (lev * NR + r) * NC
            out_ref[lev, r] = dst[at : at + NC, :].astype(BF)


def join_call(high, low, lat, lon, diag):
    return pl.pallas_call(
        join_kernel,
        out_shape=jax.ShapeDtypeStruct((LEV, NR, NC, D), BF),
        scratch_shapes=[pltpu.VMEM((128, D), F32), pltpu.VMEM((ROWS, D), F32)],
        compiler_params=params(12),
        cost_estimate=cost(1e6, 4e6),
        name="join",
    )(high, low, lat, lon, diag)


MSG = 272


def x_of():
    return lax.axis_index("xh") * 2 + lax.axis_index("xl")


def x_block(x):
    return lax.rem(x, 2) * 2 + x // 2


def put_gain(out, at, gg):
    hi = gg.astype(BF)
    out[at : at + 16, :] = jnp.zeros((16, 512), BF)
    out[at : at + 8, 0:128] = hi
    out[at : at + 8, 128:256] = (gg - hi.astype(F32)).astype(BF)


def take_gain(ref, at):
    return ref[at : at + 8, 0:128].astype(F32) + ref[at : at + 8, 128:256].astype(F32)


def split_kernel(keep_ref, recv_ref, gg_ref, owna, a1, a2, a3, ownb, b1, b2, b3):
    y = lax.axis_index("y")
    x = x_of()

    def total(rows, cols):
        return keep_ref[rows, cols].astype(F32) + recv_ref[rows, cols].astype(F32)

    for k, out in enumerate((owna, a1, a2, a3)):
        rows = pl.ds(pl.multiple_of(lax.rem(y + k, 4) * 256, 256), 256)
        out[0:256, :] = total(rows, slice(0, 512)).astype(out.dtype)
        if k:
            put_gain(out, 256, gg_ref[...])
    for k, out in enumerate((ownb, b1, b2, b3)):
        block = x_block(lax.rem(x + k, 4))
        for j in range(4):
            rows = pl.ds(pl.multiple_of(j * 256 + block * 64, 64), 64)
            out[j * 64 : (j + 1) * 64, :] = total(rows, slice(512, 1024)).astype(out.dtype)


def split_call(keep, recv, gg):
    mine = jax.ShapeDtypeStruct((256, 512), F32)
    a = jax.ShapeDtypeStruct((MSG, 512), BF)
    b = jax.ShapeDtypeStruct((256, 512), BF)
    return pl.pallas_call(
        split_kernel,
        out_shape=(mine, a, a, a, mine, b, b, b),
        compiler_params=params(12),
        cost_estimate=cost(1e6, 8e6),
        name="split",
    )(keep, recv, gg)


def cross_kernel(owna, a1, a2, a3, ownb, b1, b2, b3, gg_ref, gout, nowna, na1, na2, na3, nownb, nb1, nb2, nb3):
    y = lax.axis_index("y")
    x = x_of()
    gg = gg_ref[...] + take_gain(a1, 256) + take_gain(a2, 256) + take_gain(a3, 256)
    gout[...] = gg

    def total(rows, own, refs):
        value = own[rows, :]
        for ref in refs:
            value += ref[rows, :].astype(F32)
        return value

    for k, out in enumerate((nowna, na1, na2, na3)):
        rows = pl.ds(pl.multiple_of(x_block(lax.rem(x + k, 4)) * 64, 64), 64)
        out[0:64, :] = total(rows, owna, (a1, a2, a3)).astype(out.dtype)
        if k:
            put_gain(out, 64, gg)
    for k, out in enumerate((nownb, nb1, nb2, nb3)):
        rows = pl.ds(pl.multiple_of(lax.rem(y + k, 4) * 64, 64), 64)
        out[...] = total(rows, ownb, (b1, b2, b3)).astype(out.dtype)


def cross_call(*operands):
    mine = jax.ShapeDtypeStruct((64, 512), F32)
    a = jax.ShapeDtypeStruct((80, 512), BF)
    b = jax.ShapeDtypeStruct((64, 512), BF)
    return pl.pallas_call(
        cross_kernel,
        out_shape=(jax.ShapeDtypeStruct((8, 128), F32), mine, a, a, a, mine, b, b, b),
        compiler_params=params(8),
        cost_estimate=cost(1e6, 4e6),
        name="cross",
    )(*operands)


def gather_kernel(owna, a1, a2, a3, ownb, b1, b2, b3, gg_ref, out_ref):
    gg = gg_ref[...] + take_gain(a1, 64) + take_gain(a2, 64) + take_gain(a3, 64)
    gg = gg.astype(BF)
    for i in range(8):
        rows = slice(i * 8, (i + 1) * 8)
        parts = []
        for own, refs in ((owna, (a1, a2, a3)), (ownb, (b1, b2, b3))):
            value = own[rows, :]
            for ref in refs:
                value += ref[rows, :].astype(F32)
            parts.append(value)
        for j in range(2):
            half = slice(j * 4, j * 4 + 4)
            out_ref[2 * i + j, :, 0:512] = jnp.concatenate([parts[0][half], parts[1][half]], 0).astype(BF)
            out_ref[2 * i + j, :, 512:640] = gg


def gather_call(*operands):
    return pl.pallas_call(
        gather_kernel,
        out_shape=jax.ShapeDtypeStruct((16, 8, 640), BF),
        compiler_params=params(6),
        cost_estimate=cost(1e6, 4e6),
        name="gather",
    )(*operands)


def final_kernel(blocks, wq_ref, wp_ref, gain_ref, gg):
    low = jnp.zeros((8, 640), F32)
    high = jnp.zeros((8, 640), F32)
    for z in range(8):
        low += blocks[2 * z].astype(F32)
        high += blocks[2 * z + 1].astype(F32)
    low = low * FACTOR
    high = high * FACTOR
    wq_ref[:, 0:512] = low[0:4, 0:512]
    wq_ref[:, 512:1024] = low[4:8, 0:512]
    wq_ref[:, 1024:1536] = high[0:4, 0:512]
    wp_ref[...] = high[4:8, 0:512]
    gg[...] = low[:, 512:640] + high[:, 512:640]
    device = lax.axis_index("y") * 64 + lax.axis_index("xl") * 32 + lax.axis_index("xh") * 16
    device = device + lax.axis_index("z") * 2 + lax.axis_index("c")
    row = gg[pl.ds(device // 32, 1), :]
    gain_ref[...] = pltpu.roll(row, lax.rem(128 - lax.rem(device, 32) * 4, 128), 1)[:, 0:4]


def final_call(blocks):
    return pl.pallas_call(
        final_kernel,
        out_shape=(
            jax.ShapeDtypeStruct((4, 1536), F32),
            jax.ShapeDtypeStruct((4, HH), F32),
            jax.ShapeDtypeStruct((1, 4), F32),
        ),
        scratch_shapes=[pltpu.VMEM((8, 128), F32)],
        compiler_params=params(4),
        cost_estimate=cost(1e6, 1e6),
        name="final",
    )(blocks)


def shift_x(value, k):
    pairs = []
    for xl in range(2):
        for xh in range(2):
            to = (xh * 2 + xl + k) % 4
            pairs.append((xl * 2 + xh, (to % 2) * 2 + to // 2))
    return lax.ppermute(value, ("xl", "xh"), pairs)


def shift_y(value, k):
    return lax.ppermute(value, "y", shift(4, k))


def shift(n, k):
    return [(i, (i + k) % n) for i in range(n)]


def shift_both(k):
    pairs = []
    for i in range(8):
        for j in range(32):
            pairs.append((i * 32 + j, ((i + k) % 8) * 32 + (j + k) % 32))
    return pairs


LAT = ("y", "xl")
LON = ("xh", "z", "c")
ALL = LAT + LON


def per_device(x, dy, gain, wq, wp):
    gain2 = gain.reshape(1, D)
    lat, lon, diag = pack(x, dy)
    diag = lax.ppermute(diag, ALL, shift_both(-1))
    lon = lax.ppermute(lon, LON, shift(32, -1))
    lat = lax.ppermute(lat, LAT, shift(8, -1))
    early = early_call(0, x, dy, gain2, wq, wp)
    lat, first = lax.optimization_barrier((lat, early[0]))
    early = (first, *early[1:], *early_call(1, x, dy, lat, gain2, wq, wp))
    keep, send, gact, xw, dyw = main_call(x, dy, lat, lon, diag, gain2, wq, wp, *early)
    recv = lax.ppermute(send, "c", [(0, 1), (1, 0)])
    low, lat, lon0, diag, gg0 = input_low_call(gact, xw, dyw, gain2, wq)
    high, lon, gg = input_high_call(gact, xw, dyw, gain2, wq, lon0, gg0)
    oa, a1, a2, a3, ob, b1, b2, b3 = split_call(keep, recv, gg)
    a1, a2, a3 = (shift_y(v, k) for k, v in ((1, a1), (2, a2), (3, a3)))
    b1, b2, b3 = (shift_x(v, k) for k, v in ((1, b1), (2, b2), (3, b3)))
    lat = lax.ppermute(lat, LAT, shift(8, 1))
    lon = lax.ppermute(lon, LON, shift(32, 1))
    diag = lax.ppermute(diag, ALL, shift_both(1))
    gg, oa, a1, a2, a3, ob, b1, b2, b3 = cross_call(oa, a1, a2, a3, ob, b1, b2, b3, gg)
    a1, a2, a3 = (shift_x(v, k) for k, v in ((1, a1), (2, a2), (3, a3)))
    b1, b2, b3 = (shift_y(v, k) for k, v in ((1, b1), (2, b2), (3, b3)))
    grad_in = join_call(high, low, lat, lon, diag)
    a1, grad_in = lax.optimization_barrier((a1, grad_in))
    blocks = gather_call(oa, a1, a2, a3, ob, b1, b2, b3, gg)
    blocks = lax.all_to_all(blocks, ("z", "c"), 0, 0, tiled=True)
    grad_qkv, grad_proj, grad_gain = final_call(blocks)
    return grad_in, grad_qkv, grad_proj.T, grad_gain.reshape(4)


def solution(mesh):
    mesh = Mesh(mesh.devices.reshape(4, 2, 2, 8, 2), ALL)
    return jax.shard_map(
        per_device,
        mesh=mesh,
        in_specs=(P(None, LAT, LON, None), P(None, LAT, LON, None), P(), P(), P()),
        out_specs=(P(None, LAT, LON, None), P(ALL, None), P(None, ALL), P(ALL)),
        check_vma=False,
    )
```

```python
import functools

import jax
import jax.numpy as jnp
from jax import lax
from jax.experimental import pallas as pl
from jax.experimental.pallas import tpu as pltpu
from jax.sharding import Mesh, PartitionSpec as P


F32 = jnp.float32
BF = jnp.bfloat16
D = 1024
HH = 512
TOK = 144
NWIN = 4
ROWS = NWIN * TOK
LEV, NR, NC = 2, 12, 24
LATN = 112
LONN = 112
DIAGN = 48
EPS = 1e-05
FACTOR = 1.0 / 384.0

NN = (((1,), (0,)), ((), ()))
NT = (((1,), (1,)), ((), ()))
TN = (((0,), (0,)), ((), ()))


def dot(a, b, dims):
    return lax.dot_general(a, b, dims, preferred_element_type=F32)


def params(mib):
    return pltpu.CompilerParams(vmem_limit_bytes=mib * 1024 * 1024)


def cost(flops, nbytes):
    return pl.CostEstimate(flops=int(flops), bytes_accessed=int(nbytes), transcendentals=0)


def window_row(lev, rr, cc):
    return ((rr // 6) * 2 + cc // 12) * TOK + lev * 72 + (rr % 6) * 12 + cc % 12


def own_segments():
    for lev in range(LEV):
        for rr in range(9):
            base = (lev * NR + rr + 3) * NC
            yield base + 6, window_row(lev, rr, 0), 12
            yield base + 18, window_row(lev, rr, 12), 6


def lat_segments():
    for lev in range(LEV):
        for r in range(3):
            base = (lev * 3 + r) * 18
            yield base, window_row(lev, 9 + r, 0), 12, (lev * NR + r) * NC + 6
            yield base + 12, window_row(lev, 9 + r, 12), 6, (lev * NR + r) * NC + 18


def lon_segments():
    for lev in range(LEV):
        for rr in range(9):
            yield (lev * 9 + rr) * 6, window_row(lev, rr, 18), 6, (lev * NR + rr + 3) * NC


def diag_segments():
    for lev in range(LEV):
        for r in range(3):
            yield (lev * 3 + r) * 6, window_row(lev, 9 + r, 18), 6, (lev * NR + r) * NC


def pack_kernel(x_ref, dy_ref, lat_ref, lon_ref, diag_ref, top, side, src, dst, sems):
    copies = []
    for a, ref in enumerate((x_ref, dy_ref)):
        copies.append(
            (
                pltpu.make_async_copy(ref.at[:, 0:3], top.at[a], sems.at[a, 0]),
                pltpu.make_async_copy(ref.at[:, 3:12, 0:8, :], side.at[a], sems.at[a, 1]),
            )
        )
    for pair in copies:
        for copy in pair:
            copy.start()
    for a, pair in enumerate(copies):
        pair[0].wait()
        for lev in range(LEV):
            for r in range(3):
                at = (lev * NR + r) * NC
                src[at : at + NC, :] = top[a, lev, r].astype(F32)
        pair[1].wait()
        for lev in range(LEV):
            for r in range(3, NR):
                at = (lev * NR + r) * NC
                src[at : at + 8, :] = side[a, lev, r - 3].astype(F32)
        for out, segments in ((lat_ref, lat_segments), (lon_ref, lon_segments), (diag_ref, diag_segments)):
            count = out.shape[1]
            dst[count - 16 : count, :] = jnp.zeros((16, D), F32)
            for at, _, size, own in segments():
                dst[at : at + size, :] = src[own : own + size, :]
            out[a] = dst[:count, :].astype(BF)


def pack(x, dy):
    return pl.pallas_call(
        pack_kernel,
        in_specs=[pl.BlockSpec(memory_space=pltpu.HBM)] * 2,
        out_shape=(
            jax.ShapeDtypeStruct((2, LATN, D), BF),
            jax.ShapeDtypeStruct((2, LONN, D), BF),
            jax.ShapeDtypeStruct((2, DIAGN, D), BF),
        ),
        scratch_shapes=[
            pltpu.VMEM((2, LEV, 3, NC, D), BF),
            pltpu.VMEM((2, LEV, 9, 8, D), BF),
            pltpu.VMEM((ROWS, D), F32),
            pltpu.VMEM((LATN, D), F32),
            pltpu.SemaphoreType.DMA((2, 2)),
        ],
        compiler_params=params(60),
        cost_estimate=cost(1e6, 4e6),
        name="pack",
    )(x, dy)


def slot(at):
    return at // TOK


def assemble(slots, ref, halos, src, win):
    for lev in range(LEV):
        for r in range(3, 9) if slots[0] < 2 else range(9, NR):
            at = (lev * NR + r) * NC
            src[at : at + NC, :] = ref[lev, r].astype(F32)
    for own, at, size in own_segments():
        if slot(at) in slots:
            win[at : at + size, :] = src[own : own + size, :]
    for halo, segments in halos:
        count = halo.shape[-2]
        src[:count, :] = halo[...].astype(F32)
        for here, at, size, _ in segments():
            if slot(at) in slots:
                win[at : at + size, :] = src[here : here + size, :]


def layer_stats(x):
    mean = jnp.mean(x, -1, keepdims=True)
    cen = x - mean
    inv = lax.rsqrt(jnp.mean(cen * cen, -1, keepdims=True) + EPS)
    return cen, inv


def normalize(slots, base, win, gain_ref, xw_ref, nrm):
    for w in slots:
        x = win[w * TOK : (w + 1) * TOK, :]
        rows = slice((w - base) * TOK, (w - base + 1) * TOK)
        xw_ref[rows, :] = x.astype(BF)
        cen, inv = layer_stats(x)
        nrm[rows, :] = (cen * inv * gain_ref[...]).astype(BF)


def project(rows, nrm, dyw_ref, wq_ref, wp_ref, qkv, gatt):
    for j in range(6):
        cols = slice(j * 256, (j + 1) * 256)
        qkv[rows, cols] = dot(nrm[rows, :], wq_ref[:, cols], NN).astype(BF)
    for j in range(2):
        cols = slice(j * 256, (j + 1) * 256)
        gatt[rows, cols] = dot(dyw_ref[rows, :], wp_ref[cols, :], NT).astype(BF)


def attend(slots, base, qkv, gatt, gact_ref):
    low = lax.broadcasted_iota(jnp.int32, (TOK, 128), 1) < 64
    keyg = (lax.broadcasted_iota(jnp.int32, (TOK, 2 * TOK), 0) // 12) % 6 < 3
    qryg = (lax.broadcasted_iota(jnp.int32, (TOK, 2 * TOK), 1) // 12) % 6 < 3
    last = jnp.logical_and(lax.axis_index("y") == 3, lax.axis_index("xl") == 1)
    apart = jnp.logical_and(keyg != qryg, last)

    def stacked(v):
        z = jnp.zeros_like(v)
        return jnp.concatenate([jnp.where(low, v, z), jnp.where(low, z, v)], axis=0)

    for w in slots:
        rows = slice((w - base) * TOK, (w - base + 1) * TOK)
        for hp in range(4):
            at = hp * 128
            q2 = stacked(qkv[rows, at : at + 128] * jnp.bfloat16(0.125))
            k = qkv[rows, HH + at : HH + at + 128]
            v = qkv[rows, 2 * HH + at : 2 * HH + at + 128]
            g2 = stacked(gatt[rows, at : at + 128])
            s = dot(k, q2, NT)
            if w >= 2:
                s = jnp.where(apart, -1000000000.0, s)
            e = jnp.exp(s - jnp.max(s, 0, keepdims=True))
            p = e * (1.0 / jnp.sum(e, 0, keepdims=True))
            pb = p.astype(BF)
            dp = dot(v, g2, NT)
            ds = (p * (dp - jnp.sum(p * dp, 0, keepdims=True))).astype(BF)
            o = dot(pb, v, TN)
            gact_ref[rows, 3 * HH + at : 3 * HH + at + 128] = jnp.where(low, o[:TOK], o[TOK:]).astype(BF)
            dq = dot(ds, k, TN)
            gact_ref[rows, at : at + 128] = (jnp.where(low, dq[:TOK], dq[TOK:]) * 0.125).astype(BF)
            gact_ref[rows, HH + at : HH + at + 128] = dot(ds, q2, NN).astype(BF)
            gact_ref[rows, 2 * HH + at : 2 * HH + at + 128] = dot(pb, g2, NN).astype(BF)


def early_kernel(w, x_ref, dy_ref, *refs):
    halo, refs = (refs[0], refs[1:]) if w else (None, refs)
    gain_ref, wq_ref, wp_ref, nrm_ref, xw_ref, dyw_ref, gact_ref, src, win, qkv, gatt = refs
    halos = [((halo.at[a], lon_segments),) if w else () for a in range(2)]
    assemble((w,), x_ref, halos[0], src, win)
    normalize((w,), w, win, gain_ref, xw_ref, nrm_ref)
    assemble((w,), dy_ref, halos[1], src, win)
    dyw_ref[...] = win[w * TOK : (w + 1) * TOK, :].astype(BF)
    project(slice(0, TOK), nrm_ref, dyw_ref, wq_ref, wp_ref, qkv, gatt)
    attend((w,), w, qkv, gatt, gact_ref)


def early_call(w, *operands):
    wide = jax.ShapeDtypeStruct((TOK, D), BF)
    return pl.pallas_call(
        functools.partial(early_kernel, w),
        out_shape=(
            wide,
            wide,
            wide,
            jax.ShapeDtypeStruct((TOK, 2048), BF),
        ),
        scratch_shapes=[
            pltpu.VMEM((ROWS, D), F32),
            pltpu.VMEM((2 * TOK, D), F32),
            pltpu.VMEM((TOK, 1536), BF),
            pltpu.VMEM((TOK, HH), BF),
        ],
        compiler_params=params(16),
        cost_estimate=cost(2e9, 9e6),
    )(*operands)


def main_kernel(x_ref, dy_ref, lat_ref, lon_ref, diag_ref, gain_ref, wq_ref, wp_ref, *refs):
    early, refs = (refs[0:4], refs[4:8]), refs[8:]
    keep_ref, send_ref, gact_ref, xw_ref, dyw_ref, src, win, nrm, qkv, gatt, lhs = refs
    core = lax.axis_index("c")
    for w in range(2):
        for to, at in zip((nrm, xw_ref, dyw_ref, gact_ref), early[w]):
            to[w * TOK : (w + 1) * TOK, :] = at[...]
    rest = slice(2 * TOK, ROWS)
    for a, ref in enumerate((x_ref, dy_ref)):
        halos = ((lat_ref.at[a], lat_segments), (lon_ref.at[a], lon_segments), (diag_ref.at[a], diag_segments))
        assemble((2, 3), ref, halos, src, win)
        if a:
            dyw_ref[rest, :] = win[rest, :].astype(BF)
        else:
            normalize((2, 3), 0, win, gain_ref, xw_ref, nrm)
    project(rest, nrm, dyw_ref, wq_ref, wp_ref, qkv, gatt)
    attend((2, 3), 0, qkv, gatt, gact_ref)

    lhs[0] = nrm[...].T
    lhs[1] = dyw_ref[...].T
    for out, half in ((send_ref, 1 - core), (keep_ref, core)):
        low = pl.ds(pl.multiple_of(half * 1024, 1024), 512)
        high = pl.ds(pl.multiple_of(half * 1024 + 512, 512), 512)
        for i in range(4):
            rows = slice(i * 256, (i + 1) * 256)
            out[rows, 0:512] = dot(lhs[0, rows, :], gact_ref[:, low], NN).astype(BF)
            out[rows, 512:1024] = dot(lhs[half, rows, :], gact_ref[:, high], NN).astype(BF)


def main_call(*operands):
    return pl.pallas_call(
        main_kernel,
        out_shape=(
            jax.ShapeDtypeStruct((D, 1024), BF),
            jax.ShapeDtypeStruct((D, 1024), BF),
            jax.ShapeDtypeStruct((ROWS, 2048), BF),
            jax.ShapeDtypeStruct((ROWS, D), BF),
            jax.ShapeDtypeStruct((ROWS, D), BF),
        ),
        scratch_shapes=[
            pltpu.VMEM((ROWS, D), F32),
            pltpu.VMEM((ROWS, D), F32),
            pltpu.VMEM((ROWS, D), BF),
            pltpu.VMEM((ROWS, 1536), BF),
            pltpu.VMEM((ROWS, HH), BF),
            pltpu.VMEM((2, D, ROWS), BF),
        ],
        compiler_params=params(32),
        cost_estimate=cost(5.5e9, 14e6),
        name="main",
    )(*operands)


def input_rows(w, gact_ref, xw_ref, dyw_ref, gain, wq_ref, win):
    rows = slice(w * TOK, (w + 1) * TOK)
    gn = dot(gact_ref[rows, 0:1536], wq_ref[...], NT)
    cen, inv = layer_stats(xw_ref[rows, :].astype(F32))
    xhat = cen * inv
    g = gn * gain
    win[rows, :] = dyw_ref[rows, :].astype(F32) + inv * (
        g - jnp.mean(g, -1, keepdims=True) - xhat * jnp.mean(g * xhat, -1, keepdims=True)
    )
    return jnp.sum(gn * xhat, 0, keepdims=True)


def input_low_kernel(
    gact_ref, xw_ref, dyw_ref, gain_ref, wq_ref, own_ref, lat_ref, lon_ref, diag_ref, gg_ref, win, dst
):
    gain = gain_ref[...]
    gg_ref[...] = sum(input_rows(w, gact_ref, xw_ref, dyw_ref, gain, wq_ref, win) for w in (2, 3))
    for out, segments in ((lat_ref, lat_segments()), (lon_ref, lon_out_segments(0)), (diag_ref, diag_segments())):
        count = out.shape[0]
        dst[count - 16 : count, :] = jnp.zeros((16, D), F32)
        for at, here, size, _ in segments:
            dst[at : at + size, :] = win[here : here + size, :]
        out[...] = dst[:count, :].astype(BF)
    for own, here, size in own_segments():
        if slot(here) >= 2:
            dst[own : own + size, :] = win[here : here + size, :]
    for lev in range(LEV):
        for r in range(9, NR):
            at = (lev * NR + r) * NC
            own_ref[lev, r - 9] = dst[at : at + NC, :].astype(BF)


def input_high_kernel(gact_ref, xw_ref, dyw_ref, gain_ref, wq_ref, lon0_ref, gg0_ref, own_ref, lon_ref, gg_ref, win, dst):
    gain = gain_ref[...]
    acc = gg0_ref[...] + sum(input_rows(w, gact_ref, xw_ref, dyw_ref, gain, wq_ref, win) for w in (0, 1))
    for j in range(8):
        gg_ref[j : j + 1, :] = acc[:, j * 128 : (j + 1) * 128]
    lon_ref[0:48, :] = lon0_ref[...]
    dst[64:80, :] = jnp.zeros((16, D), F32)
    for at, here, size, _ in lon_out_segments(1):
        dst[at - 48 : at - 48 + size, :] = win[here : here + size, :]
    lon_ref[48:128, :] = dst[0:80, :].astype(BF)
    for own, here, size in own_segments():
        if slot(here) < 2:
            dst[own : own + size, :] = win[here : here + size, :]
    for lev in range(LEV):
        for r in range(3, 9):
            at = (lev * NR + r) * NC
            own_ref[lev, r - 3] = dst[at : at + NC, :].astype(BF)


def lon_out_segments(part):
    for lev in range(LEV):
        for rr in (range(6, 9), range(6))[part]:
            at = (48 + (lev * 6 + rr) * 6) if part else (lev * 3 + rr - 6) * 6
            yield at, window_row(lev, rr, 18), 6, (lev * NR + rr + 3) * NC


def input_low_call(gact, xw, dyw, gain, wq):
    return pl.pallas_call(
        input_low_kernel,
        out_shape=(
            jax.ShapeDtypeStruct((LEV, 3, NC, D), BF),
            jax.ShapeDtypeStruct((LATN, D), BF),
            jax.ShapeDtypeStruct((48, D), BF),
            jax.ShapeDtypeStruct((DIAGN, D), BF),
            jax.ShapeDtypeStruct((1, D), F32),
        ),
        scratch_shapes=[pltpu.VMEM((ROWS, D), F32), pltpu.VMEM((ROWS, D), F32)],
        compiler_params=params(24),
        cost_estimate=cost(1e9, 9e6),
        name="input_low",
    )(gact, xw, dyw, gain, wq)


def input_high_call(gact, xw, dyw, gain, wq, lon0, gg0):
    return pl.pallas_call(
        input_high_kernel,
        out_shape=(
            jax.ShapeDtypeStruct((LEV, 6, NC, D), BF),
            jax.ShapeDtypeStruct((128, D), BF),
            jax.ShapeDtypeStruct((8, 128), F32),
        ),
        scratch_shapes=[pltpu.VMEM((ROWS, D), F32), pltpu.VMEM((ROWS, D), F32)],
        compiler_params=params(24),
        cost_estimate=cost(1e9, 9e6),
        name="input_high",
    )(gact, xw, dyw, gain, wq, lon0, gg0)


def join_kernel(high_ref, low_ref, lat_ref, lon_ref, diag_ref, out_ref, src, dst):
    for lev in range(LEV):
        for r in range(3, NR):
            at = (lev * NR + r) * NC
            part = high_ref[lev, r - 3] if r < 9 else low_ref[lev, r - 9]
            dst[at : at + NC, :] = part.astype(F32)
    lon_parts = [*lon_out_segments(0), *lon_out_segments(1)]
    for halo, segments in ((lat_ref, lat_segments()), (lon_ref, lon_parts), (diag_ref, diag_segments())):
        count = halo.shape[0]
        src[:count, :] = halo[...].astype(F32)
        for here, _, size, own in segments:
            dst[own : own + size, :] = src[here : here + size, :]
    for lev in range(LEV):
        for r in range(NR):
            at = (lev * NR + r) * NC
            out_ref[lev, r] = dst[at : at + NC, :].astype(BF)


def join_call(high, low, lat, lon, diag):
    return pl.pallas_call(
        join_kernel,
        out_shape=jax.ShapeDtypeStruct((LEV, NR, NC, D), BF),
        scratch_shapes=[pltpu.VMEM((128, D), F32), pltpu.VMEM((ROWS, D), F32)],
        compiler_params=params(12),
        cost_estimate=cost(1e6, 4e6),
        name="join",
    )(high, low, lat, lon, diag)


MSG = 272


def x_of():
    return lax.axis_index("xh") * 2 + lax.axis_index("xl")


def x_block(x):
    return lax.rem(x, 2) * 2 + x // 2


def put_gain(out, at, gg):
    hi = gg.astype(BF)
    out[at : at + 16, :] = jnp.zeros((16, 512), BF)
    out[at : at + 8, 0:128] = hi
    out[at : at + 8, 128:256] = (gg - hi.astype(F32)).astype(BF)


def take_gain(ref, at):
    return ref[at : at + 8, 0:128].astype(F32) + ref[at : at + 8, 128:256].astype(F32)


def split_kernel(keep_ref, recv_ref, gg_ref, owna, a1, a2, a3, ownb, b1, b2, b3):
    y = lax.axis_index("y")
    x = x_of()

    def total(rows, cols):
        return keep_ref[rows, cols].astype(F32) + recv_ref[rows, cols].astype(F32)

    for k, out in enumerate((owna, a1, a2, a3)):
        rows = pl.ds(pl.multiple_of(lax.rem(y + k, 4) * 256, 256), 256)
        out[0:256, :] = total(rows, slice(0, 512)).astype(out.dtype)
        if k:
            put_gain(out, 256, gg_ref[...])
    for k, out in enumerate((ownb, b1, b2, b3)):
        block = x_block(lax.rem(x + k, 4))
        for j in range(4):
            rows = pl.ds(pl.multiple_of(j * 256 + block * 64, 64), 64)
            out[j * 64 : (j + 1) * 64, :] = total(rows, slice(512, 1024)).astype(out.dtype)


def split_call(keep, recv, gg):
    mine = jax.ShapeDtypeStruct((256, 512), F32)
    a = jax.ShapeDtypeStruct((MSG, 512), BF)
    b = jax.ShapeDtypeStruct((256, 512), BF)
    return pl.pallas_call(
        split_kernel,
        out_shape=(mine, a, a, a, mine, b, b, b),
        compiler_params=params(12),
        cost_estimate=cost(1e6, 8e6),
        name="split",
    )(keep, recv, gg)


def cross_kernel(owna, a1, a2, a3, ownb, b1, b2, b3, gg_ref, gout, nowna, na1, na2, na3, nownb, nb1, nb2, nb3):
    y = lax.axis_index("y")
    x = x_of()
    gg = gg_ref[...] + take_gain(a1, 256) + take_gain(a2, 256) + take_gain(a3, 256)
    gout[...] = gg

    def total(rows, own, refs):
        value = own[rows, :]
        for ref in refs:
            value += ref[rows, :].astype(F32)
        return value

    for k, out in enumerate((nowna, na1, na2, na3)):
        rows = pl.ds(pl.multiple_of(x_block(lax.rem(x + k, 4)) * 64, 64), 64)
        out[0:64, :] = total(rows, owna, (a1, a2, a3)).astype(out.dtype)
        if k:
            put_gain(out, 64, gg)
    for k, out in enumerate((nownb, nb1, nb2, nb3)):
        rows = pl.ds(pl.multiple_of(lax.rem(y + k, 4) * 64, 64), 64)
        out[...] = total(rows, ownb, (b1, b2, b3)).astype(out.dtype)


def cross_call(*operands):
    mine = jax.ShapeDtypeStruct((64, 512), F32)
    a = jax.ShapeDtypeStruct((80, 512), BF)
    b = jax.ShapeDtypeStruct((64, 512), BF)
    return pl.pallas_call(
        cross_kernel,
        out_shape=(jax.ShapeDtypeStruct((8, 128), F32), mine, a, a, a, mine, b, b, b),
        compiler_params=params(8),
        cost_estimate=cost(1e6, 4e6),
        name="cross",
    )(*operands)


def gather_kernel(owna, a1, a2, a3, ownb, b1, b2, b3, gg_ref, out_ref):
    gg = gg_ref[...] + take_gain(a1, 64) + take_gain(a2, 64) + take_gain(a3, 64)
    gg = gg.astype(BF)
    for i in range(8):
        rows = slice(i * 8, (i + 1) * 8)
        parts = []
        for own, refs in ((owna, (a1, a2, a3)), (ownb, (b1, b2, b3))):
            value = own[rows, :]
            for ref in refs:
                value += ref[rows, :].astype(F32)
            parts.append(value)
        for j in range(2):
            half = slice(j * 4, j * 4 + 4)
            out_ref[2 * i + j, :, 0:512] = jnp.concatenate([parts[0][half], parts[1][half]], 0).astype(BF)
            out_ref[2 * i + j, :, 512:640] = gg


def gather_call(*operands):
    return pl.pallas_call(
        gather_kernel,
        out_shape=jax.ShapeDtypeStruct((16, 8, 640), BF),
        compiler_params=params(6),
        cost_estimate=cost(1e6, 4e6),
        name="gather",
    )(*operands)


def final_kernel(blocks, wq_ref, wp_ref, gain_ref, gg):
    low = jnp.zeros((8, 640), F32)
    high = jnp.zeros((8, 640), F32)
    for z in range(8):
        low += blocks[2 * z].astype(F32)
        high += blocks[2 * z + 1].astype(F32)
    low = low * FACTOR
    high = high * FACTOR
    wq_ref[:, 0:512] = low[0:4, 0:512]
    wq_ref[:, 512:1024] = low[4:8, 0:512]
    wq_ref[:, 1024:1536] = high[0:4, 0:512]
    wp_ref[...] = high[4:8, 0:512]
    gg[...] = low[:, 512:640] + high[:, 512:640]
    device = lax.axis_index("y") * 64 + lax.axis_index("xl") * 32 + lax.axis_index("xh") * 16
    device = device + lax.axis_index("z") * 2 + lax.axis_index("c")
    row = gg[pl.ds(device // 32, 1), :]
    gain_ref[...] = pltpu.roll(row, lax.rem(128 - lax.rem(device, 32) * 4, 128), 1)[:, 0:4]


def final_call(blocks):
    return pl.pallas_call(
        final_kernel,
        out_shape=(
            jax.ShapeDtypeStruct((4, 1536), F32),
            jax.ShapeDtypeStruct((4, HH), F32),
            jax.ShapeDtypeStruct((1, 4), F32),
        ),
        scratch_shapes=[pltpu.VMEM((8, 128), F32)],
        compiler_params=params(4),
        cost_estimate=cost(1e6, 1e6),
        name="final",
    )(blocks)


def shift_x(value, k):
    pairs = []
    for xl in range(2):
        for xh in range(2):
            to = (xh * 2 + xl + k) % 4
            pairs.append((xl * 2 + xh, (to % 2) * 2 + to // 2))
    return lax.ppermute(value, ("xl", "xh"), pairs)


def shift_y(value, k):
    return lax.ppermute(value, "y", shift(4, k))


def shift(n, k):
    return [(i, (i + k) % n) for i in range(n)]


def shift_both(k):
    pairs = []
    for i in range(8):
        for j in range(32):
            pairs.append((i * 32 + j, ((i + k) % 8) * 32 + (j + k) % 32))
    return pairs


LAT = ("y", "xl")
LON = ("xh", "z", "c")
ALL = LAT + LON


def program(x, dy, gain, wq, wp):
    gain2 = gain.reshape(1, D)
    lat, lon, diag = pack(x, dy)
    lon = lax.ppermute(lon, LON, shift(32, -1))
    lat = lax.ppermute(lat, LAT, shift(8, -1))
    diag = lax.ppermute(diag, ALL, shift_both(-1))
    early = early_call(0, x, dy, gain2, wq, wp)
    lon, first = lax.optimization_barrier((lon, early[0]))
    early = (first, *early[1:], *early_call(1, x, dy, lon, gain2, wq, wp))
    keep, send, gact, xw, dyw = main_call(x, dy, lat, lon, diag, gain2, wq, wp, *early)
    recv = lax.ppermute(send, "c", [(0, 1), (1, 0)])
    low, lat, lon0, diag, gg0 = input_low_call(gact, xw, dyw, gain2, wq)
    high, lon, gg = input_high_call(gact, xw, dyw, gain2, wq, lon0, gg0)
    oa, a1, a2, a3, ob, b1, b2, b3 = split_call(keep, recv, gg)
    a1, a2, a3 = (shift_y(v, k) for k, v in ((1, a1), (2, a2), (3, a3)))
    b1, b2, b3 = (shift_x(v, k) for k, v in ((1, b1), (2, b2), (3, b3)))
    lat = lax.ppermute(lat, LAT, shift(8, 1))
    lon = lax.ppermute(lon, LON, shift(32, 1))
    diag = lax.ppermute(diag, ALL, shift_both(1))
    gg, oa, a1, a2, a3, ob, b1, b2, b3 = cross_call(oa, a1, a2, a3, ob, b1, b2, b3, gg)
    a1, a2, a3 = (shift_x(v, k) for k, v in ((1, a1), (2, a2), (3, a3)))
    b1, b2, b3 = (shift_y(v, k) for k, v in ((1, b1), (2, b2), (3, b3)))
    grad_in = join_call(high, low, lat, lon, diag)
    a1, grad_in = lax.optimization_barrier((a1, grad_in))
    blocks = gather_call(oa, a1, a2, a3, ob, b1, b2, b3, gg)
    blocks = lax.all_to_all(blocks, ("z", "c"), 0, 0, tiled=True)
    grad_qkv, grad_proj, grad_gain = final_call(blocks)
    return grad_in, grad_qkv, grad_proj.T, grad_gain.reshape(4)


def solution(mesh):
    mesh = Mesh(mesh.devices.reshape(4, 2, 2, 8, 2), ALL)
    return jax.shard_map(
        program,
        mesh=mesh,
        in_specs=(P(None, LAT, LON, None), P(None, LAT, LON, None), P(), P(), P()),
        out_specs=(P(None, LAT, LON, None), P(ALL, None), P(None, ALL), P(ALL)),
        check_vma=False,
    )
```

```python
import functools

import jax
import jax.numpy as jnp
from jax import lax
from jax.experimental import pallas as pl
from jax.experimental.pallas import tpu as pltpu
from jax.sharding import Mesh, PartitionSpec as P


F32 = jnp.float32
BF = jnp.bfloat16
D = 1024
HH = 512
TOK = 144
NWIN = 4
ROWS = NWIN * TOK
LEV, NR, NC = 2, 12, 24
LATN = 112
LONN = 112
DIAGN = 48
EPS = 1e-05
FACTOR = 1.0 / 384.0

NN = (((1,), (0,)), ((), ()))
NT = (((1,), (1,)), ((), ()))
TN = (((0,), (0,)), ((), ()))


def dot(a, b, dims):
    return lax.dot_general(a, b, dims, preferred_element_type=F32)


def params(mib):
    return pltpu.CompilerParams(vmem_limit_bytes=mib * 1024 * 1024)


def cost(flops, nbytes):
    return pl.CostEstimate(flops=int(flops), bytes_accessed=int(nbytes), transcendentals=0)


def window_row(lev, rr, cc):
    return ((rr // 6) * 2 + cc // 12) * TOK + lev * 72 + (rr % 6) * 12 + cc % 12


def own_segments():
    for lev in range(LEV):
        for rr in range(9):
            base = (lev * NR + rr + 3) * NC
            yield base + 6, window_row(lev, rr, 0), 12
            yield base + 18, window_row(lev, rr, 12), 6


def lat_segments():
    for lev in range(LEV):
        for r in range(3):
            base = (lev * 3 + r) * 18
            yield base, window_row(lev, 9 + r, 0), 12, (lev * NR + r) * NC + 6
            yield base + 12, window_row(lev, 9 + r, 12), 6, (lev * NR + r) * NC + 18


def lon_segments():
    for lev in range(LEV):
        for rr in range(9):
            yield (lev * 9 + rr) * 6, window_row(lev, rr, 18), 6, (lev * NR + rr + 3) * NC


def diag_segments():
    for lev in range(LEV):
        for r in range(3):
            yield (lev * 3 + r) * 6, window_row(lev, 9 + r, 18), 6, (lev * NR + r) * NC


def pack_kernel(x_ref, dy_ref, lat_ref, lon_ref, diag_ref, top, side, src, dst, sems):
    copies = []
    for a, ref in enumerate((x_ref, dy_ref)):
        copies.append(
            (
                pltpu.make_async_copy(ref.at[:, 0:3], top.at[a], sems.at[a, 0]),
                pltpu.make_async_copy(ref.at[:, 3:12, 0:8, :], side.at[a], sems.at[a, 1]),
            )
        )
    for pair in copies:
        for copy in pair:
            copy.start()
    for a, pair in enumerate(copies):
        pair[0].wait()
        for lev in range(LEV):
            for r in range(3):
                at = (lev * NR + r) * NC
                src[at : at + NC, :] = top[a, lev, r].astype(F32)
        pair[1].wait()
        for lev in range(LEV):
            for r in range(3, NR):
                at = (lev * NR + r) * NC
                src[at : at + 8, :] = side[a, lev, r - 3].astype(F32)
        for out, segments in ((lat_ref, lat_segments), (lon_ref, lon_segments), (diag_ref, diag_segments)):
            count = out.shape[1]
            dst[count - 16 : count, :] = jnp.zeros((16, D), F32)
            for at, _, size, own in segments():
                dst[at : at + size, :] = src[own : own + size, :]
            out[a] = dst[:count, :].astype(BF)


def pack(x, dy):
    return pl.pallas_call(
        pack_kernel,
        in_specs=[pl.BlockSpec(memory_space=pltpu.HBM)] * 2,
        out_shape=(
            jax.ShapeDtypeStruct((2, LATN, D), BF),
            jax.ShapeDtypeStruct((2, LONN, D), BF),
            jax.ShapeDtypeStruct((2, DIAGN, D), BF),
        ),
        scratch_shapes=[
            pltpu.VMEM((2, LEV, 3, NC, D), BF),
            pltpu.VMEM((2, LEV, 9, 8, D), BF),
            pltpu.VMEM((ROWS, D), F32),
            pltpu.VMEM((LATN, D), F32),
            pltpu.SemaphoreType.DMA((2, 2)),
        ],
        compiler_params=params(60),
        cost_estimate=cost(1e6, 4e6),
        name="pack",
    )(x, dy)


def slot(at):
    return at // TOK


def assemble(slots, ref, halos, src, win):
    for lev in range(LEV):
        for r in range(3, 9) if slots[0] < 2 else range(9, NR):
            at = (lev * NR + r) * NC
            src[at : at + NC, :] = ref[lev, r].astype(F32)
    for own, at, size in own_segments():
        if slot(at) in slots:
            win[at : at + size, :] = src[own : own + size, :]
    for halo, segments in halos:
        count = halo.shape[-2]
        src[:count, :] = halo[...].astype(F32)
        for here, at, size, _ in segments():
            if slot(at) in slots:
                win[at : at + size, :] = src[here : here + size, :]


def layer_stats(x):
    mean = jnp.mean(x, -1, keepdims=True)
    cen = x - mean
    inv = lax.rsqrt(jnp.mean(cen * cen, -1, keepdims=True) + EPS)
    return cen, inv


def normalize(slots, base, win, gain_ref, xw_ref, nrm):
    for w in slots:
        x = win[w * TOK : (w + 1) * TOK, :]
        rows = slice((w - base) * TOK, (w - base + 1) * TOK)
        xw_ref[rows, :] = x.astype(BF)
        cen, inv = layer_stats(x)
        nrm[rows, :] = (cen * inv * gain_ref[...]).astype(BF)


def project(rows, nrm, dyw_ref, wq_ref, wp_ref, qkv, gatt):
    for j in range(6):
        cols = slice(j * 256, (j + 1) * 256)
        qkv[rows, cols] = dot(nrm[rows, :], wq_ref[:, cols], NN).astype(BF)
    for j in range(2):
        cols = slice(j * 256, (j + 1) * 256)
        gatt[rows, cols] = dot(dyw_ref[rows, :], wp_ref[cols, :], NT).astype(BF)


def attend(slots, base, qkv, gatt, gact_ref):
    low = lax.broadcasted_iota(jnp.int32, (TOK, 128), 1) < 64
    keyg = (lax.broadcasted_iota(jnp.int32, (TOK, 2 * TOK), 0) // 12) % 6 < 3
    qryg = (lax.broadcasted_iota(jnp.int32, (TOK, 2 * TOK), 1) // 12) % 6 < 3
    last = jnp.logical_and(lax.axis_index("y") == 3, lax.axis_index("xl") == 1)
    apart = jnp.logical_and(keyg != qryg, last)

    def stacked(v):
        z = jnp.zeros_like(v)
        return jnp.concatenate([jnp.where(low, v, z), jnp.where(low, z, v)], axis=0)

    for w in slots:
        rows = slice((w - base) * TOK, (w - base + 1) * TOK)
        for hp in range(4):
            at = hp * 128
            q2 = stacked(qkv[rows, at : at + 128] * jnp.bfloat16(0.125))
            k = qkv[rows, HH + at : HH + at + 128]
            v = qkv[rows, 2 * HH + at : 2 * HH + at + 128]
            g2 = stacked(gatt[rows, at : at + 128])
            s = dot(k, q2, NT)
            if w >= 2:
                s = jnp.where(apart, -1000000000.0, s)
            e = jnp.exp(s - jnp.max(s, 0, keepdims=True))
            p = e * (1.0 / jnp.sum(e, 0, keepdims=True))
            pb = p.astype(BF)
            dp = dot(v, g2, NT)
            ds = (p * (dp - jnp.sum(p * dp, 0, keepdims=True))).astype(BF)
            o = dot(pb, v, TN)
            gact_ref[rows, 3 * HH + at : 3 * HH + at + 128] = jnp.where(low, o[:TOK], o[TOK:]).astype(BF)
            dq = dot(ds, k, TN)
            gact_ref[rows, at : at + 128] = (jnp.where(low, dq[:TOK], dq[TOK:]) * 0.125).astype(BF)
            gact_ref[rows, HH + at : HH + at + 128] = dot(ds, q2, NN).astype(BF)
            gact_ref[rows, 2 * HH + at : 2 * HH + at + 128] = dot(pb, g2, NN).astype(BF)


def early_kernel(w, x_ref, dy_ref, *refs):
    halo, refs = (refs[0], refs[1:]) if w else (None, refs)
    gain_ref, wq_ref, wp_ref, nrm_ref, xw_ref, dyw_ref, gact_ref, src, win, qkv, gatt = refs
    halos = [((halo.at[a], lon_segments),) if w else () for a in range(2)]
    assemble((w,), x_ref, halos[0], src, win)
    normalize((w,), w, win, gain_ref, xw_ref, nrm_ref)
    assemble((w,), dy_ref, halos[1], src, win)
    dyw_ref[...] = win[w * TOK : (w + 1) * TOK, :].astype(BF)
    project(slice(0, TOK), nrm_ref, dyw_ref, wq_ref, wp_ref, qkv, gatt)
    attend((w,), w, qkv, gatt, gact_ref)


def early_call(w, *operands):
    wide = jax.ShapeDtypeStruct((TOK, D), BF)
    return pl.pallas_call(
        functools.partial(early_kernel, w),
        out_shape=(
            wide,
            wide,
            wide,
            jax.ShapeDtypeStruct((TOK, 2048), BF),
        ),
        scratch_shapes=[
            pltpu.VMEM((ROWS, D), F32),
            pltpu.VMEM((2 * TOK, D), F32),
            pltpu.VMEM((TOK, 1536), BF),
            pltpu.VMEM((TOK, HH), BF),
        ],
        compiler_params=params(16),
        cost_estimate=cost(2e9, 9e6),
    )(*operands)


def main_kernel(x_ref, dy_ref, lat_ref, lon_ref, diag_ref, gain_ref, wq_ref, wp_ref, *refs):
    early, refs = (refs[0:4], refs[4:8]), refs[8:]
    keep_ref, send_ref, gact_ref, xw_ref, dyw_ref, src, win, nrm, qkv, gatt, lhs = refs
    core = lax.axis_index("c")
    for w in range(2):
        for to, at in zip((nrm, xw_ref, dyw_ref, gact_ref), early[w]):
            to[w * TOK : (w + 1) * TOK, :] = at[...]
    rest = slice(2 * TOK, ROWS)
    for a, ref in enumerate((x_ref, dy_ref)):
        halos = ((lat_ref.at[a], lat_segments), (lon_ref.at[a], lon_segments), (diag_ref.at[a], diag_segments))
        assemble((2, 3), ref, halos, src, win)
        if a:
            dyw_ref[rest, :] = win[rest, :].astype(BF)
        else:
            normalize((2, 3), 0, win, gain_ref, xw_ref, nrm)
    project(rest, nrm, dyw_ref, wq_ref, wp_ref, qkv, gatt)
    attend((2, 3), 0, qkv, gatt, gact_ref)

    lhs[0] = nrm[...].T
    lhs[1] = dyw_ref[...].T
    for out, half in ((send_ref, 1 - core), (keep_ref, core)):
        low = pl.ds(pl.multiple_of(half * 1024, 1024), 512)
        high = pl.ds(pl.multiple_of(half * 1024 + 512, 512), 512)
        for i in range(4):
            rows = slice(i * 256, (i + 1) * 256)
            out[rows, 0:512] = dot(lhs[0, rows, :], gact_ref[:, low], NN).astype(BF)
            out[rows, 512:1024] = dot(lhs[half, rows, :], gact_ref[:, high], NN).astype(BF)


def main_call(*operands):
    return pl.pallas_call(
        main_kernel,
        out_shape=(
            jax.ShapeDtypeStruct((D, 1024), BF),
            jax.ShapeDtypeStruct((D, 1024), BF),
            jax.ShapeDtypeStruct((ROWS, 2048), BF),
            jax.ShapeDtypeStruct((ROWS, D), BF),
            jax.ShapeDtypeStruct((ROWS, D), BF),
        ),
        scratch_shapes=[
            pltpu.VMEM((ROWS, D), F32),
            pltpu.VMEM((ROWS, D), F32),
            pltpu.VMEM((ROWS, D), BF),
            pltpu.VMEM((ROWS, 1536), BF),
            pltpu.VMEM((ROWS, HH), BF),
            pltpu.VMEM((2, D, ROWS), BF),
        ],
        compiler_params=params(32),
        cost_estimate=cost(5.5e9, 14e6),
        name="main",
    )(*operands)


def input_rows(w, gact_ref, xw_ref, dyw_ref, gain, wq_ref, win):
    rows = slice(w * TOK, (w + 1) * TOK)
    gn = dot(gact_ref[rows, 0:1536], wq_ref[...], NT)
    cen, inv = layer_stats(xw_ref[rows, :].astype(F32))
    xhat = cen * inv
    g = gn * gain
    win[rows, :] = dyw_ref[rows, :].astype(F32) + inv * (
        g - jnp.mean(g, -1, keepdims=True) - xhat * jnp.mean(g * xhat, -1, keepdims=True)
    )
    return jnp.sum(gn * xhat, 0, keepdims=True)


def input_low_kernel(
    gact_ref, xw_ref, dyw_ref, gain_ref, wq_ref, own_ref, lat_ref, lon_ref, diag_ref, gg_ref, win, dst
):
    gain = gain_ref[...]
    gg_ref[...] = sum(input_rows(w, gact_ref, xw_ref, dyw_ref, gain, wq_ref, win) for w in (2, 3))
    for out, segments in ((lat_ref, lat_segments()), (lon_ref, lon_out_segments(0)), (diag_ref, diag_segments())):
        count = out.shape[0]
        dst[count - 16 : count, :] = jnp.zeros((16, D), F32)
        for at, here, size, _ in segments:
            dst[at : at + size, :] = win[here : here + size, :]
        out[...] = dst[:count, :].astype(BF)
    for own, here, size in own_segments():
        if slot(here) >= 2:
            dst[own : own + size, :] = win[here : here + size, :]
    for lev in range(LEV):
        for r in range(9, NR):
            at = (lev * NR + r) * NC
            own_ref[lev, r - 9] = dst[at : at + NC, :].astype(BF)


def input_high_kernel(
    gact_ref, xw_ref, dyw_ref, gain_ref, wq_ref, lon0_ref, diag_ref, gg0_ref, own_ref, lon_ref, gg_ref, win, dst
):
    gain = gain_ref[...]
    acc = gg0_ref[...] + sum(input_rows(w, gact_ref, xw_ref, dyw_ref, gain, wq_ref, win) for w in (0, 1))
    for j in range(8):
        gg_ref[j : j + 1, :] = acc[:, j * 128 : (j + 1) * 128]
    lon_ref[0:48, :] = lon0_ref[...]
    dst[64:80, :] = jnp.zeros((16, D), F32)
    for at, here, size, _ in lon_out_segments(1):
        dst[at - 48 : at - 48 + size, :] = win[here : here + size, :]
    lon_ref[48:128, :] = dst[0:80, :].astype(BF)
    lon_ref[128:176, :] = diag_ref[...]
    for own, here, size in own_segments():
        if slot(here) < 2:
            dst[own : own + size, :] = win[here : here + size, :]
    for lev in range(LEV):
        for r in range(3, 9):
            at = (lev * NR + r) * NC
            own_ref[lev, r - 3] = dst[at : at + NC, :].astype(BF)


def lon_out_segments(part):
    for lev in range(LEV):
        for rr in (range(6, 9), range(6))[part]:
            at = (48 + (lev * 6 + rr) * 6) if part else (lev * 3 + rr - 6) * 6
            yield at, window_row(lev, rr, 18), 6, (lev * NR + rr + 3) * NC


def input_low_call(gact, xw, dyw, gain, wq):
    return pl.pallas_call(
        input_low_kernel,
        out_shape=(
            jax.ShapeDtypeStruct((LEV, 3, NC, D), BF),
            jax.ShapeDtypeStruct((LATN, D), BF),
            jax.ShapeDtypeStruct((48, D), BF),
            jax.ShapeDtypeStruct((DIAGN, D), BF),
            jax.ShapeDtypeStruct((1, D), F32),
        ),
        scratch_shapes=[pltpu.VMEM((ROWS, D), F32), pltpu.VMEM((ROWS, D), F32)],
        compiler_params=params(24),
        cost_estimate=cost(1e9, 9e6),
        name="input_low",
    )(gact, xw, dyw, gain, wq)


def input_high_call(*operands):
    return pl.pallas_call(
        input_high_kernel,
        out_shape=(
            jax.ShapeDtypeStruct((LEV, 6, NC, D), BF),
            jax.ShapeDtypeStruct((176, D), BF),
            jax.ShapeDtypeStruct((8, 128), F32),
        ),
        scratch_shapes=[pltpu.VMEM((ROWS, D), F32), pltpu.VMEM((ROWS, D), F32)],
        compiler_params=params(24),
        cost_estimate=cost(1e9, 9e6),
        name="input_high",
    )(*operands)


def join_kernel(high_ref, low_ref, lat_ref, lon_ref, out_ref, src, dst):
    for lev in range(LEV):
        for r in range(3, NR):
            at = (lev * NR + r) * NC
            part = high_ref[lev, r - 3] if r < 9 else low_ref[lev, r - 9]
            dst[at : at + NC, :] = part.astype(F32)
    lon_parts = [*lon_out_segments(0), *lon_out_segments(1)]
    corner = [(LATN + here, at, size, own) for here, at, size, own in diag_segments()]
    for halo, segments in ((lat_ref, [*lat_segments(), *corner]), (lon_ref, lon_parts)):
        count = halo.shape[0]
        src[:count, :] = halo[...].astype(F32)
        for here, _, size, own in segments:
            dst[own : own + size, :] = src[here : here + size, :]
    for lev in range(LEV):
        for r in range(NR):
            at = (lev * NR + r) * NC
            out_ref[lev, r] = dst[at : at + NC, :].astype(BF)


def join_call(high, low, lat, lon):
    return pl.pallas_call(
        join_kernel,
        out_shape=jax.ShapeDtypeStruct((LEV, NR, NC, D), BF),
        scratch_shapes=[pltpu.VMEM((176, D), F32), pltpu.VMEM((ROWS, D), F32)],
        compiler_params=params(12),
        cost_estimate=cost(1e6, 4e6),
        name="join",
    )(high, low, lat, lon)


MSG = 272


def x_of():
    return lax.axis_index("xh") * 2 + lax.axis_index("xl")


def x_block(x):
    return lax.rem(x, 2) * 2 + x // 2


def put_gain(out, at, gg):
    hi = gg.astype(BF)
    out[at : at + 16, :] = jnp.zeros((16, 512), BF)
    out[at : at + 8, 0:128] = hi
    out[at : at + 8, 128:256] = (gg - hi.astype(F32)).astype(BF)


def take_gain(ref, at):
    return ref[at : at + 8, 0:128].astype(F32) + ref[at : at + 8, 128:256].astype(F32)


def split_kernel(keep_ref, recv_ref, gg_ref, owna, a1, a2, a3, ownb, b1, b2, b3):
    y = lax.axis_index("y")
    x = x_of()

    def total(rows, cols):
        return keep_ref[rows, cols].astype(F32) + recv_ref[rows, cols].astype(F32)

    for k, out in enumerate((owna, a1, a2, a3)):
        rows = pl.ds(pl.multiple_of(lax.rem(y + k, 4) * 256, 256), 256)
        out[0:256, :] = total(rows, slice(0, 512)).astype(out.dtype)
        if k:
            put_gain(out, 256, gg_ref[...])
    for k, out in enumerate((ownb, b1, b2, b3)):
        block = x_block(lax.rem(x + k, 4))
        for j in range(4):
            rows = pl.ds(pl.multiple_of(j * 256 + block * 64, 64), 64)
            out[j * 64 : (j + 1) * 64, :] = total(rows, slice(512, 1024)).astype(out.dtype)


def split_call(keep, recv, gg):
    mine = jax.ShapeDtypeStruct((256, 512), F32)
    a = jax.ShapeDtypeStruct((MSG, 512), BF)
    b = jax.ShapeDtypeStruct((256, 512), BF)
    return pl.pallas_call(
        split_kernel,
        out_shape=(mine, a, a, a, mine, b, b, b),
        compiler_params=params(12),
        cost_estimate=cost(1e6, 8e6),
        name="split",
    )(keep, recv, gg)


def cross_kernel(
    owna, a1, a2, a3, ownb, b1, b2, b3, gg_ref, gout, nowna, na1, na2, na3, nownb, nb1, nb2, nb3
):
    y = lax.axis_index("y")
    x = x_of()
    gg = gg_ref[...] + take_gain(a1, 256) + take_gain(a2, 256) + take_gain(a3, 256)
    gout[...] = gg

    def total(rows, own, refs):
        value = own[rows, :]
        for ref in refs:
            value += ref[rows, :].astype(F32)
        return value

    for k, out in enumerate((nowna, na1, na2, na3)):
        rows = pl.ds(pl.multiple_of(x_block(lax.rem(x + k, 4)) * 64, 64), 64)
        out[0:64, :] = total(rows, owna, (a1, a2, a3)).astype(out.dtype)
        if k:
            put_gain(out, 64, gg)
    for k, out in enumerate((nownb, nb1, nb2, nb3)):
        rows = pl.ds(pl.multiple_of(lax.rem(y + k, 4) * 64, 64), 64)
        out[...] = total(rows, ownb, (b1, b2, b3)).astype(out.dtype)


def cross_call(*operands):
    mine = jax.ShapeDtypeStruct((64, 512), F32)
    a = jax.ShapeDtypeStruct((80, 512), BF)
    b = jax.ShapeDtypeStruct((64, 512), BF)
    return pl.pallas_call(
        cross_kernel,
        out_shape=(jax.ShapeDtypeStruct((8, 128), F32), mine, a, a, a, mine, b, b, b),
        compiler_params=params(8),
        cost_estimate=cost(1e6, 4e6),
        name="cross",
    )(*operands)


def gather_kernel(owna, a1, a2, a3, ownb, b1, b2, b3, gg_ref, out_ref):
    gg = gg_ref[...] + take_gain(a1, 64) + take_gain(a2, 64) + take_gain(a3, 64)
    gg = gg.astype(BF)
    for i in range(8):
        rows = slice(i * 8, (i + 1) * 8)
        parts = []
        for own, refs in ((owna, (a1, a2, a3)), (ownb, (b1, b2, b3))):
            value = own[rows, :]
            for ref in refs:
                value += ref[rows, :].astype(F32)
            parts.append(value)
        for j in range(2):
            half = slice(j * 4, j * 4 + 4)
            out_ref[2 * i + j, :, 0:512] = jnp.concatenate([parts[0][half], parts[1][half]], 0).astype(BF)
            out_ref[2 * i + j, :, 512:640] = gg


def gather_call(*operands):
    return pl.pallas_call(
        gather_kernel,
        out_shape=jax.ShapeDtypeStruct((16, 8, 640), BF),
        compiler_params=params(6),
        cost_estimate=cost(1e6, 4e6),
        name="gather",
    )(*operands)


def final_kernel(blocks, wq_ref, wp_ref, gain_ref, gg):
    low = jnp.zeros((8, 640), F32)
    high = jnp.zeros((8, 640), F32)
    for z in range(8):
        low += blocks[2 * z].astype(F32)
        high += blocks[2 * z + 1].astype(F32)
    low = low * FACTOR
    high = high * FACTOR
    wq_ref[:, 0:512] = low[0:4, 0:512]
    wq_ref[:, 512:1024] = low[4:8, 0:512]
    wq_ref[:, 1024:1536] = high[0:4, 0:512]
    wp_ref[...] = high[4:8, 0:512]
    gg[...] = low[:, 512:640] + high[:, 512:640]
    device = lax.axis_index("y") * 64 + lax.axis_index("xl") * 32 + lax.axis_index("xh") * 16
    device = device + lax.axis_index("z") * 2 + lax.axis_index("c")
    row = gg[pl.ds(device // 32, 1), :]
    gain_ref[...] = pltpu.roll(row, lax.rem(128 - lax.rem(device, 32) * 4, 128), 1)[:, 0:4]


def final_call(blocks):
    return pl.pallas_call(
        final_kernel,
        out_shape=(
            jax.ShapeDtypeStruct((4, 1536), F32),
            jax.ShapeDtypeStruct((4, HH), F32),
            jax.ShapeDtypeStruct((1, 4), F32),
        ),
        scratch_shapes=[pltpu.VMEM((8, 128), F32)],
        compiler_params=params(4),
        cost_estimate=cost(1e6, 1e6),
        name="final",
    )(blocks)


def shift_x(value, k):
    pairs = []
    for xl in range(2):
        for xh in range(2):
            to = (xh * 2 + xl + k) % 4
            pairs.append((xl * 2 + xh, (to % 2) * 2 + to // 2))
    return lax.ppermute(value, ("xl", "xh"), pairs)


def shift_y(value, k):
    return lax.ppermute(value, "y", shift(4, k))


def shift(n, k):
    return [(i, (i + k) % n) for i in range(n)]


def shift_both(k):
    pairs = []
    for i in range(8):
        for j in range(32):
            pairs.append((i * 32 + j, ((i + k) % 8) * 32 + (j + k) % 32))
    return pairs


LAT = ("y", "xl")
LON = ("xh", "z", "c")
ALL = LAT + LON


def exchange(move, values):
    out = []
    for k, v in enumerate(values):
        out.append(move(v, k + 1))
    return out


def program(x, dy, gain, wq, wp):
    gain2 = gain.reshape(1, D)
    lat, lon, diag = pack(x, dy)
    lon = lax.ppermute(lon, LON, shift(32, -1))
    lat = lax.ppermute(lat, LAT, shift(8, -1))
    diag = lax.ppermute(diag, ALL, shift_both(-1))
    early = early_call(0, x, dy, gain2, wq, wp)
    lon, first = lax.optimization_barrier((lon, early[0]))
    early = (first, *early[1:], *early_call(1, x, dy, lon, gain2, wq, wp))
    keep, send, gact, xw, dyw = main_call(x, dy, lat, lon, diag, gain2, wq, wp, *early)
    recv = lax.ppermute(send, "c", [(0, 1), (1, 0)])
    low, lat, lon0, diag, gg0 = input_low_call(gact, xw, dyw, gain2, wq)
    high, lon, gg = input_high_call(gact, xw, dyw, gain2, wq, lon0, diag, gg0)
    oa, a1, a2, a3, ob, b1, b2, b3 = split_call(keep, recv, gg)
    a1, a2, a3 = exchange(shift_y, (a1, a2, a3))
    b1, b2, b3 = exchange(shift_x, (b1, b2, b3))
    lon = lax.ppermute(lon, LON, shift(32, 1))
    gg, oa, a1, a2, a3, ob, b1, b2, b3 = cross_call(oa, a1, a2, a3, ob, b1, b2, b3, gg)
    a1, a2, a3 = exchange(shift_x, (a1, a2, a3))
    b1, b2, b3 = exchange(shift_y, (b1, b2, b3))
    lat = jnp.concatenate([lat, lon[128:176]], 0)
    lat = lax.ppermute(lat, LAT, shift(8, 1))
    blocks = gather_call(oa, a1, a2, a3, ob, b1, b2, b3, gg)
    blocks = lax.all_to_all(blocks, ("z", "c"), 0, 0, tiled=True)
    lat, blocks = lax.optimization_barrier((lat, blocks))
    grad_in = join_call(high, low, lat, lon)
    grad_qkv, grad_proj, grad_gain = final_call(blocks)
    return grad_in, grad_qkv, grad_proj.T, grad_gain.reshape(4)


def solution(mesh):
    mesh = Mesh(mesh.devices.reshape(4, 2, 2, 8, 2), ALL)
    return jax.shard_map(
        program,
        mesh=mesh,
        in_specs=(P(None, LAT, LON, None), P(None, LAT, LON, None), P(), P(), P()),
        out_specs=(P(None, LAT, LON, None), P(ALL, None), P(None, ALL), P(ALL)),
        check_vma=False,
    )
```

```python
import functools

import jax
import jax.numpy as jnp
from jax import lax
from jax.experimental import pallas as pl
from jax.experimental.pallas import tpu as pltpu
from jax.sharding import Mesh, PartitionSpec as P


F32 = jnp.float32
BF = jnp.bfloat16
D = 1024
HH = 512
TOK = 144
NWIN = 4
ROWS = NWIN * TOK
LEV, NR, NC = 2, 12, 24
LATN = 112
LONN = 112
DIAGN = 48
EPS = 1e-05
FACTOR = 1.0 / 384.0

NN = (((1,), (0,)), ((), ()))
NT = (((1,), (1,)), ((), ()))
TN = (((0,), (0,)), ((), ()))


def dot(a, b, dims):
    return lax.dot_general(a, b, dims, preferred_element_type=F32)


def params(mib, **more):
    return pltpu.CompilerParams(vmem_limit_bytes=mib * 1024 * 1024, **more)


def cost(flops, nbytes):
    return pl.CostEstimate(flops=int(flops), bytes_accessed=int(nbytes), transcendentals=0)


def window_row(lev, rr, cc):
    return ((rr // 6) * 2 + cc // 12) * TOK + lev * 72 + (rr % 6) * 12 + cc % 12


def own_segments():
    for lev in range(LEV):
        for rr in range(9):
            base = (lev * NR + rr + 3) * NC
            yield base + 6, window_row(lev, rr, 0), 12
            yield base + 18, window_row(lev, rr, 12), 6


def lat_segments():
    for lev in range(LEV):
        for r in range(3):
            base = (lev * 3 + r) * 18
            yield base, window_row(lev, 9 + r, 0), 12, (lev * NR + r) * NC + 6
            yield base + 12, window_row(lev, 9 + r, 12), 6, (lev * NR + r) * NC + 18


def lon_segments():
    for lev in range(LEV):
        for rr in range(9):
            yield (lev * 9 + rr) * 6, window_row(lev, rr, 18), 6, (lev * NR + rr + 3) * NC


def diag_segments():
    for lev in range(LEV):
        for r in range(3):
            yield (lev * 3 + r) * 6, window_row(lev, 9 + r, 18), 6, (lev * NR + r) * NC


def pack_kernel(x_ref, dy_ref, lat_ref, lon_ref, diag_ref, top, side, src, dst, sems):
    copies = []
    for a, ref in enumerate((x_ref, dy_ref)):
        copies.append(
            (
                pltpu.make_async_copy(ref.at[:, 0:3], top.at[a], sems.at[a, 0]),
                pltpu.make_async_copy(ref.at[:, 3:12, 0:8, :], side.at[a], sems.at[a, 1]),
            )
        )
    for pair in copies:
        for copy in pair:
            copy.start()
    for a, pair in enumerate(copies):
        pair[0].wait()
        for lev in range(LEV):
            for r in range(3):
                at = (lev * NR + r) * NC
                src[at : at + NC, :] = top[a, lev, r].astype(F32)
        pair[1].wait()
        for lev in range(LEV):
            for r in range(3, NR):
                at = (lev * NR + r) * NC
                src[at : at + 8, :] = side[a, lev, r - 3].astype(F32)
        for out, segments in ((lat_ref, lat_segments), (lon_ref, lon_segments), (diag_ref, diag_segments)):
            count = out.shape[1]
            dst[count - 16 : count, :] = jnp.zeros((16, D), F32)
            for at, _, size, own in segments():
                dst[at : at + size, :] = src[own : own + size, :]
            out[a] = dst[:count, :].astype(BF)


def pack(x, dy):
    return pl.pallas_call(
        pack_kernel,
        in_specs=[pl.BlockSpec(memory_space=pltpu.HBM)] * 2,
        out_shape=(
            jax.ShapeDtypeStruct((2, LATN, D), BF),
            jax.ShapeDtypeStruct((2, LONN, D), BF),
            jax.ShapeDtypeStruct((2, DIAGN, D), BF),
        ),
        scratch_shapes=[
            pltpu.VMEM((2, LEV, 3, NC, D), BF),
            pltpu.VMEM((2, LEV, 9, 8, D), BF),
            pltpu.VMEM((ROWS, D), F32),
            pltpu.VMEM((LATN, D), F32),
            pltpu.SemaphoreType.DMA((2, 2)),
        ],
        compiler_params=params(60),
        cost_estimate=cost(1e6, 4e6),
        name="pack",
    )(x, dy)


def slot(at):
    return at // TOK


def assemble(slots, ref, halos, src, win):
    for lev in range(LEV):
        for r in range(3, 9) if slots[0] < 2 else range(9, NR):
            at = (lev * NR + r) * NC
            src[at : at + NC, :] = ref[lev, r].astype(F32)
    for own, at, size in own_segments():
        if slot(at) in slots:
            win[at : at + size, :] = src[own : own + size, :]
    for halo, segments in halos:
        count = halo.shape[-2]
        src[:count, :] = halo[...].astype(F32)
        for here, at, size, _ in segments():
            if slot(at) in slots:
                win[at : at + size, :] = src[here : here + size, :]


def layer_stats(x):
    mean = jnp.mean(x, -1, keepdims=True)
    cen = x - mean
    inv = lax.rsqrt(jnp.mean(cen * cen, -1, keepdims=True) + EPS)
    return cen, inv


def normalize(slots, base, win, gain_ref, xw_ref, nrm):
    for w in slots:
        x = win[w * TOK : (w + 1) * TOK, :]
        rows = slice((w - base) * TOK, (w - base + 1) * TOK)
        xw_ref[rows, :] = x.astype(BF)
        cen, inv = layer_stats(x)
        nrm[rows, :] = (cen * inv * gain_ref[...]).astype(BF)


def project(rows, nrm, dyw_ref, wq_ref, wp_ref, qkv, gatt):
    for j in range(6):
        cols = slice(j * 256, (j + 1) * 256)
        qkv[rows, cols] = dot(nrm[rows, :], wq_ref[:, cols], NN).astype(BF)
    for j in range(2):
        cols = slice(j * 256, (j + 1) * 256)
        gatt[rows, cols] = dot(dyw_ref[rows, :], wp_ref[cols, :], NT).astype(BF)


def attend(slots, base, qkv, gatt, gact_ref):
    low = lax.broadcasted_iota(jnp.int32, (TOK, 128), 1) < 64
    keyg = (lax.broadcasted_iota(jnp.int32, (TOK, 2 * TOK), 0) // 12) % 6 < 3
    qryg = (lax.broadcasted_iota(jnp.int32, (TOK, 2 * TOK), 1) // 12) % 6 < 3
    last = jnp.logical_and(lax.axis_index("y") == 3, lax.axis_index("xl") == 1)
    apart = jnp.logical_and(keyg != qryg, last)

    def stacked(v):
        z = jnp.zeros_like(v)
        return jnp.concatenate([jnp.where(low, v, z), jnp.where(low, z, v)], axis=0)

    for w in slots:
        rows = slice((w - base) * TOK, (w - base + 1) * TOK)
        for hp in range(4):
            at = hp * 128
            q2 = stacked(qkv[rows, at : at + 128] * jnp.bfloat16(0.125))
            k = qkv[rows, HH + at : HH + at + 128]
            v = qkv[rows, 2 * HH + at : 2 * HH + at + 128]
            g2 = stacked(gatt[rows, at : at + 128])
            s = dot(k, q2, NT)
            if w >= 2:
                s = jnp.where(apart, -1000000000.0, s)
            e = jnp.exp(s - jnp.max(s, 0, keepdims=True))
            p = e * (1.0 / jnp.sum(e, 0, keepdims=True))
            pb = p.astype(BF)
            dp = dot(v, g2, NT)
            ds = (p * (dp - jnp.sum(p * dp, 0, keepdims=True))).astype(BF)
            o = dot(pb, v, TN)
            gact_ref[rows, 3 * HH + at : 3 * HH + at + 128] = jnp.where(low, o[:TOK], o[TOK:]).astype(BF)
            dq = dot(ds, k, TN)
            gact_ref[rows, at : at + 128] = (jnp.where(low, dq[:TOK], dq[TOK:]) * 0.125).astype(BF)
            gact_ref[rows, HH + at : HH + at + 128] = dot(ds, q2, NN).astype(BF)
            gact_ref[rows, 2 * HH + at : 2 * HH + at + 128] = dot(pb, g2, NN).astype(BF)


def early_kernel(w, x_ref, dy_ref, *refs):
    halo, refs = (refs[0], refs[1:]) if w else (None, refs)
    gain_ref, wq_ref, wp_ref, nrm_ref, xw_ref, dyw_ref, gact_ref, src, win, qkv, gatt = refs
    halos = [((halo.at[a], lon_segments),) if w else () for a in range(2)]
    assemble((w,), x_ref, halos[0], src, win)
    normalize((w,), w, win, gain_ref, xw_ref, nrm_ref)
    assemble((w,), dy_ref, halos[1], src, win)
    dyw_ref[...] = win[w * TOK : (w + 1) * TOK, :].astype(BF)
    project(slice(0, TOK), nrm_ref, dyw_ref, wq_ref, wp_ref, qkv, gatt)
    attend((w,), w, qkv, gatt, gact_ref)


def early_call(w, *operands):
    wide = jax.ShapeDtypeStruct((TOK, D), BF)
    return pl.pallas_call(
        functools.partial(early_kernel, w),
        out_shape=(
            wide,
            wide,
            wide,
            jax.ShapeDtypeStruct((TOK, 2048), BF),
        ),
        scratch_shapes=[
            pltpu.VMEM((ROWS, D), F32),
            pltpu.VMEM((2 * TOK, D), F32),
            pltpu.VMEM((TOK, 1536), BF),
            pltpu.VMEM((TOK, HH), BF),
        ],
        compiler_params=params(16),
        cost_estimate=cost(2e9, 9e6),
    )(*operands)


def main_kernel(x_ref, dy_ref, lat_ref, lon_ref, diag_ref, gain_ref, wq_ref, wp_ref, *refs):
    early, refs = (refs[0:4], refs[4:8]), refs[8:]
    keep_ref, send_ref, gact_ref, xw_ref, dyw_ref, src, win, nrm, qkv, gatt, lhs = refs
    core = lax.axis_index("c")
    for w in range(2):
        for to, at in zip((nrm, xw_ref, dyw_ref, gact_ref), early[w]):
            to[w * TOK : (w + 1) * TOK, :] = at[...]
    rest = slice(2 * TOK, ROWS)
    for a, ref in enumerate((x_ref, dy_ref)):
        halos = ((lat_ref.at[a], lat_segments), (lon_ref.at[a], lon_segments), (diag_ref.at[a], diag_segments))
        assemble((2, 3), ref, halos, src, win)
        if a:
            dyw_ref[rest, :] = win[rest, :].astype(BF)
        else:
            normalize((2, 3), 0, win, gain_ref, xw_ref, nrm)
    project(rest, nrm, dyw_ref, wq_ref, wp_ref, qkv, gatt)
    attend((2, 3), 0, qkv, gatt, gact_ref)

    lhs[0] = nrm[...].T
    lhs[1] = dyw_ref[...].T
    for out, half in ((send_ref, 1 - core), (keep_ref, core)):
        low = pl.ds(pl.multiple_of(half * 1024, 1024), 512)
        high = pl.ds(pl.multiple_of(half * 1024 + 512, 512), 512)
        for i in range(4):
            rows = slice(i * 256, (i + 1) * 256)
            out[rows, 0:512] = dot(lhs[0, rows, :], gact_ref[:, low], NN).astype(BF)
            out[rows, 512:1024] = dot(lhs[half, rows, :], gact_ref[:, high], NN).astype(BF)


def main_call(*operands):
    return pl.pallas_call(
        main_kernel,
        out_shape=(
            jax.ShapeDtypeStruct((D, 1024), BF),
            jax.ShapeDtypeStruct((D, 1024), BF),
            jax.ShapeDtypeStruct((ROWS, 2048), BF),
            jax.ShapeDtypeStruct((ROWS, D), BF),
            jax.ShapeDtypeStruct((ROWS, D), BF),
        ),
        scratch_shapes=[
            pltpu.VMEM((ROWS, D), F32),
            pltpu.VMEM((ROWS, D), F32),
            pltpu.VMEM((ROWS, D), BF),
            pltpu.VMEM((ROWS, 1536), BF),
            pltpu.VMEM((ROWS, HH), BF),
            pltpu.VMEM((2, D, ROWS), BF),
        ],
        compiler_params=params(32),
        cost_estimate=cost(5.5e9, 14e6),
        name="main",
    )(*operands)


def input_rows(w, gact_ref, xw_ref, dyw_ref, gain, wq_ref, win):
    rows = slice(w * TOK, (w + 1) * TOK)
    gn = dot(gact_ref[rows, 0:1536], wq_ref[...], NT)
    cen, inv = layer_stats(xw_ref[rows, :].astype(F32))
    xhat = cen * inv
    g = gn * gain
    win[rows, :] = dyw_ref[rows, :].astype(F32) + inv * (
        g - jnp.mean(g, -1, keepdims=True) - xhat * jnp.mean(g * xhat, -1, keepdims=True)
    )
    return jnp.sum(gn * xhat, 0, keepdims=True)


def input_low_kernel(
    gact_ref, xw_ref, dyw_ref, gain_ref, wq_ref, own_ref, lat_ref, lon_ref, diag_ref, gg_ref, win, dst
):
    gain = gain_ref[...]
    gg_ref[...] = sum(input_rows(w, gact_ref, xw_ref, dyw_ref, gain, wq_ref, win) for w in (2, 3))
    for out, segments in ((lat_ref, lat_segments()), (lon_ref, lon_out_segments(0)), (diag_ref, diag_segments())):
        count = out.shape[0]
        dst[count - 16 : count, :] = jnp.zeros((16, D), F32)
        for at, here, size, _ in segments:
            dst[at : at + size, :] = win[here : here + size, :]
        out[...] = dst[:count, :].astype(BF)
    for own, here, size in own_segments():
        if slot(here) >= 2:
            dst[own : own + size, :] = win[here : here + size, :]
    for lev in range(LEV):
        for r in range(9, NR):
            at = (lev * NR + r) * NC
            own_ref[lev, r - 9] = dst[at : at + NC, :].astype(BF)


def input_high_kernel(
    gact_ref, xw_ref, dyw_ref, gain_ref, wq_ref, lon0_ref, diag_ref, gg0_ref, own_ref, lon_ref, gg_ref, win, dst
):
    gain = gain_ref[...]
    acc = gg0_ref[...] + sum(input_rows(w, gact_ref, xw_ref, dyw_ref, gain, wq_ref, win) for w in (0, 1))
    for j in range(8):
        gg_ref[j : j + 1, :] = acc[:, j * 128 : (j + 1) * 128]
    lon_ref[0:48, :] = lon0_ref[...]
    dst[64:80, :] = jnp.zeros((16, D), F32)
    for at, here, size, _ in lon_out_segments(1):
        dst[at - 48 : at - 48 + size, :] = win[here : here + size, :]
    lon_ref[48:128, :] = dst[0:80, :].astype(BF)
    lon_ref[128:176, :] = diag_ref[...]
    for own, here, size in own_segments():
        if slot(here) < 2:
            dst[own : own + size, :] = win[here : here + size, :]
    for lev in range(LEV):
        for r in range(3, 9):
            at = (lev * NR + r) * NC
            own_ref[lev, r - 3] = dst[at : at + NC, :].astype(BF)


def lon_out_segments(part):
    for lev in range(LEV):
        for rr in (range(6, 9), range(6))[part]:
            at = (48 + (lev * 6 + rr) * 6) if part else (lev * 3 + rr - 6) * 6
            yield at, window_row(lev, rr, 18), 6, (lev * NR + rr + 3) * NC


def input_low_call(gact, xw, dyw, gain, wq):
    return pl.pallas_call(
        input_low_kernel,
        out_shape=(
            jax.ShapeDtypeStruct((LEV, 3, NC, D), BF),
            jax.ShapeDtypeStruct((LATN, D), BF),
            jax.ShapeDtypeStruct((48, D), BF),
            jax.ShapeDtypeStruct((DIAGN, D), BF),
            jax.ShapeDtypeStruct((1, D), F32),
        ),
        scratch_shapes=[pltpu.VMEM((ROWS, D), F32), pltpu.VMEM((ROWS, D), F32)],
        compiler_params=params(24),
        cost_estimate=cost(1e9, 9e6),
        name="input_low",
    )(gact, xw, dyw, gain, wq)


def input_high_call(*operands):
    return pl.pallas_call(
        input_high_kernel,
        out_shape=(
            jax.ShapeDtypeStruct((LEV, 6, NC, D), BF),
            jax.ShapeDtypeStruct((176, D), BF),
            jax.ShapeDtypeStruct((8, 128), F32),
        ),
        scratch_shapes=[pltpu.VMEM((ROWS, D), F32), pltpu.VMEM((ROWS, D), F32)],
        compiler_params=params(24),
        cost_estimate=cost(1e9, 9e6),
        name="input_high",
    )(*operands)


def join_rest_kernel(high_ref, low_ref, lon_ref, out_ref, src, dst):
    step = pl.program_id(0)

    @pl.when(step == 0)
    def _():
        for lev in range(LEV):
            for r in range(3, NR):
                at = (lev * NR + r) * NC
                part = high_ref[lev, r - 3] if r < 9 else low_ref[lev, r - 9]
                dst[at : at + NC, :] = part.astype(F32)
        src[0:128, :] = lon_ref[0:128, :].astype(F32)
        for here, _, size, own in [*lon_out_segments(0), *lon_out_segments(1)]:
            dst[own : own + size, :] = src[here : here + size, :]

    for lev in range(LEV):
        for r in range(3):
            at = pl.multiple_of((lev * NR + 3 + r + 3 * step) * NC, 8)
            out_ref[lev, r] = dst[pl.ds(at, NC), :].astype(BF)


def join_top_kernel(lat_ref, rest_ref, out_ref, src, dst):
    src[...] = lat_ref[...].astype(F32)
    corner = [(LATN + here, at, size, own) for here, at, size, own in diag_segments()]
    for here, _, size, own in [*lat_segments(), *corner]:
        dst[own : own + size, :] = src[here : here + size, :]
    for lev in range(LEV):
        for r in range(3):
            at = (lev * NR + r) * NC
            out_ref[lev, r] = dst[at : at + NC, :].astype(BF)


WHOLE = pl.BlockSpec(memory_space=pltpu.VMEM)
GRID_OUT = jax.ShapeDtypeStruct((LEV, NR, NC, D), BF)


def join_rest(high, low, lon):
    return pl.pallas_call(
        join_rest_kernel,
        grid=(3,),
        in_specs=[WHOLE] * 3,
        out_specs=pl.BlockSpec((LEV, 3, NC, D), lambda i: (0, i + 1, 0, 0)),
        out_shape=GRID_OUT,
        scratch_shapes=[pltpu.VMEM((128, D), F32), pltpu.VMEM((ROWS, D), F32)],
        compiler_params=params(12),
        cost_estimate=cost(1e6, 4e6),
        name="join_rest",
    )(high, low, lon)


def join_top(lat, rest):
    return pl.pallas_call(
        join_top_kernel,
        grid=(1,),
        in_specs=[WHOLE, pl.BlockSpec(memory_space=pl.ANY)],
        out_specs=pl.BlockSpec((LEV, 3, NC, D), lambda i: (0, 0, 0, 0)),
        out_shape=GRID_OUT,
        input_output_aliases={1: 0},
        scratch_shapes=[pltpu.VMEM((160, D), F32), pltpu.VMEM((ROWS, D), F32)],
        compiler_params=params(8),
        cost_estimate=cost(1e6, 2e6),
        name="join_top",
    )(lat, rest)


MSG = 272


def x_of():
    return lax.axis_index("xh") * 2 + lax.axis_index("xl")


def x_block(x):
    return lax.rem(x, 2) * 2 + x // 2


def put_gain(out, at, gg):
    hi = gg.astype(BF)
    out[at : at + 16, :] = jnp.zeros((16, 512), BF)
    out[at : at + 8, 0:128] = hi
    out[at : at + 8, 128:256] = (gg - hi.astype(F32)).astype(BF)


def take_gain(ref, at):
    return ref[at : at + 8, 0:128].astype(F32) + ref[at : at + 8, 128:256].astype(F32)


def split_kernel(keep_ref, recv_ref, gg_ref, owna, a1, a2, a3, ownb, b1, b2, b3):
    y = lax.axis_index("y")
    x = x_of()

    def total(rows, cols):
        return keep_ref[rows, cols].astype(F32) + recv_ref[rows, cols].astype(F32)

    for k, out in enumerate((owna, a1, a2, a3)):
        rows = pl.ds(pl.multiple_of(lax.rem(y + k, 4) * 256, 256), 256)
        out[0:256, :] = total(rows, slice(0, 512)).astype(out.dtype)
        if k:
            put_gain(out, 256, gg_ref[...])
    for k, out in enumerate((ownb, b1, b2, b3)):
        block = x_block(lax.rem(x + k, 4))
        for j in range(4):
            rows = pl.ds(pl.multiple_of(j * 256 + block * 64, 64), 64)
            out[j * 64 : (j + 1) * 64, :] = total(rows, slice(512, 1024)).astype(out.dtype)


def split_call(keep, recv, gg):
    mine = jax.ShapeDtypeStruct((256, 512), F32)
    a = jax.ShapeDtypeStruct((MSG, 512), BF)
    b = jax.ShapeDtypeStruct((256, 512), BF)
    return pl.pallas_call(
        split_kernel,
        out_shape=(mine, a, a, a, mine, b, b, b),
        compiler_params=params(12),
        cost_estimate=cost(1e6, 8e6),
        name="split",
    )(keep, recv, gg)


def cross_kernel(
    owna, a1, a2, a3, ownb, b1, b2, b3, gg_ref, gout, nowna, na1, na2, na3, nownb, nb1, nb2, nb3
):
    y = lax.axis_index("y")
    x = x_of()
    gg = gg_ref[...] + take_gain(a1, 256) + take_gain(a2, 256) + take_gain(a3, 256)
    gout[...] = gg

    def total(rows, own, refs):
        value = own[rows, :]
        for ref in refs:
            value += ref[rows, :].astype(F32)
        return value

    for k, out in enumerate((nowna, na1, na2, na3)):
        rows = pl.ds(pl.multiple_of(x_block(lax.rem(x + k, 4)) * 64, 64), 64)
        out[0:64, :] = total(rows, owna, (a1, a2, a3)).astype(out.dtype)
        if k:
            put_gain(out, 64, gg)
    for k, out in enumerate((nownb, nb1, nb2, nb3)):
        rows = pl.ds(pl.multiple_of(lax.rem(y + k, 4) * 64, 64), 64)
        out[...] = total(rows, ownb, (b1, b2, b3)).astype(out.dtype)


def cross_call(*operands):
    mine = jax.ShapeDtypeStruct((64, 512), F32)
    a = jax.ShapeDtypeStruct((80, 512), BF)
    b = jax.ShapeDtypeStruct((64, 512), BF)
    return pl.pallas_call(
        cross_kernel,
        out_shape=(jax.ShapeDtypeStruct((8, 128), F32), mine, a, a, a, mine, b, b, b),
        compiler_params=params(8),
        cost_estimate=cost(1e6, 4e6),
        name="cross",
    )(*operands)


def gather_kernel(owna, a1, a2, a3, ownb, b1, b2, b3, gg_ref, out_ref):
    gg = gg_ref[...] + take_gain(a1, 64) + take_gain(a2, 64) + take_gain(a3, 64)
    gg = gg.astype(BF)
    for i in range(8):
        rows = slice(i * 8, (i + 1) * 8)
        parts = []
        for own, refs in ((owna, (a1, a2, a3)), (ownb, (b1, b2, b3))):
            value = own[rows, :]
            for ref in refs:
                value += ref[rows, :].astype(F32)
            parts.append(value)
        for j in range(2):
            half = slice(j * 4, j * 4 + 4)
            out_ref[2 * i + j, :, 0:512] = jnp.concatenate([parts[0][half], parts[1][half]], 0).astype(BF)
            out_ref[2 * i + j, :, 512:640] = gg


def gather_call(*operands):
    return pl.pallas_call(
        gather_kernel,
        out_shape=jax.ShapeDtypeStruct((16, 8, 640), BF),
        compiler_params=params(6),
        cost_estimate=cost(1e6, 4e6),
        name="gather",
    )(*operands)


def final_kernel(blocks, wq_ref, wp_ref, gain_ref, gg):
    low = jnp.zeros((8, 640), F32)
    high = jnp.zeros((8, 640), F32)
    for z in range(8):
        low += blocks[2 * z].astype(F32)
        high += blocks[2 * z + 1].astype(F32)
    low = low * FACTOR
    high = high * FACTOR
    wq_ref[:, 0:512] = low[0:4, 0:512]
    wq_ref[:, 512:1024] = low[4:8, 0:512]
    wq_ref[:, 1024:1536] = high[0:4, 0:512]
    wp_ref[...] = high[4:8, 0:512]
    gg[...] = low[:, 512:640] + high[:, 512:640]
    device = lax.axis_index("y") * 64 + lax.axis_index("xl") * 32 + lax.axis_index("xh") * 16
    device = device + lax.axis_index("z") * 2 + lax.axis_index("c")
    row = gg[pl.ds(device // 32, 1), :]
    gain_ref[...] = pltpu.roll(row, lax.rem(128 - lax.rem(device, 32) * 4, 128), 1)[:, 0:4]


def final_call(blocks):
    return pl.pallas_call(
        final_kernel,
        out_shape=(
            jax.ShapeDtypeStruct((4, 1536), F32),
            jax.ShapeDtypeStruct((4, HH), F32),
            jax.ShapeDtypeStruct((1, 4), F32),
        ),
        scratch_shapes=[pltpu.VMEM((8, 128), F32)],
        compiler_params=params(4),
        cost_estimate=cost(1e6, 1e6),
        name="final",
    )(blocks)


def shift_x(value, k):
    pairs = []
    for xl in range(2):
        for xh in range(2):
            to = (xh * 2 + xl + k) % 4
            pairs.append((xl * 2 + xh, (to % 2) * 2 + to // 2))
    return lax.ppermute(value, ("xl", "xh"), pairs)


def shift_y(value, k):
    return lax.ppermute(value, "y", shift(4, k))


def shift(n, k):
    return [(i, (i + k) % n) for i in range(n)]


def shift_both(k):
    pairs = []
    for i in range(8):
        for j in range(32):
            pairs.append((i * 32 + j, ((i + k) % 8) * 32 + (j + k) % 32))
    return pairs


LAT = ("y", "xl")
LON = ("xh", "z", "c")
ALL = LAT + LON


def exchange(move, values):
    out = []
    for k, v in enumerate(values):
        out.append(move(v, k + 1))
    return out


def program(x, dy, gain, wq, wp):
    gain2 = gain.reshape(1, D)
    lat, lon, diag = pack(x, dy)
    lon = lax.ppermute(lon, LON, shift(32, -1))
    lat = lax.ppermute(lat, LAT, shift(8, -1))
    diag = lax.ppermute(diag, ALL, shift_both(-1))
    early = early_call(0, x, dy, gain2, wq, wp)
    lon, first = lax.optimization_barrier((lon, early[0]))
    early = (first, *early[1:], *early_call(1, x, dy, lon, gain2, wq, wp))
    keep, send, gact, xw, dyw = main_call(x, dy, lat, lon, diag, gain2, wq, wp, *early)
    recv = lax.ppermute(send, "c", [(0, 1), (1, 0)])
    low, lat, lon0, diag, gg0 = input_low_call(gact, xw, dyw, gain2, wq)
    high, lon, gg = input_high_call(gact, xw, dyw, gain2, wq, lon0, diag, gg0)
    oa, a1, a2, a3, ob, b1, b2, b3 = split_call(keep, recv, gg)
    a1, a2, a3 = exchange(shift_y, (a1, a2, a3))
    b1, b2, b3 = exchange(shift_x, (b1, b2, b3))
    lon = lax.ppermute(lon, LON, shift(32, 1))
    gg, oa, a1, a2, a3, ob, b1, b2, b3 = cross_call(oa, a1, a2, a3, ob, b1, b2, b3, gg)
    a1, a2, a3 = exchange(shift_x, (a1, a2, a3))
    b1, b2, b3 = exchange(shift_y, (b1, b2, b3))
    lat = jnp.concatenate([lat, lon[128:176]], 0)
    lat = lax.ppermute(lat, LAT, shift(8, 1))
    rest = join_rest(high, low, lon)
    a1, rest = lax.optimization_barrier((a1, rest))
    blocks = gather_call(oa, a1, a2, a3, ob, b1, b2, b3, gg)
    blocks = lax.all_to_all(blocks, ("z", "c"), 0, 0, tiled=True)
    lat, blocks = lax.optimization_barrier((lat, blocks))
    grad_in = join_top(lat, rest)
    grad_qkv, grad_proj, grad_gain = final_call(blocks)
    return grad_in, grad_qkv, grad_proj.T, grad_gain.reshape(4)


def solution(mesh):
    mesh = Mesh(mesh.devices.reshape(4, 2, 2, 8, 2), ALL)
    return jax.shard_map(
        program,
        mesh=mesh,
        in_specs=(P(None, LAT, LON, None), P(None, LAT, LON, None), P(), P(), P()),
        out_specs=(P(None, LAT, LON, None), P(ALL, None), P(None, ALL), P(ALL)),
        check_vma=False,
    )
```
